32 devices in a mesh: band: 16 (over z, x, core), fld: 2 (over y).
Axes of the slice: x: 2, y: 2, z: 4, core: 2. Of those that a mesh axis runs over, the one named last changes fastest.
Arguments:
- grid_field: bfloat16 [2, 4, 1280, 2, 5248], P(None, 'fld', 'band'), may hold values from -6 to 6
- coupling: float32 [2, 4], P(None, 'fld'), may hold values from 0.1 to 1
- points: int32 [1280], replicated, may hold values from 20 to 5136, as said below
- lat_ids: int32 [1280], P('band'), may hold values from 0 to 1279, each once
- wn_ids: int32 [128], P('band'), may hold values from 0 to 1279, as said below
Outputs:
- new_grid: bfloat16 [2, 4, 1280, 2, 5248], P(None, 'fld', 'band')
The draws below stay inside these ranges and needn't reach their ends.
Inputs may be any that keep to these rules, and one draw needn't show every extreme that they name: Latitude i has 20 + 4 i points or up to 8 fewer, a multiple of 4, never under 20; the last latitude has exactly the most. `lat_ids`: each hemispheric latitude stands in exactly one slot. `wn_ids`: distinct wavenumbers; 0 and 1279 are always among them.
All inputs are finite; a program needn't handle non-finite values.
Results may differ from the reference program's by a relative error of at most 0.014.
Values may be sent and summed in bfloat16 or wider, within the bound.
No kernel may reach another device: no remote copies, remote signals or barrier semaphores. Data moves between devices by JAX's collectives and lax.ppermute only.
A program may use at most 128 MiB of HBM per device.

```python
import math
import jax
import jax.numpy as jnp
from jax import lax

NT = 1279
NH = 1280
VARS = 2
PPAD = 5248
WN_TOTAL = 128
LEVELS = 4


def draw_points(key, part):
    position = jnp.arange(NH, dtype=jnp.int32)
    jitter = jax.random.randint(key, (NH,), 0, 3, dtype=jnp.int32)
    jitter = jnp.where((position >= 2) & (position < NH - 1), jitter, 0)
    return (20 + 4 * position - 4 * jitter).astype(jnp.int32)


def draw_wn_ids(key, part):
    middle = jax.random.permutation(jax.random.fold_in(key, 11), NT - 1)[:WN_TOTAL - 2] + 1
    chosen = jnp.concatenate([jnp.array([0, NT], dtype=jnp.int32), middle.astype(jnp.int32)])
    return jax.random.permutation(jax.random.fold_in(key, 12), chosen).astype(jnp.int32)


def block_scale(key, extent, pieces, low, top_value):
    loudness = 1.0
    for axis_at, shards_of in pieces:
        draws = jax.random.uniform(jax.random.fold_in(jax.random.fold_in(key, 6), axis_at), (shards_of,), jnp.float32, low / len(pieces), top_value / len(pieces))
        loudness = loudness * jnp.repeat(jnp.exp(draws), extent[axis_at] // shards_of).reshape((-1,) + (1,) * (len(extent) - 1 - axis_at))
    return loudness


def centred(stream_key, dims, width, limit, cuts=(), kind=jnp.bfloat16):
    level = block_scale(stream_key, dims, cuts, -0.22, 0.18) if cuts else 1.0
    values = jax.random.normal(stream_key, dims, jnp.float32) * width * level
    return jnp.minimum(jnp.maximum(values, -limit), limit).astype(kind)


def setup_inputs(seed: int = 0) -> dict:
    key_of = jax.random.split(jax.random.key(seed), 6)
    grid_field = centred(key_of[0], (VARS, LEVELS, NH, 2, PPAD), 1.0, 6.0, ((1, 2), (2, 16)))
    coupling = jnp.clip(jnp.exp(math.log(1.0) - 2.3025851 * jax.random.uniform(key_of[1], (VARS, LEVELS), jnp.float32) ** block_scale(key_of[1], (VARS, LEVELS), ((1, 2),), -0.2, 0.2)), 0.1, 1.0)
    points = draw_points(jax.random.fold_in(key_of[5], 71), 0)
    lat_ids = jax.random.permutation(key_of[3], NH).astype(jnp.int32)
    wn_ids = draw_wn_ids(jax.random.fold_in(key_of[5], 71), 0)
    return {"grid_field": grid_field, "coupling": coupling, "points": points, "lat_ids": lat_ids, "wn_ids": wn_ids}


rescale_limit = 2.0 ** 60
rescale_log = 60.0 * math.log(2.0)

def latitude_angles(lat_index):
    colatitude = math.pi * (lat_index.astype(jnp.float32) + 0.5) / (2.0 * NH)
    return (jnp.cos(colatitude), jnp.sin(colatitude))

def damping(orders):
    row_index = jnp.arange(NT + 1).astype(jnp.float32).reshape((NT + 1) // 2, 2)
    degree = row_index[:, :, None] + orders.astype(jnp.float32)[None, None, :]
    return 1.0 / (1.0 + 4.0 * degree * (degree + 1.0) / (NT * (NT + 1.0)))

def legendre_rows(orders, cosines, sines):
    order_f = orders.astype(jnp.float32)[:, None]
    step_index = jnp.arange(1, NT + 1).astype(jnp.float32)
    log_terms = jnp.log1p(0.5 / step_index)
    log_norm = 0.5 * math.log(0.5) + 0.5 * lax.optimization_barrier(jnp.sum(jnp.where(step_index[None, :] <= order_f, log_terms[None, :], 0.0), axis=1))
    scaled_log = log_norm[:, None] + order_f * jnp.log(sines)[None, :]
    start_row = jnp.ones(scaled_log.shape, jnp.float32)
    cosine_row = cosines[None, :]

    def advance(state_now, offset):
        current, previous, running_log = state_now
        offset_f = offset.astype(jnp.float32)
        degree = order_f + offset_f
        factor = jnp.sqrt((4.0 * degree * degree - 1.0) / (offset_f * (2.0 * order_f + offset_f)))
        backward = jnp.sqrt((offset_f - 1.0) * (2.0 * order_f + offset_f - 1.0) / (4.0 * (degree - 1.0) * (degree - 1.0) - 1.0))
        newest = factor * (cosine_row * current - backward * previous)
        oversize = jnp.abs(newest) > rescale_limit
        shrink = jnp.where(oversize, 1.0 / rescale_limit, 1.0)
        running_log = running_log + jnp.where(oversize, rescale_log, 0.0)
        newest = newest * shrink
        current = current * shrink
        row_value = jnp.where(degree <= NT, newest * jnp.exp(running_log), 0.0)
        return ((newest, current, running_log), row_value.astype(jnp.bfloat16))
    final_state, later_rows = lax.scan(advance, (start_row, jnp.zeros_like(start_row), scaled_log), jnp.arange(1, NT + 1))
    first_values = jnp.exp(scaled_log).astype(jnp.bfloat16)
    every_row = jnp.concatenate([first_values[None], later_rows], axis=0)
    return every_row.reshape(((NT + 1) // 2, 2) + every_row.shape[1:])

def fourier_tables(counts, orders, blocks):
    inner_index = jnp.arange(128).astype(jnp.int32)
    block_start = (jnp.arange(blocks) * 128).astype(jnp.int32)
    periods = counts[:, None, None]
    inner_residue = inner_index[None, :, None] * orders[None, None, :] % periods
    block_residue = block_start[None, :, None] * orders[None, None, :] % periods
    period_f = periods.astype(jnp.float32)
    inner_angle = 2.0 * math.pi * inner_residue.astype(jnp.float32) / period_f
    block_angle = 2.0 * math.pi * block_residue.astype(jnp.float32) / period_f
    return (jnp.cos(inner_angle).astype(jnp.bfloat16), jnp.sin(inner_angle).astype(jnp.bfloat16), jnp.cos(block_angle), jnp.sin(block_angle))

def reference(grid_field, coupling, points, lat_ids, wn_ids):
    orders = wn_ids
    order_count = orders.shape[0]
    counts = jnp.take(points, lat_ids)
    cosines, sines = latitude_angles(lat_ids)
    weights = math.pi / (2.0 * NH) * sines
    blocks = PPAD // 128

    def analyse_slot(inputs):
        values, slot_count, weight = inputs
        cos_inner, sin_inner, cos_outer, sin_outer = fourier_tables(slot_count[None], orders, blocks)
        inside = jnp.arange(PPAD) < slot_count
        masked = jnp.where(inside, values, jnp.zeros((), values.dtype)).astype(jnp.float32)
        shaped = masked.reshape(values.shape[:-1] + (blocks, 128))
        dft_table = jnp.concatenate([cos_inner[0], -sin_inner[0]], axis=-1).astype(jnp.float32)
        partial_sums = jnp.einsum('vlhbk,kc->vlhbc', shaped, dft_table)
        real_sums = partial_sums[..., :order_count]
        imag_sums = partial_sums[..., order_count:]
        period_f = slot_count.astype(jnp.float32)
        real_coef = lax.optimization_barrier(jnp.sum(cos_outer[0] * real_sums + sin_outer[0] * imag_sums, axis=-2)) / period_f
        imag_coef = lax.optimization_barrier(jnp.sum(cos_outer[0] * imag_sums - sin_outer[0] * real_sums, axis=-2)) / period_f
        kept_mask = 2 * orders < slot_count
        real_coef = jnp.where(kept_mask, real_coef, 0.0)
        imag_coef = jnp.where(kept_mask, imag_coef, 0.0)
        even_parts = jnp.stack([real_coef[:, :, 0] + real_coef[:, :, 1], imag_coef[:, :, 0] + imag_coef[:, :, 1]], axis=2)
        odd_parts = jnp.stack([real_coef[:, :, 0] - real_coef[:, :, 1], imag_coef[:, :, 0] - imag_coef[:, :, 1]], axis=2)
        return (weight * jnp.stack([even_parts, odd_parts], axis=2)).astype(jnp.bfloat16)
    fourier = lax.map(analyse_slot, (jnp.moveaxis(grid_field, 2, 0), counts, weights))
    by_order = jnp.moveaxis(fourier, 5, 0)

    def spectral_order(inputs):
        order_one, coeffs = inputs
        legendre_table = legendre_rows(order_one[None], cosines, sines)[:, :, 0, :].astype(jnp.float32)
        spectral = jnp.einsum('ivlpr,qpi->vlprq', coeffs.astype(jnp.float32), legendre_table)
        weighted = coupling[:, :, None, None, None] * spectral
        below = jnp.cumsum(weighted, axis=1) - weighted
        damping_rows = damping(order_one[None])[:, :, 0]
        updated = (damping_rows.T[None, None, :, None, :] * (spectral + below)).astype(jnp.bfloat16)
        backward = jnp.einsum('vlprq,qpi->vlpri', updated.astype(jnp.float32), legendre_table)
        return backward.astype(jnp.bfloat16)
    synthesised = lax.map(spectral_order, (orders, by_order))
    by_slot = jnp.moveaxis(synthesised, (0, 5), (5, 0))

    def synthesise_slot(inputs):
        coeffs, slot_count = inputs
        cos_inner, sin_inner, cos_outer, sin_outer = fourier_tables(slot_count[None], orders, blocks)
        even_parts = coeffs[:, :, 0].astype(jnp.float32)
        odd_parts = coeffs[:, :, 1].astype(jnp.float32)
        hemispheres = jnp.stack([even_parts + odd_parts, even_parts - odd_parts], axis=2)
        kept_mask = 2 * orders < slot_count
        factor = jnp.where(orders == 0, 1.0, 2.0)
        hemispheres = jnp.where(kept_mask, hemispheres, 0.0) * factor
        real_hemisphere = hemispheres[:, :, :, 0][:, :, :, None, :]
        imag_hemisphere = hemispheres[:, :, :, 1][:, :, :, None, :]
        real_phase = cos_outer[0] * real_hemisphere - sin_outer[0] * imag_hemisphere
        imag_phase = sin_outer[0] * real_hemisphere + cos_outer[0] * imag_hemisphere
        stacked = jnp.concatenate([real_phase, imag_phase], axis=-1).astype(jnp.bfloat16)
        dft_table = jnp.concatenate([cos_inner[0], -sin_inner[0]], axis=-1)
        values = jnp.einsum('vlhbc,kc->vlhbk', stacked.astype(jnp.float32), dft_table.astype(jnp.float32))
        flattened = values.reshape(values.shape[:3] + (PPAD,))
        inside = jnp.arange(PPAD) < slot_count
        return jnp.where(inside, flattened, 0.0).astype(jnp.bfloat16)
    result = lax.map(synthesise_slot, (by_slot, counts))
    return jnp.moveaxis(result, 0, 2)
```

```python
import math

import jax
import jax.numpy as jnp
from jax import lax
from jax.experimental import pallas as pl
from jax.experimental.pallas import tpu as pltpu
from jax.sharding import PartitionSpec as P

NT = 1279
NH = 1280
BF = jnp.bfloat16
F32 = jnp.float32
GROUP = 8
STEPS = 32
CHECK = 8
RESCALE_LOG = 60.0 * math.log(2.0)


def iota(shape, dim):
    return lax.broadcasted_iota(jnp.int32, shape, dim)


def turn_cos_sin(turns):
    x = turns * math.pi
    y = x * x
    s = 1.0 / 362880 - y * (1.0 / 39916800)
    s = -1.0 / 5040 + y * s
    s = 1.0 / 120 + y * s
    s = -1.0 / 6 + y * s
    s = x * (1.0 + y * s)
    c = -1.0 / 3628800 + y * (1.0 / 479001600)
    c = 1.0 / 40320 + y * c
    c = -1.0 / 720 + y * c
    c = 1.0 / 24 + y * c
    c = -0.5 + y * c
    c = 1.0 + y * c
    return 1.0 - 2.0 * s * s, 2.0 * s * c


def block_transpose(planes):
    lane = iota((1, 128), 1) // 8
    planes = list(planes)
    for bit in (8, 4, 2, 1):
        low = (lane & bit) == 0
        for at in range(16):
            if at & bit:
                continue
            a, b = planes[at], planes[at | bit]
            planes[at] = jnp.where(low, a, pltpu.roll(b, 8 * bit, 1))
            planes[at | bit] = jnp.where(low, pltpu.roll(a, 128 - 8 * bit, 1), b)
    return planes


def window(i, rows):
    start = i * rows
    base = start // 16 * 16
    return base, start - base


def analyse(grid_field, points, lat_ids, weights, orders, coupling):
    nv, nl, slots, _, width = grid_field.shape
    fields = nv * nl
    blocks = width // 128
    rows = 2 * blocks
    span = -(-(rows + 14) // 16) * 16
    tiles = span // 8
    count = orders.shape[1]
    bands = count // 8
    half = slots // 2
    grid = slots // GROUP
    field = grid_field.reshape(fields, slots, 2, width)

    def kernel(points_ref, lat_ref, weight_ref, coupling_ref, x_ref, order_ref, own_ref, sum_ref, table_ref, phase_ref, staged, planes):
        step = pl.program_id(0)
        for b in range(blocks):
            staged[:, :, b] = x_ref[..., b * 128 : (b + 1) * 128]
        flat = staged.reshape(fields, GROUP * rows, 128)
        order = order_ref[...]
        position = 128 * (iota((span, 128), 0) // 2) + iota((span, 128), 1)
        r8 = iota((8, count), 0)
        r16 = iota((16, count), 0)
        for i in range(GROUP):
            base, off = window(i, rows)
            slot = step * GROUP + i
            period = points_ref[lat_ref[slot]]
            period_v = jnp.full((1, count), period, jnp.int32).astype(F32)
            inverse = 1.0 / period_v
            multiple = jnp.concatenate([8 * r16, r8, 512 * r16, 128 * (r8 // 2 - off // 2)], axis=0).astype(F32)
            product = multiple * order
            turns = (product - jnp.floor(product * inverse + 0.5) * period_v) * inverse
            cosv, sinv = turn_cos_sin(turns)
            fc, fs = cosv[16:24], sinv[16:24]
            parts_c, parts_s = [], []
            for a in range(16):
                ec, es = cosv[a : a + 1], sinv[a : a + 1]
                parts_c.append(ec * fc - es * fs)
                parts_s.append(-(es * fc) - ec * fs)
            table = jnp.concatenate([jnp.concatenate(parts_c, 0), jnp.concatenate(parts_s, 0)], axis=1).astype(BF)
            table_ref[i] = table
            phase_ref[i] = jnp.concatenate([cosv[24:48], sinv[24:48]], axis=1)
            place = position - 64 * off
            keep = jnp.where((place >= 0) & (place < period), 1.0, 0.0).astype(BF)
            data = jnp.concatenate([flat[f, base : base + span, :] * keep for f in range(fields)], axis=0)
            sums = jnp.dot(data, table, preferred_element_type=F32)
            hc, hs = cosv[40:48], sinv[40:48]
            re = [jnp.zeros((8, count), F32) for _ in range(fields)]
            im = [jnp.zeros((8, count), F32) for _ in range(fields)]
            for t in range(tiles):
                gc, gs = cosv[24 + t : 25 + t], sinv[24 + t : 25 + t]
                pc = gc * hc - gs * hs
                ps = gs * hc + gc * hs
                for f in range(fields):
                    at = f * span + 8 * t
                    yr = sums[at : at + 8, :count]
                    yi = sums[at : at + 8, count:]
                    re[f] = re[f] + (pc * yr + ps * yi)
                    im[f] = im[f] + (pc * yi - ps * yr)
            factor = jnp.where(2.0 * order < period_v, weight_ref[slot] * inverse, 0.0)
            for f in range(fields):
                for ri, acc in ((0, re[f]), (1, im[f])):
                    acc = acc + pltpu.roll(acc, 2, 0)
                    acc = acc + pltpu.roll(acc, 4, 0)
                    other = pltpu.roll(acc, 1, 0)
                    planes[2 * f + ri, pl.ds(slot, 1), :] = ((acc + other)[0:1] * factor)
                    planes[2 * fields + 2 * f + ri, pl.ds(slot, 1), :] = ((acc - other)[0:1] * factor)

        @pl.when(step == grid - 1)
        def _():
            for tile in range(count // 128):
                lanes = slice(128 * tile, 128 * tile + 128)
                value = [planes[k, :, lanes].astype(BF).astype(F32) for k in range(16)]
                own, totals = [None] * 16, [None] * 8
                for p in range(2):
                    for v in range(nv):
                        for ri in range(2):
                            running = None
                            for l in range(nl):
                                at = ((p * nv + v) * nl + l) * 2 + ri
                                own[at] = value[at] if running is None else value[at] + running
                                term = coupling_ref[v, l] * value[at]
                                running = term if running is None else running + term
                            totals[(p * nv + v) * 2 + ri] = running
                for d, w in enumerate(block_transpose(own)):
                    own_ref[16 * tile + d] = w.astype(BF)
                packed = [t[:half] for t in totals] + [t[half:] for t in totals]
                for d, w in enumerate(block_transpose(packed)):
                    sum_ref[16 * tile + d] = w.astype(BF)

    smem = pl.BlockSpec(memory_space=pltpu.SMEM)
    return pl.pallas_call(
        kernel,
        name="analyse",
        grid=(grid,),
        in_specs=[
            smem,
            smem,
            smem,
            smem,
            pl.BlockSpec((fields, GROUP, 2, width), lambda i: (0, i, 0, 0)),
            pl.BlockSpec((1, count), lambda i: (0, 0)),
        ],
        out_specs=[
            pl.BlockSpec((bands, slots, 128), lambda i: (0, 0, 0)),
            pl.BlockSpec((bands, half, 128), lambda i: (0, 0, 0)),
            pl.BlockSpec((GROUP, 128, 2 * count), lambda i: (i, 0, 0)),
            pl.BlockSpec((GROUP, 24, 2 * count), lambda i: (i, 0, 0)),
        ],
        out_shape=[
            jax.ShapeDtypeStruct((bands, slots, 128), BF),
            jax.ShapeDtypeStruct((bands, half, 128), BF),
            jax.ShapeDtypeStruct((slots, 128, 2 * count), BF),
            jax.ShapeDtypeStruct((slots, 24, 2 * count), F32),
        ],
        scratch_shapes=[
            pltpu.VMEM((fields, GROUP, blocks, 2, 128), BF),
            pltpu.VMEM((16, slots, count), F32),
        ],
        compiler_params=pltpu.CompilerParams(dimension_semantics=("arbitrary",)),
    )(points, lat_ids, weights, coupling, field, orders)


def legendre(pairs, own, earlier, cosines, start_log, ahead, behind, order_rows, nv, nl):
    bands, slots, _ = own.shape
    half = slots // 2
    total = bands * slots
    chunk = total // 2
    height = 8 * STEPS

    def kernel(pairs_ref, own_ref, earlier_ref, cos_ref, log_ref, ahead_ref, behind_ref, order_ref, out_ref, mixed, weights, even_rows, odd_rows, acc, now, before, log_now):
        source, target = iota((128, 128), 0), iota((128, 128), 1)
        span_l = 16 * nl
        wanted = target // span_l * 16 + target % 16
        pick0 = jnp.where(source == wanted, 1.0, 0.0).astype(BF)
        pick1 = jnp.where(source == wanted + 64, 1.0, 0.0).astype(BF)
        for b in range(bands):
            part = earlier_ref[b]
            top = jnp.dot(part, pick0, preferred_element_type=F32)
            low = jnp.dot(part, pick1, preferred_element_type=F32)
            mixed[b * slots : (b + 1) * slots] = own_ref[b].astype(F32) + jnp.concatenate([top, low], axis=0)
        weights[...] = mixed[...].astype(BF)
        acc[...] = jnp.zeros((128, total), F32)
        now[...] = jnp.ones((8, total), F32)
        before[...] = jnp.zeros((8, total), F32)
        log_now[...] = log_ref[...]
        row, lane = iota((height, 128), 0), iota((height, 128), 1)
        select = (row % 8 == lane % 8) & (row // 8 % 2 == lane // 64)
        degree_base = jnp.concatenate([order_ref[...]] * STEPS, axis=0) + (row // 8).astype(F32)

        def make(block, rows_ref):
            a_all = ahead_ref[block]
            b_all = behind_ref[block]
            for h in range(total // chunk):
                lanes = slice(h * chunk, (h + 1) * chunk)
                current, previous, running = now[:, lanes], before[:, lanes], log_now[:, lanes]
                cosine = cos_ref[:, lanes]
                scale = None
                held = None
                for j in range(STEPS):
                    if j % CHECK == 0:
                        large = jnp.maximum(jnp.abs(current), jnp.abs(previous)) > 1.0
                        shrink = jnp.where(large, 2.0**-60, 1.0)
                        running = running + jnp.where(large, RESCALE_LOG, 0.0)
                        current = current * shrink
                        previous = previous * shrink
                        scale = jnp.exp(running)
                    value = current * scale
                    if j % 2 == 0:
                        held = value
                    else:
                        rows_ref[8 * (j - 1) : 8 * (j + 1), lanes] = jnp.concatenate([held, value], axis=0).astype(BF)
                    a = a_all[:, j : j + 1]
                    b = b_all[:, j : j + 1]
                    current, previous = (a * cosine) * current - b * previous, current
                now[:, lanes] = current
                before[:, lanes] = previous
                log_now[:, lanes] = running

        def use(block, rows_ref):
            rows = rows_ref[...]
            found = jnp.dot(rows, weights[...], preferred_element_type=F32)
            degree = degree_base + (block * STEPS).astype(F32)
            damp = 1.0 / (1.0 + 4.0 * degree * (degree + 1.0) / (NT * (NT + 1.0)))
            kept = jnp.where(select, found * damp, 0.0).astype(BF)
            acc[...] += lax.dot_general(kept, rows, (((0,), (0,)), ((), ())), preferred_element_type=F32)

        make(0, even_rows)

        def body(i, carry):
            make(2 * i + 1, odd_rows)
            use(2 * i, even_rows)
            make(2 * i + 2, even_rows)
            use(2 * i + 1, odd_rows)
            return carry

        lax.fori_loop(0, pairs_ref[0], body, 0)
        for c in range(total // 128):
            mixed[128 * c : 128 * (c + 1)] = jnp.transpose(acc[:, 128 * c : 128 * (c + 1)])
        for b in range(bands):
            out_ref[b] = mixed[b * slots : (b + 1) * slots].astype(BF)

    vmem = pl.BlockSpec(memory_space=pltpu.VMEM)
    return pl.pallas_call(
        kernel,
        name="legendre",
        in_specs=[pl.BlockSpec(memory_space=pltpu.SMEM)] + [vmem] * 7,
        out_specs=vmem,
        out_shape=jax.ShapeDtypeStruct((bands, slots, 128), BF),
        scratch_shapes=[
            pltpu.VMEM((total, 128), F32),
            pltpu.VMEM((total, 128), BF),
            pltpu.VMEM((height, total), BF),
            pltpu.VMEM((height, total), BF),
            pltpu.VMEM((128, total), F32),
            pltpu.VMEM((8, total), F32),
            pltpu.VMEM((8, total), F32),
            pltpu.VMEM((8, total), F32),
        ],
    )(pairs, own, earlier, cosines, start_log, ahead, behind, order_rows)


def synthesise(back, table, phases, points, lat_ids, orders, nv, nl, width):
    bands, slots, _ = back.shape
    fields = nv * nl
    blocks = width // 128
    rows = 2 * blocks
    span = -(-(rows + 14) // 16) * 16
    tiles = span // 8
    count = orders.shape[1]
    grid = slots // GROUP

    def kernel(points_ref, lat_ref, back_ref, table_ref, phase_ref, order_ref, out_ref, planes, waves, staged):
        step = pl.program_id(0)
        result = staged.reshape(fields, GROUP * rows, 128)

        @pl.when(step == 0)
        def _():
            for tile in range(count // 128):
                value = [back_ref[16 * tile + d].astype(F32) for d in range(16)]
                for k, w in enumerate(block_transpose(value)):
                    planes[k, :, 128 * tile : 128 * tile + 128] = w

        order = order_ref[...]
        position = 128 * (iota((span, 128), 0) // 2) + iota((span, 128), 1)
        sign = jnp.where(iota((8, count), 0) % 2 == 0, 1.0, -1.0)
        row8 = iota((8, count), 0)
        for i in range(GROUP):
            base, off = window(i, rows)
            slot = step * GROUP + i
            period = points_ref[lat_ref[slot]]
            period_v = jnp.full((1, count), period, jnp.int32).astype(F32)
            factor = jnp.where(2.0 * order < period_v, jnp.where(order == 0.0, 1.0, 2.0), 0.0)
            hc, hs = phase_ref[i, 16:24, :count], phase_ref[i, 16:24, count:]
            re, im = [], []
            for f in range(fields):
                for ri, keep in ((0, re), (1, im)):
                    even = planes[2 * f + ri, pl.ds(slot, 1), :] * factor
                    odd = planes[2 * fields + 2 * f + ri, pl.ds(slot, 1), :] * factor
                    keep.append(even + sign * odd)
            for t in range(0, tiles, 2):
                pair = []
                for u in (t, t + 1):
                    gc, gs = phase_ref[i, u : u + 1, :count], phase_ref[i, u : u + 1, count:]
                    pc = gc * hc - gs * hs
                    ps = gs * hc + gc * hs
                    if 8 * u < off or 8 * u + 8 > off + rows:
                        valid = (row8 + 8 * u >= off) & (row8 + 8 * u < off + rows)
                        pc = jnp.where(valid, pc, 0.0)
                        ps = jnp.where(valid, ps, 0.0)
                    pair.append((pc, ps))
                for f in range(fields):
                    zr = jnp.concatenate([pc * re[f] - ps * im[f] for pc, ps in pair], axis=0)
                    zi = jnp.concatenate([ps * re[f] + pc * im[f] for pc, ps in pair], axis=0)
                    at = f * span + 8 * t
                    waves[at : at + 16, :count] = zr.astype(BF)
                    waves[at : at + 16, count:] = zi.astype(BF)
            values = lax.dot_general(waves[...], table_ref[i], (((1,), (1,)), ((), ())), preferred_element_type=F32)
            inside = position - 64 * off < period
            for f in range(fields):
                part = jnp.where(inside, values[f * span : (f + 1) * span], 0.0)
                if off:
                    first = part[:16] + result[f, base : base + 16, :].astype(F32)
                    result[f, base : base + 16, :] = first.astype(BF)
                    result[f, base + 16 : base + span, :] = part[16:].astype(BF)
                else:
                    result[f, base : base + span, :] = part.astype(BF)
        for b in range(blocks):
            out_ref[..., b * 128 : (b + 1) * 128] = staged[:, :, b]

    smem = pl.BlockSpec(memory_space=pltpu.SMEM)
    out = pl.pallas_call(
        kernel,
        name="synthesise",
        grid=(grid,),
        in_specs=[
            smem,
            smem,
            pl.BlockSpec((bands, slots, 128), lambda i: (0, 0, 0)),
            pl.BlockSpec((GROUP, 128, 2 * count), lambda i: (i, 0, 0)),
            pl.BlockSpec((GROUP, 24, 2 * count), lambda i: (i, 0, 0)),
            pl.BlockSpec((1, count), lambda i: (0, 0)),
        ],
        out_specs=pl.BlockSpec((fields, GROUP, 2, width), lambda i: (0, i, 0, 0)),
        out_shape=jax.ShapeDtypeStruct((fields, slots, 2, width), BF),
        scratch_shapes=[
            pltpu.VMEM((16, slots, count), F32),
            pltpu.VMEM((fields * span, 2 * count), BF),
            pltpu.VMEM((fields, GROUP, blocks, 2, 128), BF),
        ],
        compiler_params=pltpu.CompilerParams(dimension_semantics=("arbitrary",)),
    )(points, lat_ids, back, table, phases, orders)
    return out.reshape(nv, nl, slots, 2, width)


def recurrence_terms(orders):
    order = orders.astype(F32)[None, :, None]
    blocks = 2 * (-(-(NT + 1) // (2 * STEPS))) + 1
    offset = (jnp.arange(blocks)[:, None] * STEPS + jnp.arange(STEPS)[None, :] + 1).astype(F32)[:, None, :]
    degree = order + offset
    ahead = jnp.sqrt((4.0 * degree * degree - 1.0) / (offset * (2.0 * order + offset)))
    below = 4.0 * (degree - 1.0) * (degree - 1.0) - 1.0
    behind = jnp.sqrt(jnp.maximum((offset - 1.0) * (2.0 * order + offset - 1.0) / below, 0.0))
    ahead = jnp.where(degree <= NT, ahead, 0.0)
    return ahead, ahead * behind


def solution(mesh):
    bands, parts = mesh.shape["band"], mesh.shape["fld"]

    def on_device(grid_field, coupling, points, lat_ids, wn_ids):
        nv, nl, slots, _, width = grid_field.shape
        mine = wn_ids.shape[0]
        packed = jnp.concatenate([wn_ids, lat_ids])
        spread = jnp.broadcast_to(packed[None], (bands, mine + slots))
        known = lax.all_to_all(spread, "band", split_axis=0, concat_axis=0, tiled=True)
        orders = known[:, :mine].reshape(1, bands * mine).astype(F32)
        lats = known[:, mine:].reshape(1, bands * slots).astype(F32)
        weights = math.pi / (2.0 * NH) * jnp.sin(math.pi * (lat_ids.astype(F32) + 0.5) / (2.0 * NH))
        own, sums, table, phases = analyse(grid_field, points, lat_ids, weights, orders, coupling)
        earlier = jnp.zeros_like(sums)
        for shift in range(1, parts):
            moved = lax.ppermute(sums, "fld", [(k, k + shift) for k in range(parts - shift)])
            earlier = moved if shift == 1 else earlier + moved
        own = lax.all_to_all(own, "band", split_axis=0, concat_axis=0, tiled=True)
        earlier = lax.all_to_all(earlier, "band", split_axis=0, concat_axis=0, tiled=True)
        colatitude = math.pi * (lats + 0.5) / (2.0 * NH)
        order = wn_ids.astype(F32)[:, None]
        index = jnp.arange(1, NT + 1).astype(F32)
        log_norm = 0.5 * math.log(0.5) + 0.5 * jnp.sum(
            jnp.where(index[None, :] <= order, jnp.log1p(0.5 / index)[None, :], 0.0), axis=1
        )
        start_log = log_norm[:, None] + order * jnp.log(jnp.sin(colatitude))
        cosines = jnp.broadcast_to(jnp.cos(colatitude), (mine, bands * slots))
        ahead, behind = recurrence_terms(wn_ids)
        longest = NT + 1 - jnp.min(wn_ids)
        pairs = ((longest + 2 * STEPS - 1) // (2 * STEPS)).reshape(1).astype(jnp.int32)
        order_rows = jnp.broadcast_to(order, (mine, 128))
        back = legendre(pairs, own, earlier, cosines, start_log, ahead, behind, order_rows, nv, nl)
        back = lax.all_to_all(back, "band", split_axis=0, concat_axis=0, tiled=True)
        return synthesise(back, table, phases, points, lat_ids, orders, nv, nl, width)

    in_specs = (P(None, "fld", "band", None, None), P(None, "fld"), P(), P("band"), P("band"))
    return jax.shard_map(on_device, mesh=mesh, in_specs=in_specs, out_specs=in_specs[0], check_vma=False)
```

```python
import math

import jax
import jax.numpy as jnp
from jax import lax
from jax.experimental import pallas as pl
from jax.experimental.pallas import tpu as pltpu
from jax.sharding import PartitionSpec as P

NT = 1279
NH = 1280
BF = jnp.bfloat16
F32 = jnp.float32
GROUP = 8
STEPS = 32
CHECK = 8
RESCALE_LOG = 60.0 * math.log(2.0)


def iota(shape, dim):
    return lax.broadcasted_iota(jnp.int32, shape, dim)


def turn_cos_sin(turns):
    x = turns * math.pi
    y = x * x
    s = 1.0 / 362880 - y * (1.0 / 39916800)
    s = -1.0 / 5040 + y * s
    s = 1.0 / 120 + y * s
    s = -1.0 / 6 + y * s
    s = x * (1.0 + y * s)
    c = -1.0 / 3628800 + y * (1.0 / 479001600)
    c = 1.0 / 40320 + y * c
    c = -1.0 / 720 + y * c
    c = 1.0 / 24 + y * c
    c = -0.5 + y * c
    c = 1.0 + y * c
    return 1.0 - 2.0 * s * s, 2.0 * s * c


def block_transpose(planes):
    lane = iota((1, 128), 1) // 8
    planes = list(planes)
    for bit in (8, 4, 2, 1):
        low = (lane & bit) == 0
        for at in range(16):
            if at & bit:
                continue
            a, b = planes[at], planes[at | bit]
            planes[at] = jnp.where(low, a, pltpu.roll(b, 8 * bit, 1))
            planes[at | bit] = jnp.where(low, pltpu.roll(a, 128 - 8 * bit, 1), b)
    return planes


def window(i, rows):
    start = i * rows
    base = start // 16 * 16
    return base, start - base


def analyse(grid_field, points, lat_ids, weights, orders, coupling):
    nv, nl, slots, _, width = grid_field.shape
    fields = nv * nl
    blocks = width // 128
    rows = 2 * blocks
    span = -(-(rows + 14) // 16) * 16
    tiles = span // 8
    count = orders.shape[1]
    bands = count // 8
    grid = slots // GROUP
    field = grid_field.reshape(fields, slots, 2, width)

    def kernel(points_ref, lat_ref, weight_ref, coupling_ref, x_ref, given_ref, own_ref, sum_ref, table_ref, phase_ref, order_ref, staged, planes):
        step = pl.program_id(0)

        @pl.when(step == 0)
        def _():
            order_ref[...] = deal(given_ref[...], bands)

        for b in range(blocks):
            staged[:, :, b] = x_ref[..., b * 128 : (b + 1) * 128]
        flat = staged.reshape(fields, GROUP * rows, 128)
        order = order_ref[...]
        position = 128 * (iota((span, 128), 0) // 2) + iota((span, 128), 1)
        r8 = iota((8, count), 0)
        r16 = iota((16, count), 0)
        for i in range(GROUP):
            base, off = window(i, rows)
            slot = step * GROUP + i
            period = points_ref[lat_ref[slot]]
            period_v = jnp.full((1, count), period, jnp.int32).astype(F32)
            inverse = 1.0 / period_v
            multiple = jnp.concatenate([8 * r16, r8, 512 * r16, 128 * (r8 // 2 - off // 2)], axis=0).astype(F32)
            product = multiple * order
            turns = (product - jnp.floor(product * inverse + 0.5) * period_v) * inverse
            cosv, sinv = turn_cos_sin(turns)
            fc, fs = cosv[16:24], sinv[16:24]
            parts_c, parts_s = [], []
            for a in range(16):
                ec, es = cosv[a : a + 1], sinv[a : a + 1]
                parts_c.append(ec * fc - es * fs)
                parts_s.append(-(es * fc) - ec * fs)
            table = jnp.concatenate([jnp.concatenate(parts_c, 0), jnp.concatenate(parts_s, 0)], axis=1).astype(BF)
            table_ref[i] = table
            phase_ref[i] = jnp.concatenate([cosv[24:48], sinv[24:48]], axis=1)
            place = position - 64 * off
            keep = jnp.where((place >= 0) & (place < period), 1.0, 0.0).astype(BF)
            data = jnp.concatenate([flat[f, base : base + span, :] * keep for f in range(fields)], axis=0)
            sums = jnp.dot(data, table, preferred_element_type=F32)
            hc, hs = cosv[40:48], sinv[40:48]
            re = [jnp.zeros((8, count), F32) for _ in range(fields)]
            im = [jnp.zeros((8, count), F32) for _ in range(fields)]
            for t in range(tiles):
                gc, gs = cosv[24 + t : 25 + t], sinv[24 + t : 25 + t]
                pc = gc * hc - gs * hs
                ps = gs * hc + gc * hs
                for f in range(fields):
                    at = f * span + 8 * t
                    yr = sums[at : at + 8, :count]
                    yi = sums[at : at + 8, count:]
                    re[f] = re[f] + (pc * yr + ps * yi)
                    im[f] = im[f] + (pc * yi - ps * yr)
            factor = jnp.where(2.0 * order < period_v, weight_ref[slot] * inverse, 0.0)
            for f in range(fields):
                for ri, acc in ((0, re[f]), (1, im[f])):
                    acc = acc + pltpu.roll(acc, 2, 0)
                    acc = acc + pltpu.roll(acc, 4, 0)
                    other = pltpu.roll(acc, 1, 0)
                    planes[2 * f + ri, pl.ds(slot, 1), :] = ((acc + other)[0:1] * factor)
                    planes[2 * fields + 2 * f + ri, pl.ds(slot, 1), :] = ((acc - other)[0:1] * factor)

        @pl.when(step == grid - 1)
        def _():
            for p in range(2):
                for v in range(nv):
                    for ri in range(2):
                        running = None
                        for l in range(nl):
                            at = ((p * nv + v) * nl + l) * 2 + ri
                            value = planes[at].astype(BF).astype(F32)
                            own_ref[at] = value if running is None else value + running
                            term = coupling_ref[v, l] * value
                            running = term if running is None else running + term
                        sum_ref[(p * nv + v) * 2 + ri] = running.astype(BF)

    smem = pl.BlockSpec(memory_space=pltpu.SMEM)
    return pl.pallas_call(
        kernel,
        name="analyse",
        grid=(grid,),
        in_specs=[
            smem,
            smem,
            smem,
            smem,
            pl.BlockSpec((fields, GROUP, 2, width), lambda i: (0, i, 0, 0)),
            pl.BlockSpec((1, count), lambda i: (0, 0)),
        ],
        out_specs=[
            pl.BlockSpec((16, slots, count), lambda i: (0, 0, 0)),
            pl.BlockSpec((16 // nl, slots, count), lambda i: (0, 0, 0)),
            pl.BlockSpec((GROUP, 128, 2 * count), lambda i: (i, 0, 0)),
            pl.BlockSpec((GROUP, 24, 2 * count), lambda i: (i, 0, 0)),
            pl.BlockSpec((1, count), lambda i: (0, 0)),
        ],
        out_shape=[
            jax.ShapeDtypeStruct((16, slots, count), F32),
            jax.ShapeDtypeStruct((16 // nl, slots, count), BF),
            jax.ShapeDtypeStruct((slots, 128, 2 * count), BF),
            jax.ShapeDtypeStruct((slots, 24, 2 * count), F32),
            jax.ShapeDtypeStruct((1, count), F32),
        ],
        scratch_shapes=[
            pltpu.VMEM((fields, GROUP, blocks, 2, 128), BF),
            pltpu.VMEM((16, slots, count), F32),
        ],
        compiler_params=pltpu.CompilerParams(dimension_semantics=("arbitrary",)),
    )(points, lat_ids, weights, coupling, field, orders)


def deal(row, bands):
    count = row.shape[1]
    line, lane = iota((count, count), 0), iota((count, count), 1)
    column = jnp.sum(jnp.where(line == lane, row, 0.0), axis=1, keepdims=True)
    rank = jnp.sum(jnp.where(row < column, 1.0, 0.0), axis=1, keepdims=True).astype(jnp.int32)
    upper = rank >= count // 2
    pair = jnp.where(upper, count - 1 - rank, rank)
    place = pair % bands * 8 + pair // bands * 2 + jnp.where(upper, 1, 0)
    return jnp.sum(jnp.where(place == lane, column, 0.0), axis=0, keepdims=True)


def mix(own, earlier, bands, nv, nl):
    _, slots, count = own.shape

    def kernel(own_ref, earlier_ref, out_ref):
        for tile in range(count // 128):
            lanes = slice(128 * tile, 128 * tile + 128)
            value = []
            for k in range(16):
                source = k // (2 * nl) * 2 + k % 2
                value.append(own_ref[k, :, lanes] + earlier_ref[source, :, lanes].astype(F32))
            for d, w in enumerate(block_transpose(value)):
                out_ref[16 * tile + d] = w.astype(BF)

    return pl.pallas_call(kernel, name="mix", out_shape=jax.ShapeDtypeStruct((bands, slots, 128), BF))(own, earlier)


def legendre(pairs, own, cosines, first_log, second_log, terms):
    bands, slots, _ = own.shape
    total = bands * slots
    half = total // 2
    height = 8 * STEPS

    def kernel(pairs_ref, own_ref, cos_ref, first_ref, second_ref, term_ref, out_ref, mixed, weights, even_rows, odd_rows, acc, now, before, log_now):
        for b in range(bands):
            mixed[b * slots : (b + 1) * slots] = own_ref[b].astype(F32)
        weights[...] = jnp.concatenate([mixed[:half], mixed[half:]], axis=1).astype(BF)
        acc[...] = jnp.zeros((256, half), F32)
        now[...] = jnp.ones((8, half), F32)
        before[...] = jnp.zeros((8, half), F32)
        log_now[...] = first_ref[...]
        line, lane = iota((8, 128), 0), iota((8, 128), 1)
        low = line < 4

        def make(block, rows_ref):
            info = term_ref[block]
            restart = jnp.broadcast_to(info[:, 97:98], (8, half)) > 0.5
            current = jnp.where(restart, 1.0, now[...])
            previous = jnp.where(restart, 0.0, before[...])
            running = jnp.where(restart, second_ref[...], log_now[...])
            cosine = cos_ref[...]
            scale = None
            held = None
            for j in range(STEPS):
                if j % CHECK == 0:
                    large = jnp.maximum(jnp.abs(current), jnp.abs(previous)) > 1.0
                    shrink = jnp.where(large, 2.0**-60, 1.0)
                    running = running + jnp.where(large, RESCALE_LOG, 0.0)
                    current = current * shrink
                    previous = previous * shrink
                    scale = jnp.exp(running)
                value = current * scale
                if j % 2 == 0:
                    held = value
                else:
                    rows_ref[8 * (j - 1) : 8 * (j + 1), :] = jnp.concatenate([held, value], axis=0).astype(BF)
                a = info[:, j : j + 1]
                b = info[:, STEPS + j : STEPS + j + 1]
                current, previous = (a * cosine) * current - b * previous, current
            now[...] = current
            before[...] = previous
            log_now[...] = running

        def use(block, rows_ref):
            info = term_ref[block]
            rows = rows_ref[...]
            found = jnp.dot(rows, weights[...], preferred_element_type=F32)
            which = jnp.broadcast_to(info[:, 96:97], (8, 128)).astype(jnp.int32)
            hit = lane % 8 == which
            masks = []
            for parity in range(2):
                match = hit & (lane // 64 == parity)
                masks.append((match & low, match & ~low))
            tops, lows = [], []
            for j in range(STEPS):
                part = found[8 * j : 8 * j + 8]
                part = jnp.where(low, part[:, :128], part[:, 128:])
                part = (part + pltpu.roll(part, 4, 0)) * info[:, 2 * STEPS + j : 2 * STEPS + j + 1]
                tops.append(jnp.where(masks[j % 2][0], part, 0.0))
                lows.append(jnp.where(masks[j % 2][1], part, 0.0))
            kept = jnp.concatenate([jnp.concatenate(tops, axis=0), jnp.concatenate(lows, axis=0)], axis=1).astype(BF)
            acc[...] += lax.dot_general(kept, rows, (((0,), (0,)), ((), ())), preferred_element_type=F32)

        make(0, even_rows)

        def body(i, carry):
            make(2 * i + 1, odd_rows)
            use(2 * i, even_rows)
            make(2 * i + 2, even_rows)
            use(2 * i + 1, odd_rows)
            return carry

        lax.fori_loop(0, pairs_ref[0], body, 0)
        for h in range(2):
            for c in range(half // 128):
                at = h * half + 128 * c
                mixed[at : at + 128] = jnp.transpose(acc[128 * h : 128 * h + 128, 128 * c : 128 * c + 128])
        for b in range(bands):
            out_ref[b] = mixed[b * slots : (b + 1) * slots].astype(BF)

    vmem = pl.BlockSpec(memory_space=pltpu.VMEM)
    return pl.pallas_call(
        kernel,
        name="legendre",
        in_specs=[pl.BlockSpec(memory_space=pltpu.SMEM)] + [vmem] * 5,
        out_specs=vmem,
        out_shape=jax.ShapeDtypeStruct((bands, slots, 128), BF),
        scratch_shapes=[
            pltpu.VMEM((total, 128), F32),
            pltpu.VMEM((half, 256), BF),
            pltpu.VMEM((height, half), BF),
            pltpu.VMEM((height, half), BF),
            pltpu.VMEM((256, half), F32),
            pltpu.VMEM((8, half), F32),
            pltpu.VMEM((8, half), F32),
            pltpu.VMEM((8, half), F32),
        ],
    )(pairs, own, cosines, first_log, second_log, terms)


def synthesise(back, table, phases, points, lat_ids, orders, nv, nl, width):
    bands, slots, _ = back.shape
    fields = nv * nl
    blocks = width // 128
    rows = 2 * blocks
    span = -(-(rows + 14) // 16) * 16
    tiles = span // 8
    count = orders.shape[1]
    grid = slots // GROUP

    def kernel(points_ref, lat_ref, back_ref, table_ref, phase_ref, order_ref, out_ref, planes, waves, staged):
        step = pl.program_id(0)
        result = staged.reshape(fields, GROUP * rows, 128)

        @pl.when(step == 0)
        def _():
            for tile in range(count // 128):
                value = [back_ref[16 * tile + d].astype(F32) for d in range(16)]
                for k, w in enumerate(block_transpose(value)):
                    planes[k, :, 128 * tile : 128 * tile + 128] = w

        order = order_ref[...]
        position = 128 * (iota((span, 128), 0) // 2) + iota((span, 128), 1)
        sign = jnp.where(iota((8, count), 0) % 2 == 0, 1.0, -1.0)
        row8 = iota((8, count), 0)
        for i in range(GROUP):
            base, off = window(i, rows)
            slot = step * GROUP + i
            period = points_ref[lat_ref[slot]]
            period_v = jnp.full((1, count), period, jnp.int32).astype(F32)
            factor = jnp.where(2.0 * order < period_v, jnp.where(order == 0.0, 1.0, 2.0), 0.0)
            hc, hs = phase_ref[i, 16:24, :count], phase_ref[i, 16:24, count:]
            re, im = [], []
            for f in range(fields):
                for ri, keep in ((0, re), (1, im)):
                    even = planes[2 * f + ri, pl.ds(slot, 1), :] * factor
                    odd = planes[2 * fields + 2 * f + ri, pl.ds(slot, 1), :] * factor
                    keep.append(even + sign * odd)
            for t in range(0, tiles, 2):
                pair = []
                for u in (t, t + 1):
                    gc, gs = phase_ref[i, u : u + 1, :count], phase_ref[i, u : u + 1, count:]
                    pc = gc * hc - gs * hs
                    ps = gs * hc + gc * hs
                    if 8 * u < off or 8 * u + 8 > off + rows:
                        valid = (row8 + 8 * u >= off) & (row8 + 8 * u < off + rows)
                        pc = jnp.where(valid, pc, 0.0)
                        ps = jnp.where(valid, ps, 0.0)
                    pair.append((pc, ps))
                for f in range(fields):
                    zr = jnp.concatenate([pc * re[f] - ps * im[f] for pc, ps in pair], axis=0)
                    zi = jnp.concatenate([ps * re[f] + pc * im[f] for pc, ps in pair], axis=0)
                    at = f * span + 8 * t
                    waves[at : at + 16, :count] = zr.astype(BF)
                    waves[at : at + 16, count:] = zi.astype(BF)
            values = lax.dot_general(waves[...], table_ref[i], (((1,), (1,)), ((), ())), preferred_element_type=F32)
            inside = position - 64 * off < period
            for f in range(fields):
                part = jnp.where(inside, values[f * span : (f + 1) * span], 0.0)
                if off:
                    first = part[:16] + result[f, base : base + 16, :].astype(F32)
                    result[f, base : base + 16, :] = first.astype(BF)
                    result[f, base + 16 : base + span, :] = part[16:].astype(BF)
                else:
                    result[f, base : base + span, :] = part.astype(BF)
        for b in range(blocks):
            out_ref[..., b * 128 : (b + 1) * 128] = staged[:, :, b]

    smem = pl.BlockSpec(memory_space=pltpu.SMEM)
    out = pl.pallas_call(
        kernel,
        name="synthesise",
        grid=(grid,),
        in_specs=[
            smem,
            smem,
            pl.BlockSpec((bands, slots, 128), lambda i: (0, 0, 0)),
            pl.BlockSpec((GROUP, 128, 2 * count), lambda i: (i, 0, 0)),
            pl.BlockSpec((GROUP, 24, 2 * count), lambda i: (i, 0, 0)),
            pl.BlockSpec((1, count), lambda i: (0, 0)),
        ],
        out_specs=pl.BlockSpec((fields, GROUP, 2, width), lambda i: (0, i, 0, 0)),
        out_shape=jax.ShapeDtypeStruct((fields, slots, 2, width), BF),
        scratch_shapes=[
            pltpu.VMEM((16, slots, count), F32),
            pltpu.VMEM((fields * span, 2 * count), BF),
            pltpu.VMEM((fields, GROUP, blocks, 2, 128), BF),
        ],
        compiler_params=pltpu.CompilerParams(dimension_semantics=("arbitrary",)),
    )(points, lat_ids, back, table, phases, orders)
    return out.reshape(nv, nl, slots, 2, width)


def recurrence_terms(mine):
    first, second = mine[0::2], mine[1::2]
    ends = jnp.floor((NT + STEPS - first) / STEPS)
    stops = ends + jnp.floor((NT + STEPS - second) / STEPS)
    pairs = jnp.floor((jnp.max(stops) + 1.0) / 2.0).astype(jnp.int32).reshape(1)
    blocks = 4 * (-(-(NT + 1) // (2 * STEPS))) + 2
    block = jnp.arange(blocks).astype(F32)[:, None]
    late = block >= ends[None]
    order = jnp.tile(jnp.where(late, second[None], first[None]), (1, 2))[:, :, None]
    start = jnp.tile(STEPS * jnp.where(late, block - ends[None], block), (1, 2))[:, :, None]
    which = jnp.tile(2.0 * jnp.arange(4).astype(F32)[None] + late, (1, 2))[:, :, None]
    restart = jnp.tile((block == ends[None]).astype(F32), (1, 2))[:, :, None]
    lane = jnp.arange(128)[None, None, :]
    step = (lane % STEPS).astype(F32)
    offset = start + step + 1.0
    degree = order + offset
    ahead = jnp.sqrt((4.0 * degree * degree - 1.0) / (offset * (2.0 * order + offset)))
    below = 4.0 * (degree - 1.0) * (degree - 1.0) - 1.0
    behind = jnp.sqrt(jnp.maximum((offset - 1.0) * (2.0 * order + offset - 1.0) / below, 0.0))
    ahead = jnp.where(degree <= NT, ahead, 0.0)
    row = order + start + step
    damp = 1.0 / (1.0 + 4.0 * row * (row + 1.0) / (NT * (NT + 1.0)))
    kind = lane // STEPS
    last = jnp.where(lane == 96, which, restart)
    terms = jnp.where(kind == 0, ahead, jnp.where(kind == 1, ahead * behind, jnp.where(kind == 2, damp, last)))
    return pairs, terms


def solution(mesh):
    bands, parts = mesh.shape["band"], mesh.shape["fld"]

    def on_device(grid_field, coupling, points, lat_ids, wn_ids):
        nv, nl, slots, _, width = grid_field.shape
        mine = wn_ids.shape[0]
        packed = jnp.concatenate([wn_ids, lat_ids])
        spread = jnp.broadcast_to(packed[None], (bands, mine + slots))
        known = lax.all_to_all(spread, "band", split_axis=0, concat_axis=0, tiled=True)
        orders = known[:, :mine].reshape(1, bands * mine).astype(F32)
        lats = known[:, mine:].reshape(1, bands * slots).astype(F32)
        weights = math.pi / (2.0 * NH) * jnp.sin(math.pi * (lat_ids.astype(F32) + 0.5) / (2.0 * NH))
        own, sums, table, phases, orders = analyse(grid_field, points, lat_ids, weights, orders, coupling)
        earlier = jnp.zeros_like(sums)
        for shift in range(1, parts):
            moved = lax.ppermute(sums, "fld", [(k, k + shift) for k in range(parts - shift)])
            earlier = moved if shift == 1 else earlier + moved
        own = mix(own, earlier, bands, nv, nl)
        own = lax.all_to_all(own, "band", split_axis=0, concat_axis=0, tiled=True)
        half = bands * slots // 2
        colatitude = (math.pi * (lats + 0.5) / (2.0 * NH)).reshape(2, 1, half)
        local = lax.dynamic_index_in_dim(orders.reshape(bands, mine), lax.axis_index("band"), 0, False)
        index = jnp.arange(1, NT + 1).astype(F32)
        log_norm = 0.5 * math.log(0.5) + 0.5 * jnp.sum(
            jnp.where(index[None, :] <= local[:, None], jnp.log1p(0.5 / index)[None, :], 0.0), axis=1
        )
        log_sine = jnp.log(jnp.sin(colatitude))
        start_log = log_norm[None, :, None] + local[None, :, None] * log_sine
        first_log = start_log[:, 0::2].reshape(mine, half)
        second_log = start_log[:, 1::2].reshape(mine, half)
        cosines = jnp.broadcast_to(jnp.cos(colatitude), (2, mine // 2, half)).reshape(mine, half)
        pairs, terms = recurrence_terms(local)
        back = legendre(pairs, own, cosines, first_log, second_log, terms)
        back = lax.all_to_all(back, "band", split_axis=0, concat_axis=0, tiled=True)
        return synthesise(back, table, phases, points, lat_ids, orders, nv, nl, width)

    in_specs = (P(None, "fld", "band", None, None), P(None, "fld"), P(), P("band"), P("band"))
    return jax.shard_map(on_device, mesh=mesh, in_specs=in_specs, out_specs=in_specs[0], check_vma=False)
```

```python
import math

import jax
import jax.numpy as jnp
from jax import lax
from jax.experimental import pallas as pl
from jax.experimental.pallas import tpu as pltpu
from jax.sharding import PartitionSpec as P

NT = 1279
NH = 1280
BF = jnp.bfloat16
F32 = jnp.float32
GROUP = 8
STEPS = 32
CHECK = 8
RESCALE_LOG = 60.0 * math.log(2.0)


def iota(shape, dim):
    return lax.broadcasted_iota(jnp.int32, shape, dim)


def turn_cos_sin(turns):
    x = turns * math.pi
    y = x * x
    s = 1.0 / 362880 - y * (1.0 / 39916800)
    s = -1.0 / 5040 + y * s
    s = 1.0 / 120 + y * s
    s = -1.0 / 6 + y * s
    s = x * (1.0 + y * s)
    c = -1.0 / 3628800 + y * (1.0 / 479001600)
    c = 1.0 / 40320 + y * c
    c = -1.0 / 720 + y * c
    c = 1.0 / 24 + y * c
    c = -0.5 + y * c
    c = 1.0 + y * c
    return 1.0 - 2.0 * s * s, 2.0 * s * c


def block_transpose(planes):
    lane = iota((1, 128), 1) // 8
    planes = list(planes)
    for bit in (8, 4, 2, 1):
        low = (lane & bit) == 0
        for at in range(16):
            if at & bit:
                continue
            a, b = planes[at], planes[at | bit]
            planes[at] = jnp.where(low, a, pltpu.roll(b, 8 * bit, 1))
            planes[at | bit] = jnp.where(low, pltpu.roll(a, 128 - 8 * bit, 1), b)
    return planes


def padded_rows(width):
    pairs = -(-(width // 128) // 2)
    return 2 * (-(-pairs // 8) * 8)


def regroup(field):
    fields, slots, _, width = field.shape
    blocks = width // 128
    depth = padded_rows(width) // 2

    def kernel(x_ref, even_ref, odd_ref):
        for b in range(2 * depth):
            target = odd_ref if b % 2 else even_ref
            if b < blocks:
                target[:, :, b // 2] = x_ref[..., b * 128 : (b + 1) * 128]
            else:
                target[:, :, b // 2] = jnp.zeros((fields, GROUP, 2, 128), BF)

    spec = pl.BlockSpec((fields, GROUP, depth, 2, 128), lambda i: (0, i, 0, 0, 0))
    shape = jax.ShapeDtypeStruct((fields, slots, depth, 2, 128), BF)
    even, odd = pl.pallas_call(
        kernel,
        name="regroup",
        grid=(slots // GROUP,),
        in_specs=[pl.BlockSpec((fields, GROUP, 2, width), lambda i: (0, i, 0, 0))],
        out_specs=[spec, spec],
        out_shape=[shape, shape],
        compiler_params=pltpu.CompilerParams(dimension_semantics=("arbitrary",)),
    )(field)
    return even.reshape(fields, slots * 2 * depth, 128), odd.reshape(fields, slots * 2 * depth, 128)


def analyse(even, odd, points, lat_ids, weights, orders, coupling, nv, nl):
    fields = nv * nl
    slots = lat_ids.shape[0]
    rows = even.shape[1] // slots
    tiles = rows // 8
    count = orders.shape[1]
    bands = count // 8
    grid = slots // GROUP

    def kernel(points_ref, lat_ref, weight_ref, coupling_ref, even_ref, odd_ref, given_ref, own_ref, sum_ref, table_ref, phase_ref, order_ref, planes):
        step = pl.program_id(0)

        @pl.when(step == 0)
        def _():
            order_ref[...] = deal(given_ref[...], bands)

        order = order_ref[...]
        position = (256 * (iota((rows, 256), 0) // 2) + iota((rows, 256), 1)).astype(F32)
        r8, r16 = iota((8, count), 0), iota((16, count), 0)
        multiple = jnp.concatenate([16 * r16, r16, 1024 * r8, 256 * (r8 // 2)], axis=0).astype(F32)
        product = multiple * order
        for i in range(GROUP):
            slot = step * GROUP + i
            period = points_ref[lat_ref[slot]]
            period_v = jnp.full((1, count), period, jnp.int32).astype(F32)
            inverse = 1.0 / period_v
            turns = (product - jnp.floor(product * inverse + 0.5) * period_v) * inverse
            cosv, sinv = turn_cos_sin(turns)
            fc, fs = cosv[16:32], sinv[16:32]
            parts_c, parts_s = [], []
            for a in range(16):
                ec, es = cosv[a : a + 1], sinv[a : a + 1]
                parts_c.append((ec * fc - es * fs).astype(BF))
                parts_s.append(((-es) * fc - ec * fs).astype(BF))
            table = jnp.concatenate([jnp.concatenate(parts_c, 0), jnp.concatenate(parts_s, 0)], axis=1)
            table_ref[i] = table
            phase_ref[i] = jnp.concatenate([cosv[32:48], sinv[32:48]], axis=1)
            limit = jnp.full((1, 256), period, jnp.int32).astype(F32)
            keep = jnp.minimum(jnp.maximum(limit - position, 0.0), 1.0).astype(BF)
            lines = slice(i * rows, (i + 1) * rows)
            data = jnp.concatenate(
                [jnp.concatenate([even_ref[f, lines], odd_ref[f, lines]], axis=1) * keep for f in range(fields)], axis=0
            )
            sums = jnp.dot(data, table, preferred_element_type=F32)
            hc, hs = cosv[40:48], sinv[40:48]
            re = [None] * fields
            im = [None] * fields
            for t in range(tiles):
                gc, gs = cosv[32 + t : 33 + t], sinv[32 + t : 33 + t]
                pc = gc * hc - gs * hs
                ps = gs * hc + gc * hs
                for f in range(fields):
                    at = f * rows + 8 * t
                    yr = sums[at : at + 8, :count]
                    yi = sums[at : at + 8, count:]
                    r = pc * yr + ps * yi
                    q = pc * yi - ps * yr
                    re[f] = r if t == 0 else re[f] + r
                    im[f] = q if t == 0 else im[f] + q
            factor = jnp.where(2.0 * order < period_v, weight_ref[slot] * inverse, 0.0)
            for f in range(fields):
                for ri, acc in ((0, re[f]), (1, im[f])):
                    acc = acc + pltpu.roll(acc, 2, 0)
                    acc = acc + pltpu.roll(acc, 4, 0)
                    other = pltpu.roll(acc, 1, 0)
                    planes[2 * f + ri, pl.ds(slot, 1), :] = (acc + other)[0:1] * factor
                    planes[2 * fields + 2 * f + ri, pl.ds(slot, 1), :] = (acc - other)[0:1] * factor

        @pl.when(step == grid - 1)
        def _():
            for p in range(2):
                for v in range(nv):
                    for ri in range(2):
                        running = None
                        for l in range(nl):
                            at = ((p * nv + v) * nl + l) * 2 + ri
                            value = planes[at].astype(BF).astype(F32)
                            own_ref[at] = value if running is None else value + running
                            term = coupling_ref[v, l] * value
                            running = term if running is None else running + term
                        sum_ref[(p * nv + v) * 2 + ri] = running.astype(BF)

    smem = pl.BlockSpec(memory_space=pltpu.SMEM)
    data_spec = pl.BlockSpec((fields, GROUP * rows, 128), lambda i: (0, i, 0))
    return pl.pallas_call(
        kernel,
        name="analyse",
        grid=(grid,),
        in_specs=[smem, smem, smem, smem, data_spec, data_spec, pl.BlockSpec((1, count), lambda i: (0, 0))],
        out_specs=[
            pl.BlockSpec((16, slots, count), lambda i: (0, 0, 0)),
            pl.BlockSpec((16 // nl, slots, count), lambda i: (0, 0, 0)),
            pl.BlockSpec((GROUP, 256, 2 * count), lambda i: (i, 0, 0)),
            pl.BlockSpec((GROUP, 16, 2 * count), lambda i: (i, 0, 0)),
            pl.BlockSpec((1, count), lambda i: (0, 0)),
        ],
        out_shape=[
            jax.ShapeDtypeStruct((16, slots, count), F32),
            jax.ShapeDtypeStruct((16 // nl, slots, count), BF),
            jax.ShapeDtypeStruct((slots, 256, 2 * count), BF),
            jax.ShapeDtypeStruct((slots, 16, 2 * count), F32),
            jax.ShapeDtypeStruct((1, count), F32),
        ],
        scratch_shapes=[pltpu.VMEM((16, slots, count), F32)],
        compiler_params=pltpu.CompilerParams(dimension_semantics=("arbitrary",)),
    )(points, lat_ids, weights, coupling, even, odd, orders)


def deal(row, bands):
    count = row.shape[1]
    line, lane = iota((count, count), 0), iota((count, count), 1)
    column = jnp.sum(jnp.where(line == lane, row, 0.0), axis=1, keepdims=True)
    rank = jnp.sum(jnp.where(row < column, 1.0, 0.0), axis=1, keepdims=True).astype(jnp.int32)
    upper = rank >= count // 2
    pair = jnp.where(upper, count - 1 - rank, rank)
    place = pair % bands * 8 + pair // bands * 2 + jnp.where(upper, 1, 0)
    return jnp.sum(jnp.where(place == lane, column, 0.0), axis=0, keepdims=True)


def mix(own, earlier, bands, nv, nl):
    _, slots, count = own.shape

    def kernel(own_ref, earlier_ref, out_ref):
        for tile in range(count // 128):
            lanes = slice(128 * tile, 128 * tile + 128)
            value = []
            for k in range(16):
                source = k // (2 * nl) * 2 + k % 2
                value.append(own_ref[k, :, lanes] + earlier_ref[source, :, lanes].astype(F32))
            for d, w in enumerate(block_transpose(value)):
                out_ref[16 * tile + d] = w.astype(BF)

    return pl.pallas_call(kernel, name="mix", out_shape=jax.ShapeDtypeStruct((bands, slots, 128), BF))(own, earlier)


def legendre(pairs, own, cosines, first_log, second_log, terms):
    bands, slots, _ = own.shape
    total = bands * slots
    half = total // 2
    height = 8 * STEPS

    def kernel(pairs_ref, own_ref, cos_ref, first_ref, second_ref, term_ref, out_ref, mixed, weights, even_rows, odd_rows, acc, now, before, log_now):
        for b in range(bands):
            mixed[b * slots : (b + 1) * slots] = own_ref[b].astype(F32)
        weights[...] = jnp.concatenate([mixed[:half], mixed[half:]], axis=1).astype(BF)
        acc[...] = jnp.zeros((256, half), F32)
        now[...] = jnp.ones((8, half), F32)
        before[...] = jnp.zeros((8, half), F32)
        log_now[...] = first_ref[...]
        line, lane = iota((8, 128), 0), iota((8, 128), 1)
        low = line < 4

        def make(block, rows_ref):
            info = term_ref[block]
            restart = jnp.broadcast_to(info[:, 97:98], (8, half)) > 0.5
            current = jnp.where(restart, 1.0, now[...])
            previous = jnp.where(restart, 0.0, before[...])
            running = jnp.where(restart, second_ref[...], log_now[...])
            cosine = cos_ref[...]
            scale = None
            held = None
            for j in range(STEPS):
                if j % CHECK == 0:
                    large = jnp.maximum(jnp.abs(current), jnp.abs(previous)) > 1.0
                    shrink = jnp.where(large, 2.0**-60, 1.0)
                    running = running + jnp.where(large, RESCALE_LOG, 0.0)
                    current = current * shrink
                    previous = previous * shrink
                    scale = jnp.exp(running)
                value = current * scale
                if j % 2 == 0:
                    held = value
                else:
                    rows_ref[8 * (j - 1) : 8 * (j + 1), :] = jnp.concatenate([held, value], axis=0).astype(BF)
                a = info[:, j : j + 1]
                b = info[:, STEPS + j : STEPS + j + 1]
                current, previous = (a * cosine) * current - b * previous, current
            now[...] = current
            before[...] = previous
            log_now[...] = running

        def use(block, rows_ref):
            info = term_ref[block]
            rows = rows_ref[...]
            found = jnp.dot(rows, weights[...], preferred_element_type=F32)
            which = jnp.broadcast_to(info[:, 96:97], (8, 128)).astype(jnp.int32)
            hit = lane % 8 == which
            masks = []
            for parity in range(2):
                match = hit & (lane // 64 == parity)
                masks.append((match & low, match & ~low))
            tops, lows = [], []
            for j in range(STEPS):
                part = found[8 * j : 8 * j + 8]
                part = jnp.where(low, part[:, :128], part[:, 128:])
                part = (part + pltpu.roll(part, 4, 0)) * info[:, 2 * STEPS + j : 2 * STEPS + j + 1]
                tops.append(jnp.where(masks[j % 2][0], part, 0.0))
                lows.append(jnp.where(masks[j % 2][1], part, 0.0))
            kept = jnp.concatenate([jnp.concatenate(tops, axis=0), jnp.concatenate(lows, axis=0)], axis=1).astype(BF)
            acc[...] += lax.dot_general(kept, rows, (((0,), (0,)), ((), ())), preferred_element_type=F32)

        make(0, even_rows)

        def body(i, carry):
            make(2 * i + 1, odd_rows)
            use(2 * i, even_rows)
            make(2 * i + 2, even_rows)
            use(2 * i + 1, odd_rows)
            return carry

        lax.fori_loop(0, pairs_ref[0], body, 0)
        for h in range(2):
            for c in range(half // 128):
                at = h * half + 128 * c
                mixed[at : at + 128] = jnp.transpose(acc[128 * h : 128 * h + 128, 128 * c : 128 * c + 128])
        for b in range(bands):
            out_ref[b] = mixed[b * slots : (b + 1) * slots].astype(BF)

    vmem = pl.BlockSpec(memory_space=pltpu.VMEM)
    return pl.pallas_call(
        kernel,
        name="legendre",
        in_specs=[pl.BlockSpec(memory_space=pltpu.SMEM)] + [vmem] * 5,
        out_specs=vmem,
        out_shape=jax.ShapeDtypeStruct((bands, slots, 128), BF),
        scratch_shapes=[
            pltpu.VMEM((total, 128), F32),
            pltpu.VMEM((half, 256), BF),
            pltpu.VMEM((height, half), BF),
            pltpu.VMEM((height, half), BF),
            pltpu.VMEM((256, half), F32),
            pltpu.VMEM((8, half), F32),
            pltpu.VMEM((8, half), F32),
            pltpu.VMEM((8, half), F32),
        ],
    )(pairs, own, cosines, first_log, second_log, terms)


def synthesise(back, table, phases, points, lat_ids, orders, nv, nl, width):
    bands, slots, _ = back.shape
    fields = nv * nl
    blocks = width // 128
    rows = padded_rows(width)
    tiles = rows // 8
    count = orders.shape[1]
    grid = slots // GROUP

    def kernel(points_ref, lat_ref, back_ref, table_ref, phase_ref, order_ref, out_ref, planes):
        step = pl.program_id(0)

        @pl.when(step == 0)
        def _():
            for tile in range(count // 128):
                value = [back_ref[16 * tile + d].astype(F32) for d in range(16)]
                for k, w in enumerate(block_transpose(value)):
                    planes[k, :, 128 * tile : 128 * tile + 128] = w

        order = order_ref[...]
        position = 256 * (iota((rows, 256), 0) // 2) + iota((rows, 256), 1)
        sign = jnp.where(iota((8, count), 0) % 2 == 0, 1.0, -1.0)
        double = jnp.where(order == 0.0, 1.0, 2.0)
        for i in range(GROUP):
            slot = step * GROUP + i
            period = points_ref[lat_ref[slot]]
            period_v = jnp.full((1, count), period, jnp.int32).astype(F32)
            factor = jnp.where(2.0 * order < period_v, double, 0.0)
            hc, hs = phase_ref[i, 8:16, :count], phase_ref[i, 8:16, count:]
            re, im = [], []
            for f in range(fields):
                for ri, keep in ((0, re), (1, im)):
                    even = planes[2 * f + ri, pl.ds(slot, 1), :] * factor
                    odd = planes[2 * fields + 2 * f + ri, pl.ds(slot, 1), :] * factor
                    keep.append(even + sign * odd)
            parts = [[] for _ in range(fields)]
            for t in range(0, tiles, 2):
                pair = []
                for u in (t, t + 1):
                    gc, gs = phase_ref[i, u : u + 1, :count], phase_ref[i, u : u + 1, count:]
                    pair.append((gc * hc - gs * hs, gs * hc + gc * hs))
                for f in range(fields):
                    zr = jnp.concatenate([pc * re[f] - ps * im[f] for pc, ps in pair], axis=0)
                    zi = jnp.concatenate([ps * re[f] + pc * im[f] for pc, ps in pair], axis=0)
                    parts[f].append(jnp.concatenate([zr.astype(BF), zi.astype(BF)], axis=1))
            waves = jnp.concatenate([jnp.concatenate(p, axis=0) for p in parts], axis=0)
            values = lax.dot_general(waves, table_ref[i], (((1,), (1,)), ((), ())), preferred_element_type=F32)
            inside = position < period
            for f in range(fields):
                part = jnp.where(inside, values[f * rows : (f + 1) * rows], 0.0).astype(BF)
                for b in range(blocks):
                    at, lane = b // 2 * 2, b % 2 * 128
                    out_ref[f, i, :, b * 128 : (b + 1) * 128] = part[at : at + 2, lane : lane + 128]

    smem = pl.BlockSpec(memory_space=pltpu.SMEM)
    out = pl.pallas_call(
        kernel,
        name="synthesise",
        grid=(grid,),
        in_specs=[
            smem,
            smem,
            pl.BlockSpec((bands, slots, 128), lambda i: (0, 0, 0)),
            pl.BlockSpec((GROUP, 256, 2 * count), lambda i: (i, 0, 0)),
            pl.BlockSpec((GROUP, 16, 2 * count), lambda i: (i, 0, 0)),
            pl.BlockSpec((1, count), lambda i: (0, 0)),
        ],
        out_specs=pl.BlockSpec((fields, GROUP, 2, width), lambda i: (0, i, 0, 0)),
        out_shape=jax.ShapeDtypeStruct((fields, slots, 2, width), BF),
        scratch_shapes=[pltpu.VMEM((16, slots, count), F32)],
        compiler_params=pltpu.CompilerParams(dimension_semantics=("arbitrary",)),
    )(points, lat_ids, back, table, phases, orders)
    return out.reshape(nv, nl, slots, 2, width)


def recurrence_terms(mine):
    first, second = mine[0::2], mine[1::2]
    ends = jnp.floor((NT + STEPS - first) / STEPS)
    stops = ends + jnp.floor((NT + STEPS - second) / STEPS)
    pairs = jnp.floor((jnp.max(stops) + 1.0) / 2.0).astype(jnp.int32).reshape(1)
    blocks = 4 * (-(-(NT + 1) // (2 * STEPS))) + 2
    block = jnp.arange(blocks).astype(F32)[:, None]
    late = block >= ends[None]
    order = jnp.tile(jnp.where(late, second[None], first[None]), (1, 2))[:, :, None]
    start = jnp.tile(STEPS * jnp.where(late, block - ends[None], block), (1, 2))[:, :, None]
    which = jnp.tile(2.0 * jnp.arange(4).astype(F32)[None] + late, (1, 2))[:, :, None]
    restart = jnp.tile((block == ends[None]).astype(F32), (1, 2))[:, :, None]
    lane = jnp.arange(128)[None, None, :]
    step = (lane % STEPS).astype(F32)
    offset = start + step + 1.0
    degree = order + offset
    ahead = jnp.sqrt((4.0 * degree * degree - 1.0) / (offset * (2.0 * order + offset)))
    below = 4.0 * (degree - 1.0) * (degree - 1.0) - 1.0
    behind = jnp.sqrt(jnp.maximum((offset - 1.0) * (2.0 * order + offset - 1.0) / below, 0.0))
    ahead = jnp.where(degree <= NT, ahead, 0.0)
    row = order + start + step
    damp = 1.0 / (1.0 + 4.0 * row * (row + 1.0) / (NT * (NT + 1.0)))
    kind = lane // STEPS
    last = jnp.where(lane == 96, which, restart)
    terms = jnp.where(kind == 0, ahead, jnp.where(kind == 1, ahead * behind, jnp.where(kind == 2, damp, last)))
    return pairs, terms


def solution(mesh):
    bands, parts = mesh.shape["band"], mesh.shape["fld"]

    def on_device(grid_field, coupling, points, lat_ids, wn_ids):
        nv, nl, slots, _, width = grid_field.shape
        mine = wn_ids.shape[0]
        even, odd = regroup(grid_field.reshape(nv * nl, slots, 2, width))
        packed = jnp.concatenate([wn_ids, lat_ids])
        spread = jnp.broadcast_to(packed[None], (bands, mine + slots))
        known = lax.all_to_all(spread, "band", split_axis=0, concat_axis=0, tiled=True)
        orders = known[:, :mine].reshape(1, bands * mine).astype(F32)
        lats = known[:, mine:].reshape(1, bands * slots).astype(F32)
        weights = math.pi / (2.0 * NH) * jnp.sin(math.pi * (lat_ids.astype(F32) + 0.5) / (2.0 * NH))
        own, sums, table, phases, orders = analyse(even, odd, points, lat_ids, weights, orders, coupling, nv, nl)
        earlier = jnp.zeros_like(sums)
        for shift in range(1, parts):
            moved = lax.ppermute(sums, "fld", [(k, k + shift) for k in range(parts - shift)])
            earlier = moved if shift == 1 else earlier + moved
        own = mix(own, earlier, bands, nv, nl)
        own = lax.all_to_all(own, "band", split_axis=0, concat_axis=0, tiled=True)
        half = bands * slots // 2
        colatitude = (math.pi * (lats + 0.5) / (2.0 * NH)).reshape(2, 1, half)
        local = lax.dynamic_index_in_dim(orders.reshape(bands, mine), lax.axis_index("band"), 0, False)
        index = jnp.arange(1, NT + 1).astype(F32)
        log_norm = 0.5 * math.log(0.5) + 0.5 * jnp.sum(
            jnp.where(index[None, :] <= local[:, None], jnp.log1p(0.5 / index)[None, :], 0.0), axis=1
        )
        log_sine = jnp.log(jnp.sin(colatitude))
        start_log = log_norm[None, :, None] + local[None, :, None] * log_sine
        first_log = start_log[:, 0::2].reshape(mine, half)
        second_log = start_log[:, 1::2].reshape(mine, half)
        cosines = jnp.broadcast_to(jnp.cos(colatitude), (2, mine // 2, half)).reshape(mine, half)
        pairs, terms = recurrence_terms(local)
        back = legendre(pairs, own, cosines, first_log, second_log, terms)
        back = lax.all_to_all(back, "band", split_axis=0, concat_axis=0, tiled=True)
        return synthesise(back, table, phases, points, lat_ids, orders, nv, nl, width)

    in_specs = (P(None, "fld", "band", None, None), P(None, "fld"), P(), P("band"), P("band"))
    return jax.shard_map(on_device, mesh=mesh, in_specs=in_specs, out_specs=in_specs[0], check_vma=False)
```

```python
import math

import jax
import jax.numpy as jnp
from jax import lax
from jax.experimental import pallas as pl
from jax.experimental.pallas import tpu as pltpu
from jax.experimental.layout import Layout, with_layout_constraint
from jax.sharding import PartitionSpec as P

NT = 1279
NH = 1280
BF = jnp.bfloat16
F32 = jnp.float32
GROUP = 8
STEPS = 32
CHECK = 8
RESCALE_LOG = 60.0 * math.log(2.0)


def iota(shape, dim):
    return lax.broadcasted_iota(jnp.int32, shape, dim)


def turn_cos_sin(turns):
    y = turns * turns
    s = -0.59828975 + y * 0.07765416
    s = 2.55007732 + y * s
    s = -5.16771007 + y * s
    s = turns * (3.14159264 + y * s)
    c = -1.33187126 + y * 0.21967748
    c = 4.05841064 + y * c
    c = -4.9347928 + y * c
    c = 0.99999995 + y * c
    twice = s + s
    return 1.0 - twice * s, twice * c


def block_transpose(planes):
    lane = iota((1, 128), 1) // 8
    planes = list(planes)
    for bit in (8, 4, 2, 1):
        low = (lane & bit) == 0
        for at in range(16):
            if at & bit:
                continue
            a, b = planes[at], planes[at | bit]
            planes[at] = jnp.where(low, a, pltpu.roll(b, 8 * bit, 1))
            planes[at | bit] = jnp.where(low, pltpu.roll(a, 128 - 8 * bit, 1), b)
    return planes


def window(i, rows):
    start = i * rows
    base = start // 16 * 16
    return base, start - base


def window_rows(width):
    return -(-(2 * (width // 128) + 14) // 16) * 16


def as_rows(field):
    nv, nl, slots, _, width = field.shape
    blocks = width // 128
    split = field.reshape(nv, nl, slots, 2, blocks, 128)
    split = with_layout_constraint(split, Layout(major_to_minor=(0, 1, 2, 4, 3, 5)))
    return split.transpose(0, 1, 2, 4, 3, 5).reshape(nv * nl, slots * 2 * blocks, 128)


def from_rows(rows, nv, nl, slots, width):
    split = rows.reshape(nv, nl, slots, width // 128, 2, 128).transpose(0, 1, 2, 4, 3, 5)
    split = with_layout_constraint(split, Layout(major_to_minor=(0, 1, 2, 4, 3, 5)))
    return split.reshape(nv, nl, slots, 2, width)


def angle_rows(order, tiles):
    count = order.shape[1]
    row = iota((8, count), 0)
    steps = jnp.where(row < tiles // 2, 256 * (2 * row + 1), 64)
    shared = jnp.concatenate([row, 8 * row, steps], axis=0).astype(F32) * order
    blocks = (128 * (2 * tiles - 2 + row // 2)).astype(F32)
    return shared, blocks


def slot_angles(shared, blocks, order, off, period):
    product = jnp.concatenate([shared, (blocks - 64.0 * off) * order], axis=0)
    period_v = jnp.full(order.shape, period, jnp.int32).astype(F32)
    inverse = 1.0 / period_v
    turns = (product - jnp.floor(product * inverse + 0.5) * period_v) * inverse
    cosv, sinv = turn_cos_sin(turns)
    return cosv, sinv, period_v, inverse


def inner_table(cosv, sinv):
    fc, fs = cosv[0:8], sinv[0:8]
    ec, es = cosv[8:16], sinv[8:16]
    wc, ws = cosv[23:24], sinv[23:24]
    ec = jnp.concatenate([ec, ec * wc - es * ws], axis=0)
    es = jnp.concatenate([es, es * wc + cosv[8:16] * ws], axis=0)
    parts_c, parts_s = [], []
    for a in range(16):
        c, s = ec[a : a + 1], es[a : a + 1]
        parts_c.append(c * fc - s * fs)
        parts_s.append((-s) * fc - c * fs)
    halves = [jnp.concatenate(p, axis=0).astype(BF) for p in (parts_c, parts_s)]
    return jnp.concatenate(halves, axis=1)


def analyse(points_rows, points, lat_ids, weights, orders, coupling, nv, nl, width):
    fields = nv * nl
    slots = lat_ids.shape[0]
    rows = 2 * (width // 128)
    span = window_rows(width)
    tiles = span // 8
    middle = tiles // 2
    count = orders.shape[1]
    bands = count // 8
    grid = slots // GROUP

    def kernel(points_ref, lat_ref, weight_ref, coupling_ref, x_ref, given_ref, own_ref, sum_ref, order_ref, planes):
        step = pl.program_id(0)

        @pl.when(step == 0)
        def _():
            order_ref[...] = deal(given_ref[...], bands)

        order = order_ref[...]
        position = (128 * (iota((span, 128), 0) // 2) + iota((span, 128), 1)).astype(F32)
        shared, blocks = angle_rows(order, tiles)
        for i in range(GROUP):
            base, off = window(i, rows)
            slot = step * GROUP + i
            period = points_ref[lat_ref[slot]]
            cosv, sinv, period_v, inverse = slot_angles(shared, blocks, order, off, period)
            table = inner_table(cosv, sinv)
            limit = jnp.full((1, 128), period, jnp.int32).astype(F32) + 64.0 * off
            keep = jnp.minimum(jnp.maximum(limit - position, 0.0), 1.0)
            if off:
                head = jnp.where(position[:16] >= 64.0 * off, keep[:16], 0.0)
                keep = jnp.concatenate([head, keep[16:]], axis=0)
            keep = keep.astype(BF)
            data = jnp.concatenate([x_ref[f, base : base + span, :] * keep for f in range(fields)], axis=0)
            sums = jnp.dot(data, table, preferred_element_type=F32)
            re = [None] * fields
            im = [None] * fields
            for u in range(middle):
                c, s = cosv[16 + u : 17 + u], sinv[16 + u : 17 + u]
                for f in range(fields):
                    up = f * span + 8 * (middle + u)
                    down = f * span + 8 * (middle - 1 - u)
                    ur, ui = sums[up : up + 8, :count], sums[up : up + 8, count:]
                    dr, di = sums[down : down + 8, :count], sums[down : down + 8, count:]
                    r = c * (ur + dr) + s * (ui - di)
                    q = c * (ui + di) - s * (ur - dr)
                    re[f] = r if u == 0 else re[f] + r
                    im[f] = q if u == 0 else im[f] + q
            factor = jnp.where(2.0 * order < period_v, weight_ref[slot] * inverse, 0.0)
            hc, hs = cosv[24:32] * factor, sinv[24:32] * factor
            for f in range(fields):
                turned = (hc * re[f] + hs * im[f], hc * im[f] - hs * re[f])
                for ri, acc in enumerate(turned):
                    acc = acc + pltpu.roll(acc, 2, 0)
                    acc = acc + pltpu.roll(acc, 4, 0)
                    other = pltpu.roll(acc, 1, 0)
                    planes[2 * f + ri, pl.ds(slot, 1), :] = (acc + other)[0:1]
                    planes[2 * fields + 2 * f + ri, pl.ds(slot, 1), :] = (acc - other)[0:1]

        @pl.when(step == grid - 1)
        def _():
            for p in range(2):
                for v in range(nv):
                    for ri in range(2):
                        running = None
                        for l in range(nl):
                            at = ((p * nv + v) * nl + l) * 2 + ri
                            value = planes[at].astype(BF).astype(F32)
                            own_ref[at] = value if running is None else value + running
                            term = coupling_ref[v, l] * value
                            running = term if running is None else running + term
                        sum_ref[(p * nv + v) * 2 + ri] = running.astype(BF)

    smem = pl.BlockSpec(memory_space=pltpu.SMEM)
    return pl.pallas_call(
        kernel,
        name="analyse",
        grid=(grid,),
        in_specs=[
            smem,
            smem,
            smem,
            smem,
            pl.BlockSpec((fields, GROUP * rows, 128), lambda i: (0, i, 0)),
            pl.BlockSpec((1, count), lambda i: (0, 0)),
        ],
        out_specs=[
            pl.BlockSpec((16, slots, count), lambda i: (0, 0, 0)),
            pl.BlockSpec((16 // nl, slots, count), lambda i: (0, 0, 0)),
            pl.BlockSpec((1, count), lambda i: (0, 0)),
        ],
        out_shape=[
            jax.ShapeDtypeStruct((16, slots, count), F32),
            jax.ShapeDtypeStruct((16 // nl, slots, count), BF),
            jax.ShapeDtypeStruct((1, count), F32),
        ],
        scratch_shapes=[pltpu.VMEM((16, slots, count), F32)],
        compiler_params=pltpu.CompilerParams(dimension_semantics=("arbitrary",)),
    )(points, lat_ids, weights, coupling, points_rows, orders)


def deal(row, bands):
    count = row.shape[1]
    line, lane = iota((count, count), 0), iota((count, count), 1)
    column = jnp.sum(jnp.where(line == lane, row, 0.0), axis=1, keepdims=True)
    rank = jnp.sum(jnp.where(row < column, 1.0, 0.0), axis=1, keepdims=True).astype(jnp.int32)
    upper = rank >= count // 2
    pair = jnp.where(upper, count - 1 - rank, rank)
    place = pair % bands * 8 + pair // bands * 2 + jnp.where(upper, 1, 0)
    return jnp.sum(jnp.where(place == lane, column, 0.0), axis=0, keepdims=True)


def mix(own, earlier, bands, nv, nl):
    _, slots, count = own.shape

    def kernel(own_ref, earlier_ref, out_ref):
        for tile in range(count // 128):
            lanes = slice(128 * tile, 128 * tile + 128)
            value = []
            for k in range(16):
                source = k // (2 * nl) * 2 + k % 2
                value.append(own_ref[k, :, lanes] + earlier_ref[source, :, lanes].astype(F32))
            for d, w in enumerate(block_transpose(value)):
                out_ref[16 * tile + d] = w.astype(BF)

    return pl.pallas_call(kernel, name="mix", out_shape=jax.ShapeDtypeStruct((bands, slots, 128), BF))(own, earlier)


def legendre(pairs, own, cosines, first_log, second_log, terms):
    bands, slots, _ = own.shape
    total = bands * slots
    half = total // 2
    height = 8 * STEPS

    def kernel(pairs_ref, own_ref, cos_ref, first_ref, second_ref, term_ref, out_ref, mixed, weights, even_rows, odd_rows, acc, now, before, log_now):
        for b in range(bands):
            mixed[b * slots : (b + 1) * slots] = own_ref[b].astype(F32)
        weights[...] = jnp.concatenate([mixed[:half], mixed[half:]], axis=1).astype(BF)
        acc[...] = jnp.zeros((256, half), F32)
        now[...] = jnp.ones((8, half), F32)
        before[...] = jnp.zeros((8, half), F32)
        log_now[...] = first_ref[...]
        line, lane = iota((8, 128), 0), iota((8, 128), 1)
        low = line < 4

        def make(block, rows_ref):
            info = term_ref[block]
            restart = jnp.broadcast_to(info[:, 97:98], (8, half)) > 0.5
            current = jnp.where(restart, 1.0, now[...])
            previous = jnp.where(restart, 0.0, before[...])
            running = jnp.where(restart, second_ref[...], log_now[...])
            cosine = cos_ref[...]
            scale = None
            held = None
            for j in range(STEPS):
                if j % CHECK == 0:
                    large = jnp.maximum(jnp.abs(current), jnp.abs(previous)) > 1.0
                    shrink = jnp.where(large, 2.0**-60, 1.0)
                    running = running + jnp.where(large, RESCALE_LOG, 0.0)
                    current = current * shrink
                    previous = previous * shrink
                    scale = jnp.exp(running)
                value = current * scale
                if j % 2 == 0:
                    held = value
                else:
                    rows_ref[8 * (j - 1) : 8 * (j + 1), :] = jnp.concatenate([held, value], axis=0).astype(BF)
                a = info[:, j : j + 1]
                b = info[:, STEPS + j : STEPS + j + 1]
                current, previous = (a * cosine) * current - b * previous, current
            now[...] = current
            before[...] = previous
            log_now[...] = running

        def use(block, rows_ref):
            info = term_ref[block]
            rows = rows_ref[...]
            found = jnp.dot(rows, weights[...], preferred_element_type=F32)
            which = jnp.broadcast_to(info[:, 96:97], (8, 128)).astype(jnp.int32)
            hit = lane % 8 == which
            masks = []
            for parity in range(2):
                match = hit & (lane // 64 == parity)
                masks.append((match & low, match & ~low))
            tops, lows = [], []
            for j in range(STEPS):
                part = found[8 * j : 8 * j + 8]
                part = jnp.where(low, part[:, :128], part[:, 128:])
                part = (part + pltpu.roll(part, 4, 0)) * info[:, 2 * STEPS + j : 2 * STEPS + j + 1]
                tops.append(jnp.where(masks[j % 2][0], part, 0.0))
                lows.append(jnp.where(masks[j % 2][1], part, 0.0))
            kept = jnp.concatenate([jnp.concatenate(tops, axis=0), jnp.concatenate(lows, axis=0)], axis=1).astype(BF)
            acc[...] += lax.dot_general(kept, rows, (((0,), (0,)), ((), ())), preferred_element_type=F32)

        make(0, even_rows)

        def body(i, carry):
            make(2 * i + 1, odd_rows)
            use(2 * i, even_rows)
            make(2 * i + 2, even_rows)
            use(2 * i + 1, odd_rows)
            return carry

        lax.fori_loop(0, pairs_ref[0], body, 0)
        for h in range(2):
            for c in range(half // 128):
                at = h * half + 128 * c
                mixed[at : at + 128] = jnp.transpose(acc[128 * h : 128 * h + 128, 128 * c : 128 * c + 128])
        for b in range(bands):
            out_ref[b] = mixed[b * slots : (b + 1) * slots].astype(BF)

    vmem = pl.BlockSpec(memory_space=pltpu.VMEM)
    return pl.pallas_call(
        kernel,
        name="legendre",
        in_specs=[pl.BlockSpec(memory_space=pltpu.SMEM)] + [vmem] * 5,
        out_specs=vmem,
        out_shape=jax.ShapeDtypeStruct((bands, slots, 128), BF),
        scratch_shapes=[
            pltpu.VMEM((total, 128), F32),
            pltpu.VMEM((half, 256), BF),
            pltpu.VMEM((height, half), BF),
            pltpu.VMEM((height, half), BF),
            pltpu.VMEM((256, half), F32),
            pltpu.VMEM((8, half), F32),
            pltpu.VMEM((8, half), F32),
            pltpu.VMEM((8, half), F32),
        ],
    )(pairs, own, cosines, first_log, second_log, terms)


def synthesise(back, points, lat_ids, orders, nv, nl, width):
    bands, slots, _ = back.shape
    fields = nv * nl
    rows = 2 * (width // 128)
    span = window_rows(width)
    tiles = span // 8
    middle = tiles // 2
    count = orders.shape[1]
    grid = slots // GROUP

    def kernel(points_ref, lat_ref, back_ref, order_ref, out_ref, planes):
        step = pl.program_id(0)

        @pl.when(step == 0)
        def _():
            for tile in range(count // 128):
                value = [back_ref[16 * tile + d].astype(F32) for d in range(16)]
                for k, w in enumerate(block_transpose(value)):
                    planes[k, :, 128 * tile : 128 * tile + 128] = w

        order = order_ref[...]
        position = 128 * (iota((span, 128), 0) // 2) + iota((span, 128), 1)
        shared, blocks = angle_rows(order, tiles)
        sign = jnp.where(iota((8, count), 0) % 2 == 0, 1.0, -1.0)
        double = jnp.where(order == 0.0, 1.0, 2.0)
        for i in range(GROUP):
            base, off = window(i, rows)
            slot = step * GROUP + i
            period = points_ref[lat_ref[slot]]
            cosv, sinv, period_v, _ = slot_angles(shared, blocks, order, off, period)
            table = inner_table(cosv, sinv)
            factor = jnp.where(2.0 * order < period_v, double, 0.0)
            hc, hs = cosv[24:32] * factor, sinv[24:32] * factor
            parts = []
            for f in range(fields):
                both = []
                for ri in range(2):
                    even = planes[2 * f + ri, pl.ds(slot, 1), :]
                    odd = planes[2 * fields + 2 * f + ri, pl.ds(slot, 1), :]
                    both.append(even + sign * odd)
                re, im = both
                wr, wi = hc * re - hs * im, hs * re + hc * im
                zr, zi = [None] * tiles, [None] * tiles
                for u in range(middle):
                    c, s = cosv[16 + u : 17 + u], sinv[16 + u : 17 + u]
                    cr, si, ci, sr = c * wr, s * wi, c * wi, s * wr
                    zr[middle + u], zr[middle - 1 - u] = cr - si, cr + si
                    zi[middle + u], zi[middle - 1 - u] = ci + sr, ci - sr
                parts.append(jnp.concatenate([jnp.concatenate(zr, 0).astype(BF), jnp.concatenate(zi, 0).astype(BF)], axis=1))
            waves = jnp.concatenate(parts, axis=0)
            values = lax.dot_general(waves, table, (((1,), (1,)), ((), ())), preferred_element_type=F32)
            inside = position < period + 64 * off
            starts = position[:16] >= 64 * off
            for f in range(fields):
                part = jnp.where(inside, values[f * span : (f + 1) * span], 0.0)
                if off:
                    first = jnp.where(starts, part[:16], out_ref[f, base : base + 16, :].astype(F32))
                    out_ref[f, base : base + 16, :] = first.astype(BF)
                    out_ref[f, base + 16 : base + span, :] = part[16:].astype(BF)
                else:
                    out_ref[f, base : base + span, :] = part.astype(BF)

    smem = pl.BlockSpec(memory_space=pltpu.SMEM)
    return pl.pallas_call(
        kernel,
        name="synthesise",
        grid=(grid,),
        in_specs=[
            smem,
            smem,
            pl.BlockSpec((bands, slots, 128), lambda i: (0, 0, 0)),
            pl.BlockSpec((1, count), lambda i: (0, 0)),
        ],
        out_specs=pl.BlockSpec((fields, GROUP * rows, 128), lambda i: (0, i, 0)),
        out_shape=jax.ShapeDtypeStruct((fields, slots * rows, 128), BF),
        scratch_shapes=[pltpu.VMEM((16, slots, count), F32)],
        compiler_params=pltpu.CompilerParams(dimension_semantics=("arbitrary",)),
    )(points, lat_ids, back, orders)


def recurrence_terms(mine):
    first, second = mine[0::2], mine[1::2]
    ends = jnp.floor((NT + STEPS - first) / STEPS)
    stops = ends + jnp.floor((NT + STEPS - second) / STEPS)
    pairs = jnp.floor((jnp.max(stops) + 1.0) / 2.0).astype(jnp.int32).reshape(1)
    blocks = 4 * (-(-(NT + 1) // (2 * STEPS))) + 2
    block = jnp.arange(blocks).astype(F32)[:, None]
    late = block >= ends[None]
    order = jnp.tile(jnp.where(late, second[None], first[None]), (1, 2))[:, :, None]
    start = jnp.tile(STEPS * jnp.where(late, block - ends[None], block), (1, 2))[:, :, None]
    which = jnp.tile(2.0 * jnp.arange(4).astype(F32)[None] + late, (1, 2))[:, :, None]
    restart = jnp.tile((block == ends[None]).astype(F32), (1, 2))[:, :, None]
    lane = jnp.arange(128)[None, None, :]
    step = (lane % STEPS).astype(F32)
    offset = start + step + 1.0
    degree = order + offset
    ahead = jnp.sqrt((4.0 * degree * degree - 1.0) / (offset * (2.0 * order + offset)))
    below = 4.0 * (degree - 1.0) * (degree - 1.0) - 1.0
    behind = jnp.sqrt(jnp.maximum((offset - 1.0) * (2.0 * order + offset - 1.0) / below, 0.0))
    ahead = jnp.where(degree <= NT, ahead, 0.0)
    row = order + start + step
    damp = 1.0 / (1.0 + 4.0 * row * (row + 1.0) / (NT * (NT + 1.0)))
    kind = lane // STEPS
    last = jnp.where(lane == 96, which, restart)
    terms = jnp.where(kind == 0, ahead, jnp.where(kind == 1, ahead * behind, jnp.where(kind == 2, damp, last)))
    return pairs, terms


def solution(mesh):
    bands, parts = mesh.shape["band"], mesh.shape["fld"]

    def on_device(grid_field, coupling, points, lat_ids, wn_ids):
        nv, nl, slots, _, width = grid_field.shape
        mine = wn_ids.shape[0]
        packed = jnp.concatenate([wn_ids, lat_ids])
        spread = jnp.broadcast_to(packed[None], (bands, mine + slots))
        known = lax.all_to_all(spread, "band", split_axis=0, concat_axis=0, tiled=True)
        orders = known[:, :mine].reshape(1, bands * mine).astype(F32)
        lats = known[:, mine:].reshape(1, bands * slots).astype(F32)
        weights = math.pi / (2.0 * NH) * jnp.sin(math.pi * (lat_ids.astype(F32) + 0.5) / (2.0 * NH))
        own, sums, orders = analyse(as_rows(grid_field), points, lat_ids, weights, orders, coupling, nv, nl, width)
        earlier = jnp.zeros_like(sums)
        for shift in range(1, parts):
            moved = lax.ppermute(sums, "fld", [(k, k + shift) for k in range(parts - shift)])
            earlier = moved if shift == 1 else earlier + moved
        own, orders = lax.optimization_barrier((mix(own, earlier, bands, nv, nl), orders))
        own = lax.all_to_all(own, "band", split_axis=0, concat_axis=0, tiled=True)
        half = bands * slots // 2
        colatitude = (math.pi * (lats + 0.5) / (2.0 * NH)).reshape(2, 1, half)
        local = lax.dynamic_index_in_dim(orders.reshape(bands, mine), lax.axis_index("band"), 0, False)
        index = jnp.arange(1, NT + 1).astype(F32)
        log_norm = 0.5 * math.log(0.5) + 0.5 * jnp.sum(
            jnp.where(index[None, :] <= local[:, None], jnp.log1p(0.5 / index)[None, :], 0.0), axis=1
        )
        log_sine = jnp.log(jnp.sin(colatitude))
        start_log = log_norm[None, :, None] + local[None, :, None] * log_sine
        first_log = start_log[:, 0::2].reshape(mine, half)
        second_log = start_log[:, 1::2].reshape(mine, half)
        cosines = jnp.broadcast_to(jnp.cos(colatitude), (2, mine // 2, half)).reshape(mine, half)
        pairs, terms = recurrence_terms(local)
        back = legendre(pairs, own, cosines, first_log, second_log, terms)
        back = lax.all_to_all(back, "band", split_axis=0, concat_axis=0, tiled=True)
        rows = synthesise(back, points, lat_ids, orders, nv, nl, width)
        return from_rows(rows, nv, nl, slots, width)

    in_specs = (P(None, "fld", "band", None, None), P(None, "fld"), P(), P("band"), P("band"))
    return jax.shard_map(on_device, mesh=mesh, in_specs=in_specs, out_specs=in_specs[0], check_vma=False)
```

```python
import math

import jax
import jax.numpy as jnp
from jax import lax
from jax.experimental import pallas as pl
from jax.experimental.pallas import tpu as pltpu
from jax.experimental.layout import Layout, with_layout_constraint
from jax.sharding import PartitionSpec as P

NT = 1279
NH = 1280
BF = jnp.bfloat16
F32 = jnp.float32
GROUP = 8
STEPS = 32
CHECK = 8
RESCALE_LOG = 60.0 * math.log(2.0)
EARLY = 16
WIDE = 2


def iota(shape, dim):
    return lax.broadcasted_iota(jnp.int32, shape, dim)


def turn_cos_sin(turns):
    y = turns * turns
    s = -0.59828975 + y * 0.07765416
    s = 2.55007732 + y * s
    s = -5.16771007 + y * s
    s = turns * (3.14159264 + y * s)
    c = -1.33187126 + y * 0.21967748
    c = 4.05841064 + y * c
    c = -4.9347928 + y * c
    c = 0.99999995 + y * c
    twice = s + s
    return 1.0 - twice * s, twice * c


def block_transpose(planes):
    lane = iota((1, 128), 1) // 8
    planes = list(planes)
    for bit in (8, 4, 2, 1):
        low = (lane & bit) == 0
        for at in range(16):
            if at & bit:
                continue
            a, b = planes[at], planes[at | bit]
            planes[at] = jnp.where(low, a, pltpu.roll(b, 8 * bit, 1))
            planes[at | bit] = jnp.where(low, pltpu.roll(a, 128 - 8 * bit, 1), b)
    return planes


def window(i, rows):
    start = i * rows
    base = start // 16 * 16
    return base, start - base


def window_rows(width):
    return -(-(2 * (width // 128) + 14) // 16) * 16


def as_rows(field):
    nv, nl, slots, _, width = field.shape
    blocks = width // 128
    split = field.reshape(nv, nl, slots, 2, blocks, 128)
    split = with_layout_constraint(split, Layout(major_to_minor=(0, 1, 2, 4, 3, 5)))
    return split.transpose(0, 1, 2, 4, 3, 5).reshape(nv * nl, slots * 2 * blocks, 128)


def from_rows(rows, nv, nl, slots, width):
    split = rows.reshape(nv, nl, slots, width // 128, 2, 128).transpose(0, 1, 2, 4, 3, 5)
    split = with_layout_constraint(split, Layout(major_to_minor=(0, 1, 2, 4, 3, 5)))
    return split.reshape(nv, nl, slots, 2, width)


def angle_rows(order, tiles):
    count = order.shape[1]
    row = iota((8, count), 0)
    steps = jnp.where(row < tiles // 2, 256 * (2 * row + 1), 64)
    shared = jnp.concatenate([row, 8 * row, steps], axis=0).astype(F32) * order
    blocks = (128 * (2 * tiles - 2 + row // 2)).astype(F32)
    return shared, blocks


def slot_angles(shared, blocks, order, off, period):
    product = jnp.concatenate([shared, (blocks - 64.0 * off) * order], axis=0)
    period_v = jnp.full(order.shape, period, jnp.int32).astype(F32)
    inverse = 1.0 / period_v
    turns = (product - jnp.floor(product * inverse + 0.5) * period_v) * inverse
    cosv, sinv = turn_cos_sin(turns)
    return cosv, sinv, period_v, inverse


def inner_table(cosv, sinv):
    fc, fs = cosv[0:8], sinv[0:8]
    ec, es = cosv[8:16], sinv[8:16]
    wc, ws = cosv[23:24], sinv[23:24]
    ec = jnp.concatenate([ec, ec * wc - es * ws], axis=0)
    es = jnp.concatenate([es, es * wc + cosv[8:16] * ws], axis=0)
    parts_c, parts_s = [], []
    for a in range(16):
        c, s = ec[a : a + 1], es[a : a + 1]
        parts_c.append(c * fc - s * fs)
        parts_s.append((-s) * fc - c * fs)
    halves = [jnp.concatenate(p, axis=0).astype(BF) for p in (parts_c, parts_s)]
    return jnp.concatenate(halves, axis=1)


def analyse(points_rows, points, lat_ids, weights, orders, coupling, nv, nl, width):
    fields = nv * nl
    slots = lat_ids.shape[0]
    rows = 2 * (width // 128)
    span = window_rows(width)
    tiles = span // 8
    middle = tiles // 2
    count = orders.shape[1]
    bands = count // 8
    grid = slots // GROUP

    def kernel(points_ref, lat_ref, weight_ref, coupling_ref, x_ref, given_ref, own_ref, sum_ref, order_ref, planes):
        step = pl.program_id(0)

        @pl.when(step == 0)
        def _():
            order_ref[...] = deal(given_ref[...], bands)

        order = order_ref[...]
        position = (128 * (iota((span, 128), 0) // 2) + iota((span, 128), 1)).astype(F32)
        shared, blocks = angle_rows(order, tiles)
        for i in range(GROUP):
            base, off = window(i, rows)
            slot = step * GROUP + i
            period = points_ref[lat_ref[slot]]
            cosv, sinv, period_v, inverse = slot_angles(shared, blocks, order, off, period)
            table = inner_table(cosv, sinv)
            limit = jnp.full((1, 128), period, jnp.int32).astype(F32) + 64.0 * off
            keep = jnp.minimum(jnp.maximum(limit - position, 0.0), 1.0)
            if off:
                head = jnp.where(position[:16] >= 64.0 * off, keep[:16], 0.0)
                keep = jnp.concatenate([head, keep[16:]], axis=0)
            keep = keep.astype(BF)
            data = jnp.concatenate([x_ref[f, base : base + span, :] * keep for f in range(fields)], axis=0)
            sums = jnp.dot(data, table, preferred_element_type=F32)
            re = [None] * fields
            im = [None] * fields
            for u in range(middle):
                c, s = cosv[16 + u : 17 + u], sinv[16 + u : 17 + u]
                for f in range(fields):
                    up = f * span + 8 * (middle + u)
                    down = f * span + 8 * (middle - 1 - u)
                    ur, ui = sums[up : up + 8, :count], sums[up : up + 8, count:]
                    dr, di = sums[down : down + 8, :count], sums[down : down + 8, count:]
                    r = c * (ur + dr) + s * (ui - di)
                    q = c * (ui + di) - s * (ur - dr)
                    re[f] = r if u == 0 else re[f] + r
                    im[f] = q if u == 0 else im[f] + q
            factor = jnp.where(2.0 * order < period_v, weight_ref[slot] * inverse, 0.0)
            hc, hs = cosv[24:32] * factor, sinv[24:32] * factor
            for f in range(fields):
                turned = (hc * re[f] + hs * im[f], hc * im[f] - hs * re[f])
                for ri, acc in enumerate(turned):
                    acc = acc + pltpu.roll(acc, 2, 0)
                    acc = acc + pltpu.roll(acc, 4, 0)
                    other = pltpu.roll(acc, 1, 0)
                    planes[2 * f + ri, pl.ds(slot, 1), :] = (acc + other)[0:1]
                    planes[2 * fields + 2 * f + ri, pl.ds(slot, 1), :] = (acc - other)[0:1]

        @pl.when(step == grid - 1)
        def _():
            for p in range(2):
                for v in range(nv):
                    for ri in range(2):
                        running = None
                        for l in range(nl):
                            at = ((p * nv + v) * nl + l) * 2 + ri
                            value = planes[at].astype(BF).astype(F32)
                            own_ref[at] = value if running is None else value + running
                            term = coupling_ref[v, l] * value
                            running = term if running is None else running + term
                        sum_ref[(p * nv + v) * 2 + ri] = running.astype(BF)

    smem = pl.BlockSpec(memory_space=pltpu.SMEM)
    return pl.pallas_call(
        kernel,
        name="analyse",
        grid=(grid,),
        in_specs=[
            smem,
            smem,
            smem,
            smem,
            pl.BlockSpec((fields, GROUP * rows, 128), lambda i: (0, i, 0)),
            pl.BlockSpec((1, count), lambda i: (0, 0)),
        ],
        out_specs=[
            pl.BlockSpec((16, slots, count), lambda i: (0, 0, 0)),
            pl.BlockSpec((16 // nl, slots, count), lambda i: (0, 0, 0)),
            pl.BlockSpec((1, count), lambda i: (0, 0)),
        ],
        out_shape=[
            jax.ShapeDtypeStruct((16, slots, count), F32),
            jax.ShapeDtypeStruct((16 // nl, slots, count), BF),
            jax.ShapeDtypeStruct((1, count), F32),
        ],
        scratch_shapes=[pltpu.VMEM((16, slots, count), F32)],
        compiler_params=pltpu.CompilerParams(dimension_semantics=("arbitrary",)),
    )(points, lat_ids, weights, coupling, points_rows, orders)


def deal(row, bands):
    count = row.shape[1]
    line, lane = iota((count, count), 0), iota((count, count), 1)
    column = jnp.sum(jnp.where(line == lane, row, 0.0), axis=1, keepdims=True)
    rank = jnp.sum(jnp.where(row < column, 1.0, 0.0), axis=1, keepdims=True).astype(jnp.int32)
    upper = rank >= count // 2
    pair = jnp.where(upper, count - 1 - rank, rank)
    place = pair % bands * 8 + pair // bands * 2 + jnp.where(upper, 1, 0)
    return jnp.sum(jnp.where(place == lane, column, 0.0), axis=0, keepdims=True)


def mix(own, earlier, bands, nv, nl):
    _, slots, count = own.shape

    def kernel(own_ref, earlier_ref, out_ref):
        for tile in range(count // 128):
            lanes = slice(128 * tile, 128 * tile + 128)
            value = []
            for k in range(16):
                source = k // (2 * nl) * 2 + k % 2
                value.append(own_ref[k, :, lanes] + earlier_ref[source, :, lanes].astype(F32))
            for d, w in enumerate(block_transpose(value)):
                out_ref[16 * tile + d] = w.astype(BF)

    return pl.pallas_call(kernel, name="mix", out_shape=jax.ShapeDtypeStruct((bands, slots, 128), BF))(own, earlier)


def make_rows(block, term_ref, cos_ref, second_ref, state, rows_ref, base):
    now, before, log_now = state
    half = cos_ref.shape[1]
    info = term_ref[block]
    restart = jnp.broadcast_to(info[:, 97:98], (8, half)) > 0.5
    current = jnp.where(restart, 1.0, now[...])
    previous = jnp.where(restart, 0.0, before[...])
    running = jnp.where(restart, second_ref[...], log_now[...])
    cosine = cos_ref[...]
    scale = None
    held = None
    for j in range(STEPS):
        if j % CHECK == 0:
            large = jnp.maximum(jnp.abs(current), jnp.abs(previous)) > 1.0
            shrink = jnp.where(large, 2.0**-60, 1.0)
            running = running + jnp.where(large, RESCALE_LOG, 0.0)
            current = current * shrink
            previous = previous * shrink
            scale = jnp.exp(running)
        value = current * scale
        if j % 2 == 0:
            held = value
        else:
            at = base + 8 * (j - 1)
            rows_ref[at : at + 16, :] = jnp.concatenate([held, value], axis=0).astype(BF)
        a = info[:, j : j + 1]
        b = info[:, STEPS + j : STEPS + j + 1]
        current, previous = (a * cosine) * current - b * previous, current
    now[...] = current
    before[...] = previous
    log_now[...] = running


def early_rows(band, orders, lats):
    total = lats.shape[1]
    half = total // 2
    count = orders.shape[1]
    height = 8 * STEPS
    blocks = 4 * (-(-(NT + 1) // (2 * STEPS))) + 2

    def kernel(band_ref, order_ref, lat_ref, rows_ref, term_ref, cos_ref, second_ref, now, before, log_now, pairs_ref):
        step = pl.program_id(0)

        @pl.when(step == 0)
        def _():
            line, lane = iota((8, count), 0), iota((8, count), 1)
            target = 8 * band_ref[0] + 2 * (line % 4)
            first = jnp.sum(jnp.where(lane == target, order_ref[...], 0.0), axis=1, keepdims=True)
            second = jnp.sum(jnp.where(lane == target + 1, order_ref[...], 0.0), axis=1, keepdims=True)
            index = (iota((1, NT + 1), 1) + 1).astype(F32)
            terms = jnp.log(1.0 + 0.5 / index)
            turned_cos, turned_sin = turn_cos_sin((lat_ref[...] + 0.5) * (1.0 / (4.0 * NH)))
            log_sine = jnp.log(turned_sin)
            top = iota((8, half), 0) < 4
            cos_ref[...] = jnp.where(top, turned_cos[:, :half], turned_cos[:, half:])
            side = jnp.where(top, log_sine[:, :half], log_sine[:, half:])
            for order, target_ref in ((first, log_now), (second, second_ref)):
                norm = jnp.sum(jnp.where(index <= order, terms, 0.0), axis=1, keepdims=True)
                target_ref[...] = (0.5 * math.log(0.5) + 0.5 * norm) + order * side
            now[...] = jnp.ones((8, half), F32)
            before[...] = jnp.zeros((8, half), F32)
            first = jnp.broadcast_to(first, (8, 128))
            second = jnp.broadcast_to(second, (8, 128))
            ends = jnp.floor((NT + STEPS - first) * (1.0 / STEPS))
            stops = ends + jnp.floor((NT + STEPS - second) * (1.0 / STEPS))
            pairs_ref[0] = jnp.max(jnp.floor((stops + 1.0) * 0.5).astype(jnp.int32))
            lane = iota((8, 128), 1)
            kind = lane // STEPS
            tick = (lane % STEPS).astype(F32)
            chain = 2.0 * (iota((8, 128), 0) % 4).astype(F32)

            def fill(block, carry):
                at = jnp.full((8, 128), block, jnp.int32).astype(F32)
                late = at >= ends
                order = jnp.where(late, second, first)
                row = order + STEPS * jnp.where(late, at - ends, at) + tick
                degree = row + 1.0
                offset = degree - order
                ahead = jnp.sqrt((4.0 * degree * degree - 1.0) / (offset * (degree + order)))
                below = jnp.maximum(4.0 * row * row - 1.0, 1.0)
                behind = jnp.sqrt((offset - 1.0) * (row + order) / below)
                ahead = jnp.where(degree <= NT, ahead, 0.0)
                damp = 1.0 / (1.0 + 4.0 * row * (row + 1.0) / (NT * (NT + 1.0)))
                last = jnp.where(lane == 96, chain + jnp.where(late, 1.0, 0.0), jnp.where(at == ends, 1.0, 0.0))
                rest = jnp.where(kind == 2, damp, last)
                term_ref[block] = jnp.where(kind == 0, ahead, jnp.where(kind == 1, ahead * behind, rest))
                return carry

            lax.fori_loop(0, blocks, fill, 0)

        @pl.when(step < (pairs_ref[0] + WIDE - 1) // WIDE * WIDE)
        def _():
            state = (now, before, log_now)
            for k in range(2):
                make_rows(2 * step + k, term_ref, cos_ref, second_ref, state, rows_ref, k * height)

    whole = lambda *shape: pl.BlockSpec(shape, lambda i: (0,) * len(shape))
    smem = pl.BlockSpec(memory_space=pltpu.SMEM)
    wide = jax.ShapeDtypeStruct((8, half), F32)
    return pl.pallas_call(
        kernel,
        name="early_rows",
        grid=(EARLY,),
        in_specs=[smem, whole(1, count), whole(1, total)],
        out_specs=[pl.BlockSpec((2 * height, half), lambda i: (i, 0)), whole(blocks, 8, 128)] + [whole(8, half)] * 5 + [smem],
        out_shape=[
            jax.ShapeDtypeStruct((EARLY * 2 * height, half), BF),
            jax.ShapeDtypeStruct((blocks, 8, 128), F32),
            wide,
            wide,
            wide,
            wide,
            wide,
            jax.ShapeDtypeStruct((1,), jnp.int32),
        ],
        compiler_params=pltpu.CompilerParams(dimension_semantics=("arbitrary",)),
    )(band, orders, lats)


def legendre(own, early):
    bands, slots, _ = own.shape
    total = bands * slots
    half = total // 2
    height = 8 * STEPS
    blocks = early[1].shape[0]

    def kernel(own_ref, early_ref, term_ref, cos_ref, second_ref, now_ref, before_ref, log_ref, pairs_ref, out_ref, mixed, weights, even_rows, odd_rows, acc, now, before, log_now):
        step = pl.program_id(0)
        pairs = pairs_ref[0]
        line, lane = iota((8, 128), 0), iota((8, 128), 1)
        low = line < 4

        @pl.when(step == 0)
        def _():
            for b in range(bands):
                mixed[b * slots : (b + 1) * slots] = own_ref[b].astype(F32)
            weights[...] = jnp.concatenate([mixed[:half], mixed[half:]], axis=1).astype(BF)
            acc[...] = jnp.zeros((256, half), F32)

        def use(block, rows, number):
            found = jnp.dot(rows, weights[...], preferred_element_type=F32)
            tops, lows = [], []
            for k in range(number):
                info = term_ref[block + k]
                which = jnp.broadcast_to(info[:, 96:97], (8, 128)).astype(jnp.int32)
                hit = lane % 8 == which
                masks = []
                for parity in range(2):
                    match = hit & (lane // 64 == parity)
                    masks.append((match & low, match & ~low))
                for j in range(STEPS):
                    at = k * height + 8 * j
                    part = found[at : at + 8]
                    part = jnp.where(low, part[:, :128], part[:, 128:])
                    part = (part + pltpu.roll(part, 4, 0)) * info[:, 2 * STEPS + j : 2 * STEPS + j + 1]
                    tops.append(jnp.where(masks[j % 2][0], part, 0.0))
                    lows.append(jnp.where(masks[j % 2][1], part, 0.0))
            kept = jnp.concatenate([jnp.concatenate(tops, axis=0), jnp.concatenate(lows, axis=0)], axis=1).astype(BF)
            acc[...] += lax.dot_general(kept, rows, (((0,), (0,)), ((), ())), preferred_element_type=F32)

        @pl.when(step * WIDE < pairs)
        def _():
            for k in range(0, 2 * WIDE, 2):
                use(2 * WIDE * step + k, early_ref[k * height : (k + 2) * height], 2)

        @pl.when(step == EARLY // WIDE - 1)
        def _():
            now[...] = now_ref[...]
            before[...] = before_ref[...]
            log_now[...] = log_ref[...]
            state = (now, before, log_now)

            def make(block, rows_ref):
                make_rows(block, term_ref, cos_ref, second_ref, state, rows_ref, 0)

            @pl.when(pairs > EARLY)
            def _():
                make(2 * EARLY, even_rows)

            def body(i, carry):
                make(2 * i + 1, odd_rows)
                use(2 * i, even_rows[...], 1)
                make(2 * i + 2, even_rows)
                use(2 * i + 1, odd_rows[...], 1)
                return carry

            lax.fori_loop(EARLY, pairs, body, 0)
            for h in range(2):
                for c in range(half // 128):
                    at = h * half + 128 * c
                    mixed[at : at + 128] = jnp.transpose(acc[128 * h : 128 * h + 128, 128 * c : 128 * c + 128])
            for b in range(bands):
                out_ref[b] = mixed[b * slots : (b + 1) * slots].astype(BF)

    whole = lambda *shape: pl.BlockSpec(shape, lambda i: (0,) * len(shape))
    return pl.pallas_call(
        kernel,
        name="legendre",
        grid=(EARLY // WIDE,),
        in_specs=[whole(bands, slots, 128), pl.BlockSpec((2 * WIDE * height, half), lambda i: (i, 0)), whole(blocks, 8, 128)]
        + [whole(8, half)] * 5
        + [pl.BlockSpec(memory_space=pltpu.SMEM)],
        out_specs=whole(bands, slots, 128),
        out_shape=jax.ShapeDtypeStruct((bands, slots, 128), BF),
        scratch_shapes=[
            pltpu.VMEM((total, 128), F32),
            pltpu.VMEM((half, 256), BF),
            pltpu.VMEM((height, half), BF),
            pltpu.VMEM((height, half), BF),
            pltpu.VMEM((256, half), F32),
            pltpu.VMEM((8, half), F32),
            pltpu.VMEM((8, half), F32),
            pltpu.VMEM((8, half), F32),
        ],
        compiler_params=pltpu.CompilerParams(dimension_semantics=("arbitrary",)),
    )(own, *early)


def synthesise(back, points, lat_ids, orders, nv, nl, width):
    bands, slots, _ = back.shape
    fields = nv * nl
    rows = 2 * (width // 128)
    span = window_rows(width)
    tiles = span // 8
    middle = tiles // 2
    count = orders.shape[1]
    grid = slots // GROUP

    def kernel(points_ref, lat_ref, back_ref, order_ref, out_ref, planes):
        step = pl.program_id(0)

        @pl.when(step == 0)
        def _():
            for tile in range(count // 128):
                value = [back_ref[16 * tile + d].astype(F32) for d in range(16)]
                for k, w in enumerate(block_transpose(value)):
                    planes[k, :, 128 * tile : 128 * tile + 128] = w

        order = order_ref[...]
        position = 128 * (iota((span, 128), 0) // 2) + iota((span, 128), 1)
        shared, blocks = angle_rows(order, tiles)
        sign = jnp.where(iota((8, count), 0) % 2 == 0, 1.0, -1.0)
        double = jnp.where(order == 0.0, 1.0, 2.0)
        for i in range(GROUP):
            base, off = window(i, rows)
            slot = step * GROUP + i
            period = points_ref[lat_ref[slot]]
            cosv, sinv, period_v, _ = slot_angles(shared, blocks, order, off, period)
            table = inner_table(cosv, sinv)
            factor = jnp.where(2.0 * order < period_v, double, 0.0)
            hc, hs = cosv[24:32] * factor, sinv[24:32] * factor
            parts = []
            for f in range(fields):
                both = []
                for ri in range(2):
                    even = planes[2 * f + ri, pl.ds(slot, 1), :]
                    odd = planes[2 * fields + 2 * f + ri, pl.ds(slot, 1), :]
                    both.append(even + sign * odd)
                re, im = both
                wr, wi = hc * re - hs * im, hs * re + hc * im
                zr, zi = [None] * tiles, [None] * tiles
                for u in range(middle):
                    c, s = cosv[16 + u : 17 + u], sinv[16 + u : 17 + u]
                    cr, si, ci, sr = c * wr, s * wi, c * wi, s * wr
                    zr[middle + u], zr[middle - 1 - u] = cr - si, cr + si
                    zi[middle + u], zi[middle - 1 - u] = ci + sr, ci - sr
                parts.append(jnp.concatenate([jnp.concatenate(zr, 0).astype(BF), jnp.concatenate(zi, 0).astype(BF)], axis=1))
            waves = jnp.concatenate(parts, axis=0)
            values = lax.dot_general(waves, table, (((1,), (1,)), ((), ())), preferred_element_type=F32)
            inside = position < period + 64 * off
            starts = position[:16] >= 64 * off
            for f in range(fields):
                part = jnp.where(inside, values[f * span : (f + 1) * span], 0.0)
                if off:
                    first = jnp.where(starts, part[:16], out_ref[f, base : base + 16, :].astype(F32))
                    out_ref[f, base : base + 16, :] = first.astype(BF)
                    out_ref[f, base + 16 : base + span, :] = part[16:].astype(BF)
                else:
                    out_ref[f, base : base + span, :] = part.astype(BF)

    smem = pl.BlockSpec(memory_space=pltpu.SMEM)
    return pl.pallas_call(
        kernel,
        name="synthesise",
        grid=(grid,),
        in_specs=[
            smem,
            smem,
            pl.BlockSpec((bands, slots, 128), lambda i: (0, 0, 0)),
            pl.BlockSpec((1, count), lambda i: (0, 0)),
        ],
        out_specs=pl.BlockSpec((fields, GROUP * rows, 128), lambda i: (0, i, 0)),
        out_shape=jax.ShapeDtypeStruct((fields, slots * rows, 128), BF),
        scratch_shapes=[pltpu.VMEM((16, slots, count), F32)],
        compiler_params=pltpu.CompilerParams(dimension_semantics=("arbitrary",)),
    )(points, lat_ids, back, orders)


def solution(mesh):
    bands, parts = mesh.shape["band"], mesh.shape["fld"]

    def on_device(grid_field, coupling, points, lat_ids, wn_ids):
        nv, nl, slots, _, width = grid_field.shape
        mine = wn_ids.shape[0]
        packed = jnp.concatenate([wn_ids, lat_ids])
        spread = jnp.broadcast_to(packed[None], (bands, mine + slots))
        known = lax.all_to_all(spread, "band", split_axis=0, concat_axis=0, tiled=True)
        orders = known[:, :mine].reshape(1, bands * mine).astype(F32)
        lats = known[:, mine:].reshape(1, bands * slots).astype(F32)
        weights = math.pi / (2.0 * NH) * jnp.sin(math.pi * (lat_ids.astype(F32) + 0.5) / (2.0 * NH))
        own, sums, orders = analyse(as_rows(grid_field), points, lat_ids, weights, orders, coupling, nv, nl, width)
        earlier = jnp.zeros_like(sums)
        for shift in range(1, parts):
            moved = lax.ppermute(sums, "fld", [(k, k + shift) for k in range(parts - shift)])
            earlier = moved if shift == 1 else earlier + moved
        own, orders = lax.optimization_barrier((mix(own, earlier, bands, nv, nl), orders))
        own = lax.all_to_all(own, "band", split_axis=0, concat_axis=0, tiled=True)
        band = lax.axis_index("band").astype(jnp.int32).reshape(1)
        back = legendre(own, early_rows(band, orders, lats))
        back = lax.all_to_all(back, "band", split_axis=0, concat_axis=0, tiled=True)
        rows = synthesise(back, points, lat_ids, orders, nv, nl, width)
        return from_rows(rows, nv, nl, slots, width)

    in_specs = (P(None, "fld", "band", None, None), P(None, "fld"), P(), P("band"), P("band"))
    return jax.shard_map(on_device, mesh=mesh, in_specs=in_specs, out_specs=in_specs[0], check_vma=False)
```

```python
import math

import jax
import jax.numpy as jnp
from jax import lax
from jax.experimental import pallas as pl
from jax.experimental.pallas import tpu as pltpu
from jax.experimental.layout import Layout, with_layout_constraint
from jax.sharding import PartitionSpec as P

NT = 1279
NH = 1280
BF = jnp.bfloat16
F32 = jnp.float32
GROUP = 8
STEPS = 32
CHECK = 8
RESCALE_LOG = 60.0 * math.log(2.0)


def iota(shape, dim):
    return lax.broadcasted_iota(jnp.int32, shape, dim)


def turn_cos_sin(turns):
    y = turns * turns
    s = -0.59828975 + y * 0.07765416
    s = 2.55007732 + y * s
    s = -5.16771007 + y * s
    s = turns * (3.14159264 + y * s)
    c = -1.33187126 + y * 0.21967748
    c = 4.05841064 + y * c
    c = -4.9347928 + y * c
    c = 0.99999995 + y * c
    twice = s + s
    return 1.0 - twice * s, twice * c


def block_transpose(planes):
    lane = iota((1, 128), 1) // 8
    planes = list(planes)
    for bit in (8, 4, 2, 1):
        low = (lane & bit) == 0
        for at in range(16):
            if at & bit:
                continue
            a, b = planes[at], planes[at | bit]
            planes[at] = jnp.where(low, a, pltpu.roll(b, 8 * bit, 1))
            planes[at | bit] = jnp.where(low, pltpu.roll(a, 128 - 8 * bit, 1), b)
    return planes


def window(i, rows):
    start = i * rows
    base = start // 16 * 16
    return base, start - base


def window_rows(width):
    return -(-(2 * (width // 128) + 14) // 16) * 16


def as_rows(field):
    nv, nl, slots, _, width = field.shape
    blocks = width // 128
    split = field.reshape(nv, nl, slots, 2, blocks, 128)
    split = with_layout_constraint(split, Layout(major_to_minor=(0, 1, 2, 4, 3, 5)))
    return split.transpose(0, 1, 2, 4, 3, 5).reshape(nv * nl, slots * 2 * blocks, 128)


def from_rows(rows, nv, nl, slots, width):
    split = rows.reshape(nv, nl, slots, width // 128, 2, 128).transpose(0, 1, 2, 4, 3, 5)
    split = with_layout_constraint(split, Layout(major_to_minor=(0, 1, 2, 4, 3, 5)))
    return split.reshape(nv, nl, slots, 2, width)


def angle_rows(order, tiles):
    count = order.shape[1]
    row = iota((8, count), 0)
    steps = jnp.where(row < tiles // 2, 256 * (2 * row + 1), 64)
    shared = jnp.concatenate([row, 8 * row, steps], axis=0).astype(F32) * order
    blocks = (128 * (2 * tiles - 2 + row // 2)).astype(F32)
    return shared, blocks


def slot_angles(shared, blocks, order, off, period):
    product = jnp.concatenate([shared, (blocks - 64.0 * off) * order], axis=0)
    period_v = jnp.full(order.shape, period, jnp.int32).astype(F32)
    inverse = 1.0 / period_v
    turns = (product - jnp.floor(product * inverse + 0.5) * period_v) * inverse
    cosv, sinv = turn_cos_sin(turns)
    return cosv, sinv, period_v, inverse


def inner_table(cosv, sinv):
    fc, fs = cosv[0:8], sinv[0:8]
    ec, es = cosv[8:16], sinv[8:16]
    wc, ws = cosv[23:24], sinv[23:24]
    ec = jnp.concatenate([ec, ec * wc - es * ws], axis=0)
    es = jnp.concatenate([es, es * wc + cosv[8:16] * ws], axis=0)
    parts_c, parts_s = [], []
    for a in range(16):
        c, s = ec[a : a + 1], es[a : a + 1]
        parts_c.append(c * fc - s * fs)
        parts_s.append((-s) * fc - c * fs)
    halves = [jnp.concatenate(p, axis=0).astype(BF) for p in (parts_c, parts_s)]
    return jnp.concatenate(halves, axis=1)


def analyse(points_rows, points, lat_ids, weights, orders, coupling, nv, nl, width):
    fields = nv * nl
    slots = lat_ids.shape[0]
    rows = 2 * (width // 128)
    span = window_rows(width)
    tiles = span // 8
    middle = tiles // 2
    count = orders.shape[1]
    bands = count // 8
    grid = slots // GROUP

    def kernel(points_ref, lat_ref, weight_ref, coupling_ref, x_ref, given_ref, own_ref, sum_ref, order_ref, planes):
        step = pl.program_id(0)

        @pl.when(step == 0)
        def _():
            order_ref[...] = deal(given_ref[...], bands)

        order = order_ref[...]
        position = (128 * (iota((span, 128), 0) // 2) + iota((span, 128), 1)).astype(F32)
        shared, blocks = angle_rows(order, tiles)
        for i in range(GROUP):
            base, off = window(i, rows)
            slot = step * GROUP + i
            period = points_ref[lat_ref[slot]]
            cosv, sinv, period_v, inverse = slot_angles(shared, blocks, order, off, period)
            table = inner_table(cosv, sinv)
            limit = jnp.full((1, 128), period, jnp.int32).astype(F32) + 64.0 * off
            keep = jnp.minimum(jnp.maximum(limit - position, 0.0), 1.0)
            if off:
                head = jnp.where(position[:16] >= 64.0 * off, keep[:16], 0.0)
                keep = jnp.concatenate([head, keep[16:]], axis=0)
            keep = keep.astype(BF)
            data = jnp.concatenate([x_ref[f, base : base + span, :] * keep for f in range(fields)], axis=0)
            sums = jnp.dot(data, table, preferred_element_type=F32)
            re = [None] * fields
            im = [None] * fields
            for u in range(middle):
                c, s = cosv[16 + u : 17 + u], sinv[16 + u : 17 + u]
                for f in range(fields):
                    up = f * span + 8 * (middle + u)
                    down = f * span + 8 * (middle - 1 - u)
                    ur, ui = sums[up : up + 8, :count], sums[up : up + 8, count:]
                    dr, di = sums[down : down + 8, :count], sums[down : down + 8, count:]
                    r = c * (ur + dr) + s * (ui - di)
                    q = c * (ui + di) - s * (ur - dr)
                    re[f] = r if u == 0 else re[f] + r
                    im[f] = q if u == 0 else im[f] + q
            factor = jnp.where(2.0 * order < period_v, weight_ref[slot] * inverse, 0.0)
            hc, hs = cosv[24:32] * factor, sinv[24:32] * factor
            for f in range(fields):
                turned = (hc * re[f] + hs * im[f], hc * im[f] - hs * re[f])
                for ri, acc in enumerate(turned):
                    acc = acc + pltpu.roll(acc, 2, 0)
                    acc = acc + pltpu.roll(acc, 4, 0)
                    other = pltpu.roll(acc, 1, 0)
                    planes[2 * f + ri, pl.ds(slot, 1), :] = (acc + other)[0:1]
                    planes[2 * fields + 2 * f + ri, pl.ds(slot, 1), :] = (acc - other)[0:1]

        @pl.when(step == grid - 1)
        def _():
            for p in range(2):
                for v in range(nv):
                    for ri in range(2):
                        running = None
                        for l in range(nl):
                            at = ((p * nv + v) * nl + l) * 2 + ri
                            value = planes[at].astype(BF).astype(F32)
                            own_ref[at] = value if running is None else value + running
                            term = coupling_ref[v, l] * value
                            running = term if running is None else running + term
                        sum_ref[(p * nv + v) * 2 + ri] = running.astype(BF)

    smem = pl.BlockSpec(memory_space=pltpu.SMEM)
    return pl.pallas_call(
        kernel,
        name="analyse",
        grid=(grid,),
        in_specs=[
            smem,
            smem,
            smem,
            smem,
            pl.BlockSpec((fields, GROUP * rows, 128), lambda i: (0, i, 0)),
            pl.BlockSpec((1, count), lambda i: (0, 0)),
        ],
        out_specs=[
            pl.BlockSpec((16, slots, count), lambda i: (0, 0, 0)),
            pl.BlockSpec((16 // nl, slots, count), lambda i: (0, 0, 0)),
            pl.BlockSpec((1, count), lambda i: (0, 0)),
        ],
        out_shape=[
            jax.ShapeDtypeStruct((16, slots, count), F32),
            jax.ShapeDtypeStruct((16 // nl, slots, count), BF),
            jax.ShapeDtypeStruct((1, count), F32),
        ],
        scratch_shapes=[pltpu.VMEM((16, slots, count), F32)],
        compiler_params=pltpu.CompilerParams(dimension_semantics=("arbitrary",)),
    )(points, lat_ids, weights, coupling, points_rows, orders)


def deal(row, bands):
    count = row.shape[1]
    line, lane = iota((count, count), 0), iota((count, count), 1)
    column = jnp.sum(jnp.where(line == lane, row, 0.0), axis=1, keepdims=True)
    rank = jnp.sum(jnp.where(row < column, 1.0, 0.0), axis=1, keepdims=True).astype(jnp.int32)
    upper = rank >= count // 2
    pair = jnp.where(upper, count - 1 - rank, rank)
    place = pair % bands * 8 + pair // bands * 2 + jnp.where(upper, 1, 0)
    return jnp.sum(jnp.where(place == lane, column, 0.0), axis=0, keepdims=True)


def mix(own, earlier, bands, nv, nl):
    _, slots, count = own.shape

    def kernel(own_ref, earlier_ref, out_ref):
        for tile in range(count // 128):
            lanes = slice(128 * tile, 128 * tile + 128)
            value = []
            for k in range(16):
                source = k // (2 * nl) * 2 + k % 2
                value.append(own_ref[k, :, lanes] + earlier_ref[source, :, lanes].astype(F32))
            for d, w in enumerate(block_transpose(value)):
                out_ref[16 * tile + d] = w.astype(BF)

    return pl.pallas_call(kernel, name="mix", out_shape=jax.ShapeDtypeStruct((bands, slots, 128), BF))(own, earlier)


def make_rows(block, term_ref, cos_ref, second_ref, state, rows_ref, base):
    now, before, log_now = state
    half = cos_ref.shape[1]
    info = term_ref[block]
    restart = jnp.broadcast_to(info[:, 97:98], (8, half)) > 0.5
    current = jnp.where(restart, 1.0, now[...])
    previous = jnp.where(restart, 0.0, before[...])
    running = jnp.where(restart, second_ref[...], log_now[...])
    cosine = cos_ref[...]
    scale = None
    held = None
    for j in range(STEPS):
        if j % CHECK == 0:
            large = jnp.maximum(jnp.abs(current), jnp.abs(previous)) > 1.0
            shrink = jnp.where(large, 2.0**-60, 1.0)
            running = running + jnp.where(large, RESCALE_LOG, 0.0)
            current = current * shrink
            previous = previous * shrink
            scale = jnp.exp(running)
        value = current * scale
        if j % 2 == 0:
            held = value
        else:
            at = base + 8 * (j - 1)
            rows_ref[at : at + 16, :] = jnp.concatenate([held, value], axis=0).astype(BF)
        a = info[:, j : j + 1]
        b = info[:, STEPS + j : STEPS + j + 1]
        current, previous = (a * cosine) * current - b * previous, current
    now[...] = current
    before[...] = previous
    log_now[...] = running


def plan(band, orders, lats):
    total = lats.shape[1]
    half = total // 2
    count = orders.shape[1]
    blocks = 4 * (-(-2 * (NT + 1) // (4 * STEPS))) + 2

    def kernel(band_ref, order_ref, lat_ref, term_ref, cos_ref, first_ref, second_ref, quads_ref):
        line, lane = iota((8, count), 0), iota((8, count), 1)
        target = 8 * band_ref[0] + 2 * (line % 4)
        first = jnp.sum(jnp.where(lane == target, order_ref[...], 0.0), axis=1, keepdims=True)
        second = jnp.sum(jnp.where(lane == target + 1, order_ref[...], 0.0), axis=1, keepdims=True)
        index = (iota((1, NT + 1), 1) + 1).astype(F32)
        terms = jnp.log(1.0 + 0.5 / index)
        turned_cos, turned_sin = turn_cos_sin((lat_ref[...] + 0.5) * (1.0 / (4.0 * NH)))
        log_sine = jnp.log(turned_sin)
        top = iota((8, half), 0) < 4
        cos_ref[...] = jnp.where(top, turned_cos[:, :half], turned_cos[:, half:])
        side = jnp.where(top, log_sine[:, :half], log_sine[:, half:])
        for order, target_ref in ((first, first_ref), (second, second_ref)):
            norm = jnp.sum(jnp.where(index <= order, terms, 0.0), axis=1, keepdims=True)
            target_ref[...] = (0.5 * math.log(0.5) + 0.5 * norm) + order * side
        first = jnp.broadcast_to(first, (8, 128))
        second = jnp.broadcast_to(second, (8, 128))
        ends = jnp.floor((NT + STEPS - first) * (1.0 / STEPS))
        stops = ends + jnp.floor((NT + STEPS - second) * (1.0 / STEPS))
        quads_ref[0] = jnp.max(jnp.floor((stops + 3.0) * 0.25).astype(jnp.int32))
        lane = iota((8, 128), 1)
        kind = lane // STEPS
        tick = (lane % STEPS).astype(F32)
        chain = 2.0 * (iota((8, 128), 0) % 4).astype(F32)

        def fill(block, carry):
            at = jnp.full((8, 128), block, jnp.int32).astype(F32)
            late = at >= ends
            order = jnp.where(late, second, first)
            row = order + STEPS * jnp.where(late, at - ends, at) + tick
            degree = row + 1.0
            offset = degree - order
            ahead = jnp.sqrt((4.0 * degree * degree - 1.0) / (offset * (degree + order)))
            below = jnp.maximum(4.0 * row * row - 1.0, 1.0)
            behind = jnp.sqrt((offset - 1.0) * (row + order) / below)
            ahead = jnp.where(degree <= NT, ahead, 0.0)
            damp = 1.0 / (1.0 + 4.0 * row * (row + 1.0) / (NT * (NT + 1.0)))
            last = jnp.where(lane == 96, chain + jnp.where(late, 1.0, 0.0), jnp.where(at == ends, 1.0, 0.0))
            rest = jnp.where(kind == 2, damp, last)
            term_ref[block] = jnp.where(kind == 0, ahead, jnp.where(kind == 1, ahead * behind, rest))
            return carry

        lax.fori_loop(0, blocks, fill, 0, unroll=2)

    smem = pl.BlockSpec(memory_space=pltpu.SMEM)
    vmem = pl.BlockSpec(memory_space=pltpu.VMEM)
    wide = jax.ShapeDtypeStruct((8, half), F32)
    return pl.pallas_call(
        kernel,
        name="plan",
        in_specs=[smem, vmem, vmem],
        out_specs=[vmem] * 4 + [smem],
        out_shape=[jax.ShapeDtypeStruct((blocks, 8, 128), F32), wide, wide, wide, jax.ShapeDtypeStruct((1,), jnp.int32)],
    )(band, orders, lats)


def legendre(own, tables):
    bands, slots, _ = own.shape
    total = bands * slots
    half = total // 2
    height = 8 * STEPS

    def kernel(own_ref, term_ref, cos_ref, first_ref, second_ref, quads_ref, out_ref, mixed, weights, rows0, rows1, rows2, rows3, kept0, kept1, acc, now, before, log_now):
        rows = (rows0, rows1, rows2, rows3)
        kept = (kept0, kept1)
        line, lane = iota((8, 128), 0), iota((8, 128), 1)
        low = line < 4
        for b in range(bands):
            mixed[b * slots : (b + 1) * slots] = own_ref[b].astype(F32)
        weights[...] = jnp.concatenate([mixed[:half], mixed[half:]], axis=1).astype(BF)
        acc[...] = jnp.zeros((256, half), F32)
        rows3[...] = jnp.zeros((height, half), BF)
        kept1[...] = jnp.zeros((height, 256), BF)
        now[...] = jnp.ones((8, half), F32)
        before[...] = jnp.zeros((8, half), F32)
        log_now[...] = first_ref[...]
        state = (now, before, log_now)

        def make(block, target):
            make_rows(block, term_ref, cos_ref, second_ref, state, target, 0)

        def analysed(block, source, target):
            found = jnp.dot(source[...], weights[...], preferred_element_type=F32)
            info = term_ref[block]
            hit = lane % 8 == jnp.broadcast_to(info[:, 96:97], (8, 128)).astype(jnp.int32)
            masks = []
            for parity in range(2):
                match = hit & (lane // 64 == parity)
                masks.append((match & low, match & ~low))
            tops, lows = [], []
            for j in range(STEPS):
                part = found[8 * j : 8 * j + 8]
                part = jnp.where(low, part[:, :128], part[:, 128:])
                part = (part + pltpu.roll(part, 4, 0)) * info[:, 2 * STEPS + j : 2 * STEPS + j + 1]
                tops.append(jnp.where(masks[j % 2][0], part, 0.0))
                lows.append(jnp.where(masks[j % 2][1], part, 0.0))
            target[...] = jnp.concatenate([jnp.concatenate(tops, axis=0), jnp.concatenate(lows, axis=0)], axis=1).astype(BF)

        def gathered(coefficients, source):
            acc[...] += lax.dot_general(
                coefficients[...], source[...], (((0,), (0,)), ((), ())), preferred_element_type=F32
            )

        make(0, rows0)

        def body(i, carry):
            for k in range(4):
                analysed(4 * i + k, rows[k], kept[k % 2])
                gathered(kept[(k + 1) % 2], rows[(k + 3) % 4])
                make(4 * i + k + 1, rows[(k + 1) % 4])
            return carry

        lax.fori_loop(0, quads_ref[0], body, 0)
        gathered(kept1, rows3)
        for h in range(2):
            for c in range(half // 128):
                at = h * half + 128 * c
                mixed[at : at + 128] = jnp.transpose(acc[128 * h : 128 * h + 128, 128 * c : 128 * c + 128])
        for b in range(bands):
            out_ref[b] = mixed[b * slots : (b + 1) * slots].astype(BF)

    vmem = pl.BlockSpec(memory_space=pltpu.VMEM)
    return pl.pallas_call(
        kernel,
        name="legendre",
        in_specs=[vmem] * 5 + [pl.BlockSpec(memory_space=pltpu.SMEM)],
        out_specs=vmem,
        out_shape=jax.ShapeDtypeStruct((bands, slots, 128), BF),
        scratch_shapes=[
            pltpu.VMEM((total, 128), F32),
            pltpu.VMEM((half, 256), BF),
            pltpu.VMEM((height, half), BF),
            pltpu.VMEM((height, half), BF),
            pltpu.VMEM((height, half), BF),
            pltpu.VMEM((height, half), BF),
            pltpu.VMEM((height, 256), BF),
            pltpu.VMEM((height, 256), BF),
            pltpu.VMEM((256, half), F32),
            pltpu.VMEM((8, half), F32),
            pltpu.VMEM((8, half), F32),
            pltpu.VMEM((8, half), F32),
        ],
    )(own, *tables)


def synthesise(back, points, lat_ids, orders, nv, nl, width):
    bands, slots, _ = back.shape
    fields = nv * nl
    rows = 2 * (width // 128)
    span = window_rows(width)
    tiles = span // 8
    middle = tiles // 2
    count = orders.shape[1]
    grid = slots // GROUP

    def kernel(points_ref, lat_ref, back_ref, order_ref, out_ref, planes):
        step = pl.program_id(0)

        @pl.when(step == 0)
        def _():
            for tile in range(count // 128):
                value = [back_ref[16 * tile + d].astype(F32) for d in range(16)]
                for k, w in enumerate(block_transpose(value)):
                    planes[k, :, 128 * tile : 128 * tile + 128] = w

        order = order_ref[...]
        position = 128 * (iota((span, 128), 0) // 2) + iota((span, 128), 1)
        shared, blocks = angle_rows(order, tiles)
        sign = jnp.where(iota((8, count), 0) % 2 == 0, 1.0, -1.0)
        double = jnp.where(order == 0.0, 1.0, 2.0)
        for i in range(GROUP):
            base, off = window(i, rows)
            slot = step * GROUP + i
            period = points_ref[lat_ref[slot]]
            cosv, sinv, period_v, _ = slot_angles(shared, blocks, order, off, period)
            table = inner_table(cosv, sinv)
            factor = jnp.where(2.0 * order < period_v, double, 0.0)
            hc, hs = cosv[24:32] * factor, sinv[24:32] * factor
            parts = []
            for f in range(fields):
                both = []
                for ri in range(2):
                    even = planes[2 * f + ri, pl.ds(slot, 1), :]
                    odd = planes[2 * fields + 2 * f + ri, pl.ds(slot, 1), :]
                    both.append(even + sign * odd)
                re, im = both
                wr, wi = hc * re - hs * im, hs * re + hc * im
                zr, zi = [None] * tiles, [None] * tiles
                for u in range(middle):
                    c, s = cosv[16 + u : 17 + u], sinv[16 + u : 17 + u]
                    cr, si, ci, sr = c * wr, s * wi, c * wi, s * wr
                    zr[middle + u], zr[middle - 1 - u] = cr - si, cr + si
                    zi[middle + u], zi[middle - 1 - u] = ci + sr, ci - sr
                parts.append(jnp.concatenate([jnp.concatenate(zr, 0).astype(BF), jnp.concatenate(zi, 0).astype(BF)], axis=1))
            waves = jnp.concatenate(parts, axis=0)
            values = lax.dot_general(waves, table, (((1,), (1,)), ((), ())), preferred_element_type=F32)
            inside = position < period + 64 * off
            starts = position[:16] >= 64 * off
            for f in range(fields):
                part = jnp.where(inside, values[f * span : (f + 1) * span], 0.0)
                if off:
                    first = jnp.where(starts, part[:16], out_ref[f, base : base + 16, :].astype(F32))
                    out_ref[f, base : base + 16, :] = first.astype(BF)
                    out_ref[f, base + 16 : base + span, :] = part[16:].astype(BF)
                else:
                    out_ref[f, base : base + span, :] = part.astype(BF)

    smem = pl.BlockSpec(memory_space=pltpu.SMEM)
    return pl.pallas_call(
        kernel,
        name="synthesise",
        grid=(grid,),
        in_specs=[
            smem,
            smem,
            pl.BlockSpec((bands, slots, 128), lambda i: (0, 0, 0)),
            pl.BlockSpec((1, count), lambda i: (0, 0)),
        ],
        out_specs=pl.BlockSpec((fields, GROUP * rows, 128), lambda i: (0, i, 0)),
        out_shape=jax.ShapeDtypeStruct((fields, slots * rows, 128), BF),
        scratch_shapes=[pltpu.VMEM((16, slots, count), F32)],
        compiler_params=pltpu.CompilerParams(dimension_semantics=("arbitrary",)),
    )(points, lat_ids, back, orders)


def solution(mesh):
    bands, parts = mesh.shape["band"], mesh.shape["fld"]

    def on_device(grid_field, coupling, points, lat_ids, wn_ids):
        nv, nl, slots, _, width = grid_field.shape
        mine = wn_ids.shape[0]
        packed = jnp.concatenate([wn_ids, lat_ids])
        spread = jnp.broadcast_to(packed[None], (bands, mine + slots))
        known = lax.all_to_all(spread, "band", split_axis=0, concat_axis=0, tiled=True)
        orders = known[:, :mine].reshape(1, bands * mine).astype(F32)
        lats = known[:, mine:].reshape(1, bands * slots).astype(F32)
        weights = math.pi / (2.0 * NH) * jnp.sin(math.pi * (lat_ids.astype(F32) + 0.5) / (2.0 * NH))
        own, sums, orders = analyse(as_rows(grid_field), points, lat_ids, weights, orders, coupling, nv, nl, width)
        earlier = jnp.zeros_like(sums)
        for shift in range(1, parts):
            moved = lax.ppermute(sums, "fld", [(k, k + shift) for k in range(parts - shift)])
            earlier = moved if shift == 1 else earlier + moved
        own, orders = lax.optimization_barrier((mix(own, earlier, bands, nv, nl), orders))
        own = lax.all_to_all(own, "band", split_axis=0, concat_axis=0, tiled=True)
        band = lax.axis_index("band").astype(jnp.int32).reshape(1)
        back = legendre(own, plan(band, orders, lats))
        back = lax.all_to_all(back, "band", split_axis=0, concat_axis=0, tiled=True)
        rows = synthesise(back, points, lat_ids, orders, nv, nl, width)
        return from_rows(rows, nv, nl, slots, width)

    in_specs = (P(None, "fld", "band", None, None), P(None, "fld"), P(), P("band"), P("band"))
    return jax.shard_map(on_device, mesh=mesh, in_specs=in_specs, out_specs=in_specs[0], check_vma=False)
```

```python
import math

import jax
import jax.numpy as jnp
from jax import lax
from jax.experimental import pallas as pl
from jax.experimental.pallas import tpu as pltpu
from jax.experimental.layout import Layout, with_layout_constraint
from jax.sharding import PartitionSpec as P

NT = 1279
NH = 1280
BF = jnp.bfloat16
F32 = jnp.float32
GROUP = 8
STEPS = 32
CHECK = 16
FOLD = 8
RESCALE_LOG = 60.0 * math.log(2.0)


def iota(shape, dim):
    return lax.broadcasted_iota(jnp.int32, shape, dim)


def turn_cos_sin(turns):
    y = turns * turns
    s = -0.59828975 + y * 0.07765416
    s = 2.55007732 + y * s
    s = -5.16771007 + y * s
    s = turns * (3.14159264 + y * s)
    c = -1.33187126 + y * 0.21967748
    c = 4.05841064 + y * c
    c = -4.9347928 + y * c
    c = 0.99999995 + y * c
    twice = s + s
    return 1.0 - twice * s, twice * c


def block_transpose(planes):
    lane = iota((1, 128), 1) // 8
    planes = list(planes)
    for bit in (8, 4, 2, 1):
        low = (lane & bit) == 0
        for at in range(16):
            if at & bit:
                continue
            a, b = planes[at], planes[at | bit]
            planes[at] = jnp.where(low, a, pltpu.roll(b, 8 * bit, 1))
            planes[at | bit] = jnp.where(low, pltpu.roll(a, 128 - 8 * bit, 1), b)
    return planes


def window(i, rows):
    start = i * rows
    base = start // 16 * 16
    return base, start - base


def window_rows(width):
    return -(-(2 * (width // 128) + 14) // 16) * 16


def as_rows(field):
    nv, nl, slots, _, width = field.shape
    blocks = width // 128
    split = field.reshape(nv, nl, slots, 2, blocks, 128)
    split = with_layout_constraint(split, Layout(major_to_minor=(0, 1, 2, 4, 3, 5)))
    return split.transpose(0, 1, 2, 4, 3, 5).reshape(nv * nl, slots * 2 * blocks, 128)


def from_rows(rows, nv, nl, slots, width):
    split = rows.reshape(nv, nl, slots, width // 128, 2, 128).transpose(0, 1, 2, 4, 3, 5)
    split = with_layout_constraint(split, Layout(major_to_minor=(0, 1, 2, 4, 3, 5)))
    return split.reshape(nv, nl, slots, 2, width)


def angle_rows(order, tiles):
    count = order.shape[1]
    row = iota((8, count), 0)
    steps = jnp.where(row < tiles // 2, 256 * (2 * row + 1), 64)
    shared = jnp.concatenate([row, 8 * row, steps], axis=0).astype(F32) * order
    blocks = (128 * (2 * tiles - 2 + row // 2)).astype(F32)
    return shared, blocks


def slot_angles(shared, blocks, order, off, period):
    product = jnp.concatenate([shared, (blocks - 64.0 * off) * order], axis=0)
    period_v = jnp.full(order.shape, period, jnp.int32).astype(F32)
    inverse = 1.0 / period_v
    turns = (product - jnp.floor(product * inverse + 0.5) * period_v) * inverse
    cosv, sinv = turn_cos_sin(turns)
    return cosv, sinv, period_v, inverse


def inner_table(cosv, sinv):
    fc, fs = cosv[0:8], sinv[0:8]
    ec, es = cosv[8:16], sinv[8:16]
    wc, ws = cosv[23:24], sinv[23:24]
    ec = jnp.concatenate([ec, ec * wc - es * ws], axis=0)
    es = jnp.concatenate([es, es * wc + cosv[8:16] * ws], axis=0)
    parts_c, parts_s = [], []
    for a in range(16):
        c, s = ec[a : a + 1], es[a : a + 1]
        parts_c.append(c * fc - s * fs)
        parts_s.append((-s) * fc - c * fs)
    halves = [jnp.concatenate(p, axis=0).astype(BF) for p in (parts_c, parts_s)]
    return jnp.concatenate(halves, axis=1)


def analyse(points_rows, points, lat_ids, weights, orders, coupling, nv, nl, width):
    fields = nv * nl
    slots = lat_ids.shape[0]
    rows = 2 * (width // 128)
    span = window_rows(width)
    tiles = span // 8
    middle = tiles // 2
    count = orders.shape[1]
    bands = count // 8
    grid = slots // GROUP

    def kernel(points_ref, lat_ref, weight_ref, coupling_ref, x_ref, given_ref, own_ref, sum_ref, order_ref, planes):
        step = pl.program_id(0)

        @pl.when(step == 0)
        def _():
            order_ref[...] = deal(given_ref[...], bands)

        order = order_ref[...]
        position = (128 * (iota((span, 128), 0) // 2) + iota((span, 128), 1)).astype(F32)
        shared, blocks = angle_rows(order, tiles)
        for i in range(GROUP):
            base, off = window(i, rows)
            slot = step * GROUP + i
            period = points_ref[lat_ref[slot]]
            cosv, sinv, period_v, inverse = slot_angles(shared, blocks, order, off, period)
            table = inner_table(cosv, sinv)
            limit = jnp.full((1, 128), period, jnp.int32).astype(F32) + 64.0 * off
            keep = jnp.minimum(jnp.maximum(limit - position, 0.0), 1.0)
            if off:
                head = jnp.where(position[:16] >= 64.0 * off, keep[:16], 0.0)
                keep = jnp.concatenate([head, keep[16:]], axis=0)
            keep = keep.astype(BF)
            data = jnp.concatenate([x_ref[f, base : base + span, :] * keep for f in range(fields)], axis=0)
            sums = jnp.dot(data, table, preferred_element_type=F32)
            re = [None] * fields
            im = [None] * fields
            for u in range(middle):
                c, s = cosv[16 + u : 17 + u], sinv[16 + u : 17 + u]
                for f in range(fields):
                    up = f * span + 8 * (middle + u)
                    down = f * span + 8 * (middle - 1 - u)
                    ur, ui = sums[up : up + 8, :count], sums[up : up + 8, count:]
                    dr, di = sums[down : down + 8, :count], sums[down : down + 8, count:]
                    r = c * (ur + dr) + s * (ui - di)
                    q = c * (ui + di) - s * (ur - dr)
                    re[f] = r if u == 0 else re[f] + r
                    im[f] = q if u == 0 else im[f] + q
            factor = jnp.where(2.0 * order < period_v, weight_ref[slot] * inverse, 0.0)
            hc, hs = cosv[24:32] * factor, sinv[24:32] * factor
            for f in range(fields):
                turned = (hc * re[f] + hs * im[f], hc * im[f] - hs * re[f])
                for ri, acc in enumerate(turned):
                    acc = acc + pltpu.roll(acc, 2, 0)
                    acc = acc + pltpu.roll(acc, 4, 0)
                    other = pltpu.roll(acc, 1, 0)
                    planes[2 * f + ri, pl.ds(slot, 1), :] = (acc + other)[0:1]
                    planes[2 * fields + 2 * f + ri, pl.ds(slot, 1), :] = (acc - other)[0:1]

        @pl.when(step == grid - 1)
        def _():
            for p in range(2):
                for v in range(nv):
                    for ri in range(2):
                        running = None
                        for l in range(nl):
                            at = ((p * nv + v) * nl + l) * 2 + ri
                            value = planes[at].astype(BF).astype(F32)
                            own_ref[at] = value if running is None else value + running
                            term = coupling_ref[v, l] * value
                            running = term if running is None else running + term
                        sum_ref[(p * nv + v) * 2 + ri] = running.astype(BF)

    smem = pl.BlockSpec(memory_space=pltpu.SMEM)
    return pl.pallas_call(
        kernel,
        name="analyse",
        grid=(grid,),
        in_specs=[
            smem,
            smem,
            smem,
            smem,
            pl.BlockSpec((fields, GROUP * rows, 128), lambda i: (0, i, 0)),
            pl.BlockSpec((1, count), lambda i: (0, 0)),
        ],
        out_specs=[
            pl.BlockSpec((16, slots, count), lambda i: (0, 0, 0)),
            pl.BlockSpec((16 // nl, slots, count), lambda i: (0, 0, 0)),
            pl.BlockSpec((1, count), lambda i: (0, 0)),
        ],
        out_shape=[
            jax.ShapeDtypeStruct((16, slots, count), F32),
            jax.ShapeDtypeStruct((16 // nl, slots, count), BF),
            jax.ShapeDtypeStruct((1, count), F32),
        ],
        scratch_shapes=[pltpu.VMEM((16, slots, count), F32)],
        compiler_params=pltpu.CompilerParams(dimension_semantics=("arbitrary",)),
    )(points, lat_ids, weights, coupling, points_rows, orders)


def deal(row, bands):
    count = row.shape[1]
    line, lane = iota((count, count), 0), iota((count, count), 1)
    column = jnp.sum(jnp.where(line == lane, row, 0.0), axis=1, keepdims=True)
    rank = jnp.sum(jnp.where(row < column, 1.0, 0.0), axis=1, keepdims=True).astype(jnp.int32)
    upper = rank >= count // 2
    pair = jnp.where(upper, count - 1 - rank, rank)
    place = pair % bands * 8 + pair // bands * 2 + jnp.where(upper, 1, 0)
    return jnp.sum(jnp.where(place == lane, column, 0.0), axis=0, keepdims=True)


def mix(own, earlier, bands, nv, nl):
    _, slots, count = own.shape

    def kernel(own_ref, earlier_ref, out_ref):
        for tile in range(count // 128):
            lanes = slice(128 * tile, 128 * tile + 128)
            value = []
            for k in range(16):
                source = k // (2 * nl) * 2 + k % 2
                value.append(own_ref[k, :, lanes] + earlier_ref[source, :, lanes].astype(F32))
            for d, w in enumerate(block_transpose(value)):
                out_ref[16 * tile + d] = w.astype(BF)

    return pl.pallas_call(kernel, name="mix", out_shape=jax.ShapeDtypeStruct((bands, slots, 128), BF))(own, earlier)


def make_rows(block, term_ref, cos_ref, second_ref, state, rows_ref):
    now, before, log_now = state
    half = cos_ref.shape[1]
    info = term_ref[block]
    restart = jnp.broadcast_to(info[:, 97:98], (8, half)) > 0.5
    current = jnp.where(restart, 1.0, now[...])
    previous = jnp.where(restart, 0.0, before[...])
    running = jnp.where(restart, second_ref[...], log_now[...])
    cosine = cos_ref[...]
    scale = None
    held = None
    for j in range(STEPS):
        if j % CHECK == 0:
            large = jnp.maximum(jnp.abs(current), jnp.abs(previous)) > 1.0
            shrink = jnp.where(large, 2.0**-60, 1.0)
            running = running + jnp.where(large, RESCALE_LOG, 0.0)
            current = current * shrink
            previous = previous * shrink
            scale = jnp.exp(running)
        value = current * scale
        if j % 2 == 0:
            held = value
        else:
            rows_ref[8 * (j - 1) : 8 * (j + 1), :] = jnp.concatenate([held, value], axis=0).astype(BF)
        current, previous = cosine * current - info[:, STEPS + j : STEPS + j + 1] * previous, current
        if j % FOLD == FOLD - 1:
            fold = info[:, j : j + 1]
            current = current * fold
            previous = previous * fold
    now[...] = current
    before[...] = previous
    log_now[...] = running


def plan(band, orders, lats):
    total = lats.shape[1]
    half = total // 2
    count = orders.shape[1]
    blocks = 4 * (-(-2 * (NT + 1) // (4 * STEPS))) + 2

    def kernel(band_ref, order_ref, lat_ref, term_ref, cos_ref, first_ref, second_ref, quads_ref):
        line, lane = iota((8, count), 0), iota((8, count), 1)
        target = 8 * band_ref[0] + 2 * (line % 4)
        first = jnp.sum(jnp.where(lane == target, order_ref[...], 0.0), axis=1, keepdims=True)
        second = jnp.sum(jnp.where(lane == target + 1, order_ref[...], 0.0), axis=1, keepdims=True)
        index = (iota((1, NT + 1), 1) + 1).astype(F32)
        terms = jnp.log(1.0 + 0.5 / index)
        turned_cos, turned_sin = turn_cos_sin((lat_ref[...] + 0.5) * (1.0 / (4.0 * NH)))
        log_sine = jnp.log(turned_sin)
        top = iota((8, half), 0) < 4
        cos_ref[...] = jnp.where(top, turned_cos[:, :half], turned_cos[:, half:])
        side = jnp.where(top, log_sine[:, :half], log_sine[:, half:])
        for order, target_ref in ((first, first_ref), (second, second_ref)):
            norm = jnp.sum(jnp.where(index <= order, terms, 0.0), axis=1, keepdims=True)
            target_ref[...] = (0.5 * math.log(0.5) + 0.5 * norm) + order * side
        first = jnp.broadcast_to(first, (8, 128))
        second = jnp.broadcast_to(second, (8, 128))
        ends = jnp.floor((NT + STEPS - first) * (1.0 / STEPS))
        stops = ends + jnp.floor((NT + STEPS - second) * (1.0 / STEPS))
        quads_ref[0] = jnp.max(jnp.floor((stops + 3.0) * 0.25).astype(jnp.int32))
        lane = iota((8, 128), 1)
        kind = lane // STEPS
        tick = (lane % STEPS).astype(F32)
        chain = 2.0 * (iota((8, 128), 0) % 4).astype(F32)

        def fill(block, carry):
            at = jnp.full((8, 128), block, jnp.int32).astype(F32)
            late = at >= ends
            order = jnp.where(late, second, first)
            row = order + STEPS * jnp.where(late, at - ends, at) + tick
            degree = row + 1.0
            offset = degree - order
            ahead = jnp.sqrt((4.0 * degree * degree - 1.0) / (offset * (degree + order)))
            below = jnp.maximum(4.0 * row * row - 1.0, 1.0)
            behind = (offset - 1.0) * (row + order) / below
            for reach in (1, 2, 4):
                ahead = ahead * jnp.where(lane % FOLD >= reach, pltpu.roll(ahead, reach, 1), 1.0)
            kappa = jnp.where(lane % FOLD == 0, 1.0, pltpu.roll(ahead, 1, 1))
            damp = kappa * kappa / (1.0 + 4.0 * row * (row + 1.0) / (NT * (NT + 1.0)))
            damp = jnp.where(row <= NT, damp, 0.0)
            last = jnp.where(lane == 96, chain + jnp.where(late, 1.0, 0.0), jnp.where(at == ends, 1.0, 0.0))
            rest = jnp.where(kind == 2, damp, last)
            term_ref[block] = jnp.where(kind == 0, ahead, jnp.where(kind == 1, behind, rest))
            return carry

        lax.fori_loop(0, blocks, fill, 0, unroll=2)

    smem = pl.BlockSpec(memory_space=pltpu.SMEM)
    vmem = pl.BlockSpec(memory_space=pltpu.VMEM)
    wide = jax.ShapeDtypeStruct((8, half), F32)
    return pl.pallas_call(
        kernel,
        name="plan",
        in_specs=[smem, vmem, vmem],
        out_specs=[vmem] * 4 + [smem],
        out_shape=[jax.ShapeDtypeStruct((blocks, 8, 128), F32), wide, wide, wide, jax.ShapeDtypeStruct((1,), jnp.int32)],
    )(band, orders, lats)


def legendre(own, tables):
    bands, slots, _ = own.shape
    total = bands * slots
    half = total // 2
    height = 8 * STEPS

    def kernel(own_ref, term_ref, cos_ref, first_ref, second_ref, quads_ref, out_ref, mixed, weights, rows0, rows1, rows2, rows3, kept0, kept1, acc, now, before, log_now):
        rows = (rows0, rows1, rows2, rows3)
        kept = (kept0, kept1)
        line, lane = iota((8, 128), 0), iota((8, 128), 1)
        low = line < 4
        for b in range(bands):
            mixed[b * slots : (b + 1) * slots] = own_ref[b].astype(F32)
        weights[...] = jnp.concatenate([mixed[:half], mixed[half:]], axis=1).astype(BF)
        acc[...] = jnp.zeros((256, half), F32)
        rows3[...] = jnp.zeros((height, half), BF)
        kept1[...] = jnp.zeros((height, 256), BF)
        now[...] = jnp.ones((8, half), F32)
        before[...] = jnp.zeros((8, half), F32)
        log_now[...] = first_ref[...]
        state = (now, before, log_now)

        def make(block, target):
            make_rows(block, term_ref, cos_ref, second_ref, state, target)

        def analysed(block, source, target):
            found = jnp.dot(source[...], weights[...], preferred_element_type=F32)
            info = term_ref[block]
            hit = lane % 8 == jnp.broadcast_to(info[:, 96:97], (8, 128)).astype(jnp.int32)
            masks = []
            for parity in range(2):
                match = hit & (lane // 64 == parity)
                masks.append((match & low, match & ~low))
            tops, lows = [], []
            for j in range(STEPS):
                part = found[8 * j : 8 * j + 8]
                part = jnp.where(low, part[:, :128], part[:, 128:])
                part = (part + pltpu.roll(part, 4, 0)) * info[:, 2 * STEPS + j : 2 * STEPS + j + 1]
                tops.append(jnp.where(masks[j % 2][0], part, 0.0))
                lows.append(jnp.where(masks[j % 2][1], part, 0.0))
            target[...] = jnp.concatenate([jnp.concatenate(tops, axis=0), jnp.concatenate(lows, axis=0)], axis=1).astype(BF)

        def gathered(coefficients, source):
            acc[...] += lax.dot_general(
                coefficients[...], source[...], (((0,), (0,)), ((), ())), preferred_element_type=F32
            )

        make(0, rows0)

        def body(i, carry):
            for k in range(4):
                make(4 * i + k + 1, rows[(k + 1) % 4])
                analysed(4 * i + k, rows[k], kept[k % 2])
                gathered(kept[(k + 1) % 2], rows[(k + 3) % 4])
            return carry

        lax.fori_loop(0, quads_ref[0], body, 0)
        gathered(kept1, rows3)
        for h in range(2):
            for c in range(half // 128):
                at = h * half + 128 * c
                mixed[at : at + 128] = jnp.transpose(acc[128 * h : 128 * h + 128, 128 * c : 128 * c + 128])
        for b in range(bands):
            out_ref[b] = mixed[b * slots : (b + 1) * slots].astype(BF)

    vmem = pl.BlockSpec(memory_space=pltpu.VMEM)
    return pl.pallas_call(
        kernel,
        name="legendre",
        in_specs=[vmem] * 5 + [pl.BlockSpec(memory_space=pltpu.SMEM)],
        out_specs=vmem,
        out_shape=jax.ShapeDtypeStruct((bands, slots, 128), BF),
        scratch_shapes=[
            pltpu.VMEM((total, 128), F32),
            pltpu.VMEM((half, 256), BF),
            pltpu.VMEM((height, half), BF),
            pltpu.VMEM((height, half), BF),
            pltpu.VMEM((height, half), BF),
            pltpu.VMEM((height, half), BF),
            pltpu.VMEM((height, 256), BF),
            pltpu.VMEM((height, 256), BF),
            pltpu.VMEM((256, half), F32),
            pltpu.VMEM((8, half), F32),
            pltpu.VMEM((8, half), F32),
            pltpu.VMEM((8, half), F32),
        ],
    )(own, *tables)


def synthesise(back, points, lat_ids, orders, nv, nl, width):
    bands, slots, _ = back.shape
    fields = nv * nl
    rows = 2 * (width // 128)
    span = window_rows(width)
    tiles = span // 8
    middle = tiles // 2
    count = orders.shape[1]
    grid = slots // GROUP

    def kernel(points_ref, lat_ref, back_ref, order_ref, out_ref, planes):
        step = pl.program_id(0)

        @pl.when(step == 0)
        def _():
            for tile in range(count // 128):
                value = [back_ref[16 * tile + d].astype(F32) for d in range(16)]
                for k, w in enumerate(block_transpose(value)):
                    planes[k, :, 128 * tile : 128 * tile + 128] = w

        order = order_ref[...]
        position = 128 * (iota((span, 128), 0) // 2) + iota((span, 128), 1)
        shared, blocks = angle_rows(order, tiles)
        sign = jnp.where(iota((8, count), 0) % 2 == 0, 1.0, -1.0)
        double = jnp.where(order == 0.0, 1.0, 2.0)
        for i in range(GROUP):
            base, off = window(i, rows)
            slot = step * GROUP + i
            period = points_ref[lat_ref[slot]]
            cosv, sinv, period_v, _ = slot_angles(shared, blocks, order, off, period)
            table = inner_table(cosv, sinv)
            factor = jnp.where(2.0 * order < period_v, double, 0.0)
            hc, hs = cosv[24:32] * factor, sinv[24:32] * factor
            turns = []
            for t in range(0, tiles, 2):
                pair = []
                for source in (cosv, sinv):
                    lines = []
                    for k in (t, t + 1):
                        u = k - middle if k >= middle else middle - 1 - k
                        line = source[16 + u : 17 + u]
                        if source is sinv and k < middle:
                            line = -line
                        lines.append(jnp.broadcast_to(line, (8, count)))
                    pair.append(jnp.concatenate(lines, axis=0).astype(BF))
                turns.append(pair)
            parts = []
            for f in range(fields):
                both = []
                for ri in range(2):
                    even = planes[2 * f + ri, pl.ds(slot, 1), :]
                    odd = planes[2 * fields + 2 * f + ri, pl.ds(slot, 1), :]
                    both.append(even + sign * odd)
                re, im = both
                wr, wi = hc * re - hs * im, hs * re + hc * im
                wr = jnp.concatenate([wr, wr], axis=0).astype(BF)
                wi = jnp.concatenate([wi, wi], axis=0).astype(BF)
                zr = [c * wr - s * wi for c, s in turns]
                zi = [s * wr + c * wi for c, s in turns]
                parts.append(jnp.concatenate([jnp.concatenate(zr, axis=0), jnp.concatenate(zi, axis=0)], axis=1))
            waves = jnp.concatenate(parts, axis=0)
            values = lax.dot_general(waves, table, (((1,), (1,)), ((), ())), preferred_element_type=F32)
            inside = position < period + 64 * off
            starts = position[:16] >= 64 * off
            for f in range(fields):
                part = jnp.where(inside, values[f * span : (f + 1) * span], 0.0)
                if off:
                    first = jnp.where(starts, part[:16], out_ref[f, base : base + 16, :].astype(F32))
                    out_ref[f, base : base + 16, :] = first.astype(BF)
                    out_ref[f, base + 16 : base + span, :] = part[16:].astype(BF)
                else:
                    out_ref[f, base : base + span, :] = part.astype(BF)

    smem = pl.BlockSpec(memory_space=pltpu.SMEM)
    return pl.pallas_call(
        kernel,
        name="synthesise",
        grid=(grid,),
        in_specs=[
            smem,
            smem,
            pl.BlockSpec((bands, slots, 128), lambda i: (0, 0, 0)),
            pl.BlockSpec((1, count), lambda i: (0, 0)),
        ],
        out_specs=pl.BlockSpec((fields, GROUP * rows, 128), lambda i: (0, i, 0)),
        out_shape=jax.ShapeDtypeStruct((fields, slots * rows, 128), BF),
        scratch_shapes=[pltpu.VMEM((16, slots, count), F32)],
        compiler_params=pltpu.CompilerParams(dimension_semantics=("arbitrary",)),
    )(points, lat_ids, back, orders)


def solution(mesh):
    bands, parts = mesh.shape["band"], mesh.shape["fld"]

    def on_device(grid_field, coupling, points, lat_ids, wn_ids):
        nv, nl, slots, _, width = grid_field.shape
        mine = wn_ids.shape[0]
        packed = jnp.concatenate([wn_ids, lat_ids])
        spread = jnp.broadcast_to(packed[None], (bands, mine + slots))
        known = lax.all_to_all(spread, "band", split_axis=0, concat_axis=0, tiled=True)
        orders = known[:, :mine].reshape(1, bands * mine).astype(F32)
        lats = known[:, mine:].reshape(1, bands * slots).astype(F32)
        weights = math.pi / (2.0 * NH) * jnp.sin(math.pi * (lat_ids.astype(F32) + 0.5) / (2.0 * NH))
        own, sums, orders = analyse(as_rows(grid_field), points, lat_ids, weights, orders, coupling, nv, nl, width)
        earlier = jnp.zeros_like(sums)
        for shift in range(1, parts):
            moved = lax.ppermute(sums, "fld", [(k, k + shift) for k in range(parts - shift)])
            earlier = moved if shift == 1 else earlier + moved
        own, orders = lax.optimization_barrier((mix(own, earlier, bands, nv, nl), orders))
        own = lax.all_to_all(own, "band", split_axis=0, concat_axis=0, tiled=True)
        band = lax.axis_index("band").astype(jnp.int32).reshape(1)
        back = legendre(own, plan(band, orders, lats))
        back = lax.all_to_all(back, "band", split_axis=0, concat_axis=0, tiled=True)
        rows = synthesise(back, points, lat_ids, orders, nv, nl, width)
        return from_rows(rows, nv, nl, slots, width)

    in_specs = (P(None, "fld", "band", None, None), P(None, "fld"), P(), P("band"), P("band"))
    return jax.shard_map(on_device, mesh=mesh, in_specs=in_specs, out_specs=in_specs[0], check_vma=False)
```

```python
import math

import jax
import jax.numpy as jnp
from jax import lax
from jax.experimental import pallas as pl
from jax.experimental.pallas import tpu as pltpu
from jax.experimental.layout import Layout, with_layout_constraint
from jax.sharding import PartitionSpec as P

NT = 1279
NH = 1280
BF = jnp.bfloat16
F32 = jnp.float32
GROUP = 8
STEPS = 32
CHECK = 16
FOLD = 8
RESCALE_LOG = 60.0 * math.log(2.0)


def resident(*arrays):
    return [pltpu.with_memory_space_constraint(a, pltpu.VMEM) for a in arrays]


def iota(shape, dim):
    return lax.broadcasted_iota(jnp.int32, shape, dim)


def turn_cos_sin(turns):
    y = turns * turns
    s = -0.59828975 + y * 0.07765416
    s = 2.55007732 + y * s
    s = -5.16771007 + y * s
    s = turns * (3.14159264 + y * s)
    c = -1.33187126 + y * 0.21967748
    c = 4.05841064 + y * c
    c = -4.9347928 + y * c
    c = 0.99999995 + y * c
    twice = s + s
    return 1.0 - twice * s, twice * c


def block_transpose(planes):
    lane = iota((1, 128), 1) // 8
    planes = list(planes)
    for bit in (8, 4, 2, 1):
        low = (lane & bit) == 0
        for at in range(16):
            if at & bit:
                continue
            a, b = planes[at], planes[at | bit]
            planes[at] = jnp.where(low, a, pltpu.roll(b, 8 * bit, 1))
            planes[at | bit] = jnp.where(low, pltpu.roll(a, 128 - 8 * bit, 1), b)
    return planes


def window(i, rows):
    start = i * rows
    base = start // 16 * 16
    return base, start - base


def window_rows(width):
    return -(-(2 * (width // 128) + 14) // 16) * 16


def as_rows(field):
    nv, nl, slots, _, width = field.shape
    blocks = width // 128
    split = field.reshape(nv, nl, slots, 2, blocks, 128)
    split = with_layout_constraint(split, Layout(major_to_minor=(0, 1, 2, 4, 3, 5)))
    return split.transpose(0, 1, 2, 4, 3, 5).reshape(nv * nl, slots * 2 * blocks, 128)


def from_rows(rows, nv, nl, slots, width):
    split = rows.reshape(nv, nl, slots, width // 128, 2, 128).transpose(0, 1, 2, 4, 3, 5)
    split = with_layout_constraint(split, Layout(major_to_minor=(0, 1, 2, 4, 3, 5)))
    return split.reshape(nv, nl, slots, 2, width)


def angle_rows(order, tiles):
    count = order.shape[1]
    row = iota((8, count), 0)
    steps = jnp.where(row < tiles // 2, 256 * (2 * row + 1), 64)
    shared = jnp.concatenate([row, 8 * row, steps], axis=0).astype(F32) * order
    blocks = (128 * (2 * tiles - 2 + row // 2)).astype(F32)
    return shared, blocks


def slot_angles(shared, blocks, order, off, period):
    product = jnp.concatenate([shared, (blocks - 64.0 * off) * order], axis=0)
    period_v = jnp.full(order.shape, period, jnp.int32).astype(F32)
    inverse = 1.0 / period_v
    turns = (product - jnp.floor(product * inverse + 0.5) * period_v) * inverse
    cosv, sinv = turn_cos_sin(turns)
    return cosv, sinv, period_v, inverse


def inner_table(cosv, sinv):
    fc, fs = cosv[0:8], sinv[0:8]
    ec, es = cosv[8:16], sinv[8:16]
    wc, ws = cosv[23:24], sinv[23:24]
    ec = jnp.concatenate([ec, ec * wc - es * ws], axis=0)
    es = jnp.concatenate([es, es * wc + cosv[8:16] * ws], axis=0)
    parts_c, parts_s = [], []
    for a in range(16):
        c, s = ec[a : a + 1], es[a : a + 1]
        parts_c.append(c * fc - s * fs)
        parts_s.append((-s) * fc - c * fs)
    halves = [jnp.concatenate(p, axis=0).astype(BF) for p in (parts_c, parts_s)]
    return jnp.concatenate(halves, axis=1)


def analyse(points_rows, points, lat_ids, weights, orders, coupling, nv, nl, width):
    fields = nv * nl
    slots = lat_ids.shape[0]
    rows = 2 * (width // 128)
    span = window_rows(width)
    tiles = span // 8
    middle = tiles // 2
    bands = orders.shape[0]
    count = 8 * bands
    grid = slots // GROUP

    def kernel(points_ref, lat_ref, weight_ref, coupling_ref, x_ref, given_ref, own_ref, sum_ref, order_ref, planes):
        step = pl.program_id(0)

        @pl.when(step == 0)
        def _():
            order_ref[...] = deal(given_ref[...], bands)

        order = order_ref[...]
        position = (128 * (iota((span, 128), 0) // 2) + iota((span, 128), 1)).astype(F32)
        shared, blocks = angle_rows(order, tiles)
        for i in range(GROUP):
            base, off = window(i, rows)
            slot = step * GROUP + i
            period = points_ref[lat_ref[slot]]
            cosv, sinv, period_v, inverse = slot_angles(shared, blocks, order, off, period)
            table = inner_table(cosv, sinv)
            limit = jnp.full((1, 128), period, jnp.int32).astype(F32) + 64.0 * off
            keep = jnp.minimum(jnp.maximum(limit - position, 0.0), 1.0)
            if off:
                head = jnp.where(position[:16] >= 64.0 * off, keep[:16], 0.0)
                keep = jnp.concatenate([head, keep[16:]], axis=0)
            keep = keep.astype(BF)
            data = jnp.concatenate([x_ref[f, base : base + span, :] * keep for f in range(fields)], axis=0)
            sums = jnp.dot(data, table, preferred_element_type=F32)
            re = [None] * fields
            im = [None] * fields
            for u in range(middle):
                c, s = cosv[16 + u : 17 + u], sinv[16 + u : 17 + u]
                for f in range(fields):
                    up = f * span + 8 * (middle + u)
                    down = f * span + 8 * (middle - 1 - u)
                    ur, ui = sums[up : up + 8, :count], sums[up : up + 8, count:]
                    dr, di = sums[down : down + 8, :count], sums[down : down + 8, count:]
                    r = c * (ur + dr) + s * (ui - di)
                    q = c * (ui + di) - s * (ur - dr)
                    re[f] = r if u == 0 else re[f] + r
                    im[f] = q if u == 0 else im[f] + q
            factor = jnp.where(2.0 * order < period_v, weight_ref[slot] * inverse, 0.0)
            hc, hs = cosv[24:32] * factor, sinv[24:32] * factor
            for f in range(fields):
                turned = (hc * re[f] + hs * im[f], hc * im[f] - hs * re[f])
                for ri, acc in enumerate(turned):
                    acc = acc + pltpu.roll(acc, 2, 0)
                    acc = acc + pltpu.roll(acc, 4, 0)
                    other = pltpu.roll(acc, 1, 0)
                    planes[2 * f + ri, pl.ds(slot, 1), :] = (acc + other)[0:1]
                    planes[2 * fields + 2 * f + ri, pl.ds(slot, 1), :] = (acc - other)[0:1]

        @pl.when(step == grid - 1)
        def _():
            for p in range(2):
                for v in range(nv):
                    for ri in range(2):
                        running = None
                        for l in range(nl):
                            at = ((p * nv + v) * nl + l) * 2 + ri
                            value = planes[at].astype(BF).astype(F32)
                            own_ref[at] = value if running is None else value + running
                            term = coupling_ref[v, l] * value
                            running = term if running is None else running + term
                        sum_ref[(p * nv + v) * 2 + ri] = running.astype(BF)

    smem = pl.BlockSpec(memory_space=pltpu.SMEM)
    return pl.pallas_call(
        kernel,
        name="analyse",
        grid=(grid,),
        in_specs=[
            smem,
            smem,
            smem,
            smem,
            pl.BlockSpec((fields, GROUP * rows, 128), lambda i: (0, i, 0)),
            pl.BlockSpec((bands, 8), lambda i: (0, 0)),
        ],
        out_specs=[
            pl.BlockSpec((16, slots, count), lambda i: (0, 0, 0)),
            pl.BlockSpec((16 // nl, slots, count), lambda i: (0, 0, 0)),
            pl.BlockSpec((1, count), lambda i: (0, 0)),
        ],
        out_shape=[
            jax.ShapeDtypeStruct((16, slots, count), F32),
            jax.ShapeDtypeStruct((16 // nl, slots, count), BF),
            jax.ShapeDtypeStruct((1, count), F32),
        ],
        scratch_shapes=[pltpu.VMEM((16, slots, count), F32)],
        compiler_params=pltpu.CompilerParams(dimension_semantics=("arbitrary",)),
    )(points, lat_ids, weights, coupling, points_rows, orders)


def deal(given, bands):
    count = bands * 8
    line, lane = iota((bands, count), 0), iota((bands, count), 1)
    spots = jnp.zeros((bands, count), F32)
    for e in range(8):
        spots = jnp.where(lane == 8 * line + e, given[:, e : e + 1], spots)
    row = jnp.sum(spots, axis=0, keepdims=True)
    line, lane = iota((count, count), 0), iota((count, count), 1)
    column = jnp.sum(jnp.where(line == lane, row, 0.0), axis=1, keepdims=True)
    rank = jnp.sum(jnp.where(row < column, 1.0, 0.0), axis=1, keepdims=True).astype(jnp.int32)
    upper = rank >= count // 2
    pair = jnp.where(upper, count - 1 - rank, rank)
    place = pair % bands * 8 + pair // bands * 2 + jnp.where(upper, 1, 0)
    return jnp.sum(jnp.where(place == lane, column, 0.0), axis=0, keepdims=True)


def mix(own, earlier, bands, nv, nl):
    _, slots, count = own.shape

    def kernel(own_ref, earlier_ref, out_ref):
        for tile in range(count // 128):
            lanes = slice(128 * tile, 128 * tile + 128)
            value = []
            for k in range(16):
                source = k // (2 * nl) * 2 + k % 2
                value.append(own_ref[k, :, lanes] + earlier_ref[source, :, lanes].astype(F32))
            for d, w in enumerate(block_transpose(value)):
                out_ref[16 * tile + d] = w.astype(BF)

    return pl.pallas_call(kernel, name="mix", out_shape=jax.ShapeDtypeStruct((bands, slots, 128), BF))(*resident(own, earlier))


def make_rows(block, term_ref, cos_ref, second_ref, state, rows_ref):
    now, before, log_now = state
    half = cos_ref.shape[1]
    info = term_ref[block]
    restart = jnp.broadcast_to(info[:, 97:98], (8, half)) > 0.5
    current = jnp.where(restart, 1.0, now[...])
    previous = jnp.where(restart, 0.0, before[...])
    running = jnp.where(restart, second_ref[...], log_now[...])
    cosine = cos_ref[...]
    scale = None
    held = None
    for j in range(STEPS):
        if j % CHECK == 0:
            large = jnp.maximum(jnp.abs(current), jnp.abs(previous)) > 1.0
            shrink = jnp.where(large, 2.0**-60, 1.0)
            running = running + jnp.where(large, RESCALE_LOG, 0.0)
            current = current * shrink
            previous = previous * shrink
            scale = jnp.exp(running)
        value = current * scale
        if j % 2 == 0:
            held = value
        else:
            rows_ref[8 * (j - 1) : 8 * (j + 1), :] = jnp.concatenate([held, value], axis=0).astype(BF)
        current, previous = cosine * current - info[:, STEPS + j : STEPS + j + 1] * previous, current
        if j % FOLD == FOLD - 1:
            fold = info[:, j : j + 1]
            current = current * fold
            previous = previous * fold
    now[...] = current
    before[...] = previous
    log_now[...] = running


def plan(band, orders, lats):
    total = lats.shape[1]
    half = total // 2
    count = orders.shape[1]
    blocks = 8 * (-(-(4 * (-(-2 * (NT + 1) // (4 * STEPS))) + 2) // 8))

    def kernel(band_ref, order_ref, lat_ref, term_ref, cos_ref, first_ref, second_ref, quads_ref):
        line, lane = iota((8, count), 0), iota((8, count), 1)
        target = 8 * band_ref[0] + 2 * (line % 4)
        first = jnp.sum(jnp.where(lane == target, order_ref[...], 0.0), axis=1, keepdims=True)
        second = jnp.sum(jnp.where(lane == target + 1, order_ref[...], 0.0), axis=1, keepdims=True)
        index = (iota((1, NT + 1), 1) + 1).astype(F32)
        terms = jnp.log(1.0 + 0.5 / index)
        turned_cos, turned_sin = turn_cos_sin((lat_ref[...] + 0.5) * (1.0 / (4.0 * NH)))
        log_sine = jnp.log(turned_sin)
        top = iota((8, half), 0) < 4
        cos_ref[...] = jnp.where(top, turned_cos[:, :half], turned_cos[:, half:])
        side = jnp.where(top, log_sine[:, :half], log_sine[:, half:])
        for order, target_ref in ((first, first_ref), (second, second_ref)):
            norm = jnp.sum(jnp.where(index <= order, terms, 0.0), axis=1, keepdims=True)
            target_ref[...] = (0.5 * math.log(0.5) + 0.5 * norm) + order * side
        first = jnp.broadcast_to(first, (8, 128))
        second = jnp.broadcast_to(second, (8, 128))
        ends = jnp.floor((NT + STEPS - first) * (1.0 / STEPS))
        stops = ends + jnp.floor((NT + STEPS - second) * (1.0 / STEPS))
        quads_ref[0] = jnp.max(jnp.floor((stops + 3.0) * 0.25).astype(jnp.int32))
        lane = iota((8, 128), 1)
        kind = lane // STEPS
        tick = (lane % STEPS).astype(F32)
        chain = 2.0 * (iota((8, 128), 0) % 4).astype(F32)

        def fill(block):
            at = jnp.full((8, 128), block, jnp.int32).astype(F32)
            late = at >= ends
            order = jnp.where(late, second, first)
            row = order + STEPS * jnp.where(late, at - ends, at) + tick
            degree = row + 1.0
            offset = degree - order
            ahead = jnp.sqrt((4.0 * degree * degree - 1.0) / (offset * (degree + order)))
            below = jnp.maximum(4.0 * row * row - 1.0, 1.0)
            behind = (offset - 1.0) * (row + order) / below
            for reach in (1, 2, 4):
                ahead = ahead * jnp.where(lane % FOLD >= reach, pltpu.roll(ahead, reach, 1), 1.0)
            kappa = jnp.where(lane % FOLD == 0, 1.0, pltpu.roll(ahead, 1, 1))
            damp = kappa * kappa / (1.0 + 4.0 * row * (row + 1.0) / (NT * (NT + 1.0)))
            damp = jnp.where(row <= NT, damp, 0.0)
            last = jnp.where(lane == 96, chain + jnp.where(late, 1.0, 0.0), jnp.where(at == ends, 1.0, 0.0))
            rest = jnp.where(kind == 2, damp, last)
            term_ref[block] = jnp.where(kind == 0, ahead, jnp.where(kind == 1, behind, rest))

        def several(i, carry):
            for k in range(8):
                fill(8 * i + k)
            return carry

        lax.fori_loop(0, blocks // 8, several, 0)

    smem = pl.BlockSpec(memory_space=pltpu.SMEM)
    vmem = pl.BlockSpec(memory_space=pltpu.VMEM)
    wide = jax.ShapeDtypeStruct((8, half), F32)
    return pl.pallas_call(
        kernel,
        name="plan",
        in_specs=[smem, vmem, vmem],
        out_specs=[vmem] * 4 + [smem],
        out_shape=[jax.ShapeDtypeStruct((blocks, 8, 128), F32), wide, wide, wide, jax.ShapeDtypeStruct((1,), jnp.int32)],
    )(band, orders, lats)


def legendre(own, tables):
    bands, slots, _ = own.shape
    total = bands * slots
    half = total // 2
    height = 8 * STEPS

    def kernel(own_ref, term_ref, cos_ref, first_ref, second_ref, quads_ref, out_ref, mixed, weights, rows0, rows1, rows2, rows3, kept0, kept1, acc, now, before, log_now):
        rows = (rows0, rows1, rows2, rows3)
        kept = (kept0, kept1)
        line, lane = iota((8, 128), 0), iota((8, 128), 1)
        low = line < 4
        for b in range(bands):
            mixed[b * slots : (b + 1) * slots] = own_ref[b].astype(F32)
        weights[...] = jnp.concatenate([mixed[:half], mixed[half:]], axis=1).astype(BF)
        acc[...] = jnp.zeros((256, half), F32)
        rows3[...] = jnp.zeros((height, half), BF)
        kept1[...] = jnp.zeros((height, 256), BF)
        now[...] = jnp.ones((8, half), F32)
        before[...] = jnp.zeros((8, half), F32)
        log_now[...] = first_ref[...]
        state = (now, before, log_now)

        def make(block, target):
            make_rows(block, term_ref, cos_ref, second_ref, state, target)

        def analysed(block, source, target):
            found = jnp.dot(source[...], weights[...], preferred_element_type=F32)
            info = term_ref[block]
            hit = lane % 8 == jnp.broadcast_to(info[:, 96:97], (8, 128)).astype(jnp.int32)
            masks = []
            for parity in range(2):
                match = hit & (lane // 64 == parity)
                masks.append((match & low, match & ~low))
            tops, lows = [], []
            for j in range(STEPS):
                part = found[8 * j : 8 * j + 8]
                part = jnp.where(low, part[:, :128], part[:, 128:])
                part = (part + pltpu.roll(part, 4, 0)) * info[:, 2 * STEPS + j : 2 * STEPS + j + 1]
                tops.append(jnp.where(masks[j % 2][0], part, 0.0))
                lows.append(jnp.where(masks[j % 2][1], part, 0.0))
            target[...] = jnp.concatenate([jnp.concatenate(tops, axis=0), jnp.concatenate(lows, axis=0)], axis=1).astype(BF)

        def gathered(coefficients, source):
            acc[...] += lax.dot_general(
                coefficients[...], source[...], (((0,), (0,)), ((), ())), preferred_element_type=F32
            )

        make(0, rows0)

        def body(i, carry):
            for k in range(4):
                make(4 * i + k + 1, rows[(k + 1) % 4])
                analysed(4 * i + k, rows[k], kept[k % 2])
                gathered(kept[(k + 1) % 2], rows[(k + 3) % 4])
            return carry

        lax.fori_loop(0, quads_ref[0], body, 0)
        gathered(kept1, rows3)
        for h in range(2):
            for c in range(half // 128):
                at = h * half + 128 * c
                mixed[at : at + 128] = jnp.transpose(acc[128 * h : 128 * h + 128, 128 * c : 128 * c + 128])
        for b in range(bands):
            out_ref[b] = mixed[b * slots : (b + 1) * slots].astype(BF)

    vmem = pl.BlockSpec(memory_space=pltpu.VMEM)
    return pl.pallas_call(
        kernel,
        name="legendre",
        in_specs=[vmem] * 5 + [pl.BlockSpec(memory_space=pltpu.SMEM)],
        out_specs=vmem,
        out_shape=jax.ShapeDtypeStruct((bands, slots, 128), BF),
        scratch_shapes=[
            pltpu.VMEM((total, 128), F32),
            pltpu.VMEM((half, 256), BF),
            pltpu.VMEM((height, half), BF),
            pltpu.VMEM((height, half), BF),
            pltpu.VMEM((height, half), BF),
            pltpu.VMEM((height, half), BF),
            pltpu.VMEM((height, 256), BF),
            pltpu.VMEM((height, 256), BF),
            pltpu.VMEM((256, half), F32),
            pltpu.VMEM((8, half), F32),
            pltpu.VMEM((8, half), F32),
            pltpu.VMEM((8, half), F32),
        ],
    )(*resident(own, *tables[:4]), tables[4])


def synthesise(back, points, lat_ids, orders, nv, nl, width):
    bands, slots, _ = back.shape
    fields = nv * nl
    rows = 2 * (width // 128)
    span = window_rows(width)
    tiles = span // 8
    middle = tiles // 2
    count = orders.shape[1]
    grid = slots // GROUP

    def kernel(points_ref, lat_ref, back_ref, order_ref, out_ref, planes):
        step = pl.program_id(0)

        @pl.when(step == 0)
        def _():
            for tile in range(count // 128):
                value = [back_ref[16 * tile + d].astype(F32) for d in range(16)]
                for k, w in enumerate(block_transpose(value)):
                    planes[k, :, 128 * tile : 128 * tile + 128] = w

        order = order_ref[...]
        position = 128 * (iota((span, 128), 0) // 2) + iota((span, 128), 1)
        shared, blocks = angle_rows(order, tiles)
        sign = jnp.where(iota((8, count), 0) % 2 == 0, 1.0, -1.0)
        double = jnp.where(order == 0.0, 1.0, 2.0)
        for i in range(GROUP):
            base, off = window(i, rows)
            slot = step * GROUP + i
            period = points_ref[lat_ref[slot]]
            cosv, sinv, period_v, _ = slot_angles(shared, blocks, order, off, period)
            table = inner_table(cosv, sinv)
            factor = jnp.where(2.0 * order < period_v, double, 0.0)
            hc, hs = cosv[24:32] * factor, sinv[24:32] * factor
            turns = []
            for t in range(0, tiles, 2):
                pair = []
                for source in (cosv, sinv):
                    lines = []
                    for k in (t, t + 1):
                        u = k - middle if k >= middle else middle - 1 - k
                        line = source[16 + u : 17 + u]
                        if source is sinv and k < middle:
                            line = -line
                        lines.append(jnp.broadcast_to(line, (8, count)))
                    pair.append(jnp.concatenate(lines, axis=0).astype(BF))
                turns.append(pair)
            parts = []
            for f in range(fields):
                both = []
                for ri in range(2):
                    even = planes[2 * f + ri, pl.ds(slot, 1), :]
                    odd = planes[2 * fields + 2 * f + ri, pl.ds(slot, 1), :]
                    both.append(even + sign * odd)
                re, im = both
                wr, wi = hc * re - hs * im, hs * re + hc * im
                wr = jnp.concatenate([wr, wr], axis=0).astype(BF)
                wi = jnp.concatenate([wi, wi], axis=0).astype(BF)
                zr = [c * wr - s * wi for c, s in turns]
                zi = [s * wr + c * wi for c, s in turns]
                parts.append(jnp.concatenate([jnp.concatenate(zr, axis=0), jnp.concatenate(zi, axis=0)], axis=1))
            waves = jnp.concatenate(parts, axis=0)
            values = lax.dot_general(waves, table, (((1,), (1,)), ((), ())), preferred_element_type=F32)
            inside = position < period + 64 * off
            starts = position[:16] >= 64 * off
            for f in range(fields):
                part = jnp.where(inside, values[f * span : (f + 1) * span], 0.0)
                if off:
                    first = jnp.where(starts, part[:16], out_ref[f, base : base + 16, :].astype(F32))
                    out_ref[f, base : base + 16, :] = first.astype(BF)
                    out_ref[f, base + 16 : base + span, :] = part[16:].astype(BF)
                else:
                    out_ref[f, base : base + span, :] = part.astype(BF)

    smem = pl.BlockSpec(memory_space=pltpu.SMEM)
    return pl.pallas_call(
        kernel,
        name="synthesise",
        grid=(grid,),
        in_specs=[
            smem,
            smem,
            pl.BlockSpec((bands, slots, 128), lambda i: (0, 0, 0)),
            pl.BlockSpec((1, count), lambda i: (0, 0)),
        ],
        out_specs=pl.BlockSpec((fields, GROUP * rows, 128), lambda i: (0, i, 0)),
        out_shape=jax.ShapeDtypeStruct((fields, slots * rows, 128), BF),
        scratch_shapes=[pltpu.VMEM((16, slots, count), F32)],
        compiler_params=pltpu.CompilerParams(dimension_semantics=("arbitrary",)),
    )(points, lat_ids, back, orders)


def solution(mesh):
    bands, parts = mesh.shape["band"], mesh.shape["fld"]

    def on_device(grid_field, coupling, points, lat_ids, wn_ids):
        nv, nl, slots, _, width = grid_field.shape
        mine = wn_ids.shape[0]
        spread = jnp.concatenate(
            [jnp.broadcast_to(wn_ids[None], (bands, mine)), jnp.broadcast_to(lat_ids[None], (bands, slots))], axis=1
        )
        known = lax.all_to_all(spread, "band", split_axis=0, concat_axis=0, tiled=True)
        orders = known[:, :mine].astype(F32)
        lats = known[:, mine:].reshape(1, bands * slots).astype(F32)
        weights = math.pi / (2.0 * NH) * jnp.sin(math.pi * (lat_ids.astype(F32) + 0.5) / (2.0 * NH))
        own, sums, orders = analyse(as_rows(grid_field), points, lat_ids, weights, orders, coupling, nv, nl, width)
        earlier = jnp.zeros_like(sums)
        for shift in range(1, parts):
            moved = lax.ppermute(sums, "fld", [(k, k + shift) for k in range(parts - shift)])
            earlier = moved if shift == 1 else earlier + moved
        own, orders = lax.optimization_barrier((mix(own, earlier, bands, nv, nl), orders))
        own = lax.all_to_all(own, "band", split_axis=0, concat_axis=0, tiled=True)
        band = lax.axis_index("band").astype(jnp.int32).reshape(1)
        back = legendre(own, plan(band, orders, lats))
        back = lax.all_to_all(back, "band", split_axis=0, concat_axis=0, tiled=True)
        rows = synthesise(back, points, lat_ids, orders, nv, nl, width)
        return from_rows(rows, nv, nl, slots, width)

    in_specs = (P(None, "fld", "band", None, None), P(None, "fld"), P(), P("band"), P("band"))
    return jax.shard_map(on_device, mesh=mesh, in_specs=in_specs, out_specs=in_specs[0], check_vma=False)
```

```python
import math

import jax
import jax.numpy as jnp
from jax import lax
from jax.experimental import pallas as pl
from jax.experimental.pallas import tpu as pltpu
from jax.experimental.layout import Layout, with_layout_constraint
from jax.sharding import PartitionSpec as P

NT = 1279
NH = 1280
BF = jnp.bfloat16
F32 = jnp.float32
GROUP = 8
STEPS = 32
CHECK = 16
FOLD = 8
RESCALE_LOG = 60.0 * math.log(2.0)


def resident(*arrays):
    return [pltpu.with_memory_space_constraint(a, pltpu.VMEM) for a in arrays]


def iota(shape, dim):
    return lax.broadcasted_iota(jnp.int32, shape, dim)


def turn_cos_sin(turns):
    y = turns * turns
    s = -0.59828975 + y * 0.07765416
    s = 2.55007732 + y * s
    s = -5.16771007 + y * s
    s = turns * (3.14159264 + y * s)
    c = -1.33187126 + y * 0.21967748
    c = 4.05841064 + y * c
    c = -4.9347928 + y * c
    c = 0.99999995 + y * c
    twice = s + s
    return 1.0 - twice * s, twice * c


def block_transpose(planes):
    lane = iota((1, 128), 1) // 8
    planes = list(planes)
    for bit in (8, 4, 2, 1):
        low = (lane & bit) == 0
        for at in range(16):
            if at & bit:
                continue
            a, b = planes[at], planes[at | bit]
            planes[at] = jnp.where(low, a, pltpu.roll(b, 8 * bit, 1))
            planes[at | bit] = jnp.where(low, pltpu.roll(a, 128 - 8 * bit, 1), b)
    return planes


def window(i, rows):
    start = i * rows
    base = start // 16 * 16
    return base, start - base


def window_rows(width):
    return -(-(2 * (width // 128) + 14) // 16) * 16


def as_rows(field):
    nv, nl, slots, _, width = field.shape
    blocks = width // 128
    split = field.reshape(nv, nl, slots, 2, blocks, 128)
    split = with_layout_constraint(split, Layout(major_to_minor=(0, 1, 2, 4, 3, 5)))
    return split.transpose(0, 1, 2, 4, 3, 5).reshape(nv * nl, slots * 2 * blocks, 128)


def from_rows(rows, nv, nl, slots, width):
    split = rows.reshape(nv, nl, slots, width // 128, 2, 128).transpose(0, 1, 2, 4, 3, 5)
    split = with_layout_constraint(split, Layout(major_to_minor=(0, 1, 2, 4, 3, 5)))
    return split.reshape(nv, nl, slots, 2, width)


def angle_rows(order, tiles):
    count = order.shape[1]
    row = iota((8, count), 0)
    steps = jnp.where(row < tiles // 2, 256 * (2 * row + 1), 64)
    shared = jnp.concatenate([row, 8 * row, steps], axis=0).astype(F32) * order
    blocks = (128 * (2 * tiles - 2 + row // 2)).astype(F32)
    return shared, blocks


def slot_angles(shared, blocks, order, off, period):
    product = jnp.concatenate([shared, (blocks - 64.0 * off) * order], axis=0)
    period_v = jnp.full(order.shape, period, jnp.int32).astype(F32)
    inverse = 1.0 / period_v
    turns = (product - jnp.floor(product * inverse + 0.5) * period_v) * inverse
    cosv, sinv = turn_cos_sin(turns)
    return cosv, sinv, period_v, inverse


def inner_table(cosv, sinv):
    fc, fs = cosv[0:8], sinv[0:8]
    ec, es = cosv[8:16], sinv[8:16]
    wc, ws = cosv[23:24], sinv[23:24]
    ec = jnp.concatenate([ec, ec * wc - es * ws], axis=0)
    es = jnp.concatenate([es, es * wc + cosv[8:16] * ws], axis=0)
    parts_c, parts_s = [], []
    for a in range(16):
        c, s = ec[a : a + 1], es[a : a + 1]
        parts_c.append(c * fc - s * fs)
        parts_s.append((-s) * fc - c * fs)
    halves = [jnp.concatenate(p, axis=0).astype(BF) for p in (parts_c, parts_s)]
    return jnp.concatenate(halves, axis=1)


def analyse(points_rows, points, lat_ids, weights, orders, coupling, nv, nl, width):
    fields = nv * nl
    slots = lat_ids.shape[0]
    rows = 2 * (width // 128)
    span = window_rows(width)
    tiles = span // 8
    middle = tiles // 2
    bands = orders.shape[0]
    count = 8 * bands
    grid = slots // GROUP

    def kernel(points_ref, lat_ref, weight_ref, coupling_ref, x_ref, given_ref, own_ref, sum_ref, order_ref, planes):
        step = pl.program_id(0)

        @pl.when(step == 0)
        def _():
            order_ref[...] = deal(given_ref[...], bands)

        order = order_ref[...]
        position = (128 * (iota((span, 128), 0) // 2) + iota((span, 128), 1)).astype(F32)
        shared, blocks = angle_rows(order, tiles)
        for i in range(GROUP):
            base, off = window(i, rows)
            slot = step * GROUP + i
            period = points_ref[lat_ref[slot]]
            cosv, sinv, period_v, inverse = slot_angles(shared, blocks, order, off, period)
            table = inner_table(cosv, sinv)
            limit = jnp.full((1, 128), period, jnp.int32).astype(F32) + 64.0 * off
            keep = jnp.minimum(jnp.maximum(limit - position, 0.0), 1.0)
            if off:
                head = jnp.where(position[:16] >= 64.0 * off, keep[:16], 0.0)
                keep = jnp.concatenate([head, keep[16:]], axis=0)
            keep = keep.astype(BF)
            data = jnp.concatenate([x_ref[f, base : base + span, :] * keep for f in range(fields)], axis=0)
            sums = jnp.dot(data, table, preferred_element_type=F32)
            re = [None] * fields
            im = [None] * fields
            for u in range(middle):
                c, s = cosv[16 + u : 17 + u], sinv[16 + u : 17 + u]
                for f in range(fields):
                    up = f * span + 8 * (middle + u)
                    down = f * span + 8 * (middle - 1 - u)
                    ur, ui = sums[up : up + 8, :count], sums[up : up + 8, count:]
                    dr, di = sums[down : down + 8, :count], sums[down : down + 8, count:]
                    r = c * (ur + dr) + s * (ui - di)
                    q = c * (ui + di) - s * (ur - dr)
                    re[f] = r if u == 0 else re[f] + r
                    im[f] = q if u == 0 else im[f] + q
            factor = jnp.where(2.0 * order < period_v, weight_ref[slot] * inverse, 0.0)
            hc, hs = cosv[24:32] * factor, sinv[24:32] * factor
            for f in range(fields):
                turned = (hc * re[f] + hs * im[f], hc * im[f] - hs * re[f])
                for ri, acc in enumerate(turned):
                    acc = acc + pltpu.roll(acc, 2, 0)
                    acc = acc + pltpu.roll(acc, 4, 0)
                    other = pltpu.roll(acc, 1, 0)
                    planes[2 * f + ri, pl.ds(slot, 1), :] = (acc + other)[0:1]
                    planes[2 * fields + 2 * f + ri, pl.ds(slot, 1), :] = (acc - other)[0:1]

        @pl.when(step == grid - 1)
        def _():
            for p in range(2):
                for v in range(nv):
                    for ri in range(2):
                        running = None
                        for l in range(nl):
                            at = ((p * nv + v) * nl + l) * 2 + ri
                            value = planes[at].astype(BF).astype(F32)
                            own_ref[at] = value if running is None else value + running
                            term = coupling_ref[v, l] * value
                            running = term if running is None else running + term
                        sum_ref[(p * nv + v) * 2 + ri] = running.astype(BF)

    smem = pl.BlockSpec(memory_space=pltpu.SMEM)
    return pl.pallas_call(
        kernel,
        name="analyse",
        grid=(grid,),
        in_specs=[
            smem,
            smem,
            smem,
            smem,
            pl.BlockSpec((fields, GROUP * rows, 128), lambda i: (0, i, 0)),
            pl.BlockSpec((bands, 8), lambda i: (0, 0)),
        ],
        out_specs=[
            pl.BlockSpec(memory_space=pltpu.VMEM),
            pl.BlockSpec((16 // nl, slots, count), lambda i: (0, 0, 0)),
            pl.BlockSpec((1, count), lambda i: (0, 0)),
        ],
        out_shape=[
            pltpu.VMEM((16, slots, count), F32),
            jax.ShapeDtypeStruct((16 // nl, slots, count), BF),
            jax.ShapeDtypeStruct((1, count), F32),
        ],
        scratch_shapes=[pltpu.VMEM((16, slots, count), F32)],
        compiler_params=pltpu.CompilerParams(dimension_semantics=("arbitrary",)),
    )(points, lat_ids, weights, coupling, points_rows, orders)


def deal(given, bands):
    count = bands * 8
    line, lane = iota((bands, count), 0), iota((bands, count), 1)
    spots = jnp.zeros((bands, count), F32)
    for e in range(8):
        spots = jnp.where(lane == 8 * line + e, given[:, e : e + 1], spots)
    row = jnp.sum(spots, axis=0, keepdims=True)
    line, lane = iota((count, count), 0), iota((count, count), 1)
    column = jnp.sum(jnp.where(line == lane, row, 0.0), axis=1, keepdims=True)
    rank = jnp.sum(jnp.where(row < column, 1.0, 0.0), axis=1, keepdims=True).astype(jnp.int32)
    upper = rank >= count // 2
    pair = jnp.where(upper, count - 1 - rank, rank)
    place = pair % bands * 8 + pair // bands * 2 + jnp.where(upper, 1, 0)
    return jnp.sum(jnp.where(place == lane, column, 0.0), axis=0, keepdims=True)


def mix(own, earlier, bands, nv, nl):
    _, slots, count = own.shape

    def kernel(own_ref, earlier_ref, out_ref):
        for tile in range(count // 128):
            lanes = slice(128 * tile, 128 * tile + 128)
            value = []
            for k in range(16):
                source = k // (2 * nl) * 2 + k % 2
                value.append(own_ref[k, :, lanes] + earlier_ref[source, :, lanes].astype(F32))
            for d, w in enumerate(block_transpose(value)):
                out_ref[16 * tile + d] = w.astype(BF)

    return pl.pallas_call(kernel, name="mix", out_shape=jax.ShapeDtypeStruct((bands, slots, 128), BF))(*resident(own, earlier))


def make_rows(block, term_ref, cos_ref, second_ref, state, rows_ref):
    now, before, log_now = state
    half = cos_ref.shape[1]
    info = term_ref[block]
    restart = jnp.broadcast_to(info[:, 97:98], (8, half)) > 0.5
    current = jnp.where(restart, 1.0, now[...])
    previous = jnp.where(restart, 0.0, before[...])
    running = jnp.where(restart, second_ref[...], log_now[...])
    cosine = cos_ref[...]
    scale = None
    held = None
    for j in range(STEPS):
        if j % CHECK == 0:
            large = jnp.maximum(jnp.abs(current), jnp.abs(previous)) > 1.0
            shrink = jnp.where(large, 2.0**-60, 1.0)
            running = running + jnp.where(large, RESCALE_LOG, 0.0)
            current = current * shrink
            previous = previous * shrink
            scale = jnp.exp(running)
        value = current * scale
        if j % 2 == 0:
            held = value
        else:
            rows_ref[8 * (j - 1) : 8 * (j + 1), :] = jnp.concatenate([held, value], axis=0).astype(BF)
        current, previous = cosine * current - info[:, STEPS + j : STEPS + j + 1] * previous, current
        if j % FOLD == FOLD - 1:
            fold = info[:, j : j + 1]
            current = current * fold
            previous = previous * fold
    now[...] = current
    before[...] = previous
    log_now[...] = running


def plan(band, orders, lats):
    total = lats.shape[1]
    half = total // 2
    count = orders.shape[1]
    blocks = 8 * (-(-(4 * (-(-2 * (NT + 1) // (4 * STEPS))) + 2) // 8))

    def kernel(band_ref, order_ref, lat_ref, term_ref, cos_ref, first_ref, second_ref, quads_ref):
        line, lane = iota((8, count), 0), iota((8, count), 1)
        target = 8 * band_ref[0] + 2 * (line % 4)
        first = jnp.sum(jnp.where(lane == target, order_ref[...], 0.0), axis=1, keepdims=True)
        second = jnp.sum(jnp.where(lane == target + 1, order_ref[...], 0.0), axis=1, keepdims=True)
        index = (iota((1, NT + 1), 1) + 1).astype(F32)
        terms = jnp.log(1.0 + 0.5 / index)
        turned_cos, turned_sin = turn_cos_sin((lat_ref[...] + 0.5) * (1.0 / (4.0 * NH)))
        log_sine = jnp.log(turned_sin)
        top = iota((8, half), 0) < 4
        cos_ref[...] = jnp.where(top, turned_cos[:, :half], turned_cos[:, half:])
        side = jnp.where(top, log_sine[:, :half], log_sine[:, half:])
        for order, target_ref in ((first, first_ref), (second, second_ref)):
            norm = jnp.sum(jnp.where(index <= order, terms, 0.0), axis=1, keepdims=True)
            target_ref[...] = (0.5 * math.log(0.5) + 0.5 * norm) + order * side
        first = jnp.broadcast_to(first, (8, 128))
        second = jnp.broadcast_to(second, (8, 128))
        ends = jnp.floor((NT + STEPS - first) * (1.0 / STEPS))
        stops = ends + jnp.floor((NT + STEPS - second) * (1.0 / STEPS))
        quads_ref[0] = jnp.max(jnp.floor((stops + 3.0) * 0.25).astype(jnp.int32))
        lane = iota((8, 128), 1)
        kind = lane // STEPS
        tick = (lane % STEPS).astype(F32)
        chain = 2.0 * (iota((8, 128), 0) % 4).astype(F32)

        def fill(block):
            at = jnp.full((8, 128), block, jnp.int32).astype(F32)
            late = at >= ends
            order = jnp.where(late, second, first)
            row = order + STEPS * jnp.where(late, at - ends, at) + tick
            degree = row + 1.0
            offset = degree - order
            ahead = jnp.sqrt((4.0 * degree * degree - 1.0) / (offset * (degree + order)))
            below = jnp.maximum(4.0 * row * row - 1.0, 1.0)
            behind = (offset - 1.0) * (row + order) / below
            for reach in (1, 2, 4):
                ahead = ahead * jnp.where(lane % FOLD >= reach, pltpu.roll(ahead, reach, 1), 1.0)
            kappa = jnp.where(lane % FOLD == 0, 1.0, pltpu.roll(ahead, 1, 1))
            damp = kappa * kappa / (1.0 + 4.0 * row * (row + 1.0) / (NT * (NT + 1.0)))
            damp = jnp.where(row <= NT, damp, 0.0)
            last = jnp.where(lane == 96, chain + jnp.where(late, 1.0, 0.0), jnp.where(at == ends, 1.0, 0.0))
            rest = jnp.where(kind == 2, damp, last)
            term_ref[block] = jnp.where(kind == 0, ahead, jnp.where(kind == 1, behind, rest))

        def several(i, carry):
            for k in range(8):
                fill(8 * i + k)
            return carry

        lax.fori_loop(0, blocks // 8, several, 0)

    smem = pl.BlockSpec(memory_space=pltpu.SMEM)
    vmem = pl.BlockSpec(memory_space=pltpu.VMEM)
    wide = pltpu.VMEM((8, half), F32)
    return pl.pallas_call(
        kernel,
        name="plan",
        in_specs=[smem, vmem, vmem],
        out_specs=[vmem] * 4 + [smem],
        out_shape=[pltpu.VMEM((blocks, 8, 128), F32), wide, wide, wide, jax.ShapeDtypeStruct((1,), jnp.int32)],
    )(band, orders, lats)


def legendre(own, tables):
    bands, slots, _ = own.shape
    total = bands * slots
    half = total // 2
    height = 8 * STEPS

    def kernel(own_ref, term_ref, cos_ref, first_ref, second_ref, quads_ref, out_ref, mixed, weights, rows0, rows1, rows2, rows3, kept0, kept1, acc, now, before, log_now):
        rows = (rows0, rows1, rows2, rows3)
        kept = (kept0, kept1)
        line, lane = iota((8, 128), 0), iota((8, 128), 1)
        low = line < 4
        for b in range(bands):
            mixed[b * slots : (b + 1) * slots] = own_ref[b].astype(F32)
        weights[...] = jnp.concatenate([mixed[:half], mixed[half:]], axis=1).astype(BF)
        acc[...] = jnp.zeros((256, half), F32)
        rows3[...] = jnp.zeros((height, half), BF)
        kept1[...] = jnp.zeros((height, 256), BF)
        now[...] = jnp.ones((8, half), F32)
        before[...] = jnp.zeros((8, half), F32)
        log_now[...] = first_ref[...]
        state = (now, before, log_now)

        def make(block, target):
            make_rows(block, term_ref, cos_ref, second_ref, state, target)

        def analysed(block, source, target):
            found = jnp.dot(source[...], weights[...], preferred_element_type=F32)
            info = term_ref[block]
            hit = lane % 8 == jnp.broadcast_to(info[:, 96:97], (8, 128)).astype(jnp.int32)
            masks = []
            for parity in range(2):
                match = hit & (lane // 64 == parity)
                masks.append((match & low, match & ~low))
            tops, lows = [], []
            for j in range(STEPS):
                part = found[8 * j : 8 * j + 8]
                part = jnp.where(low, part[:, :128], part[:, 128:])
                part = (part + pltpu.roll(part, 4, 0)) * info[:, 2 * STEPS + j : 2 * STEPS + j + 1]
                tops.append(jnp.where(masks[j % 2][0], part, 0.0))
                lows.append(jnp.where(masks[j % 2][1], part, 0.0))
            target[...] = jnp.concatenate([jnp.concatenate(tops, axis=0), jnp.concatenate(lows, axis=0)], axis=1).astype(BF)

        def gathered(coefficients, source):
            acc[...] += lax.dot_general(
                coefficients[...], source[...], (((0,), (0,)), ((), ())), preferred_element_type=F32
            )

        make(0, rows0)

        def body(i, carry):
            for k in range(4):
                make(4 * i + k + 1, rows[(k + 1) % 4])
                analysed(4 * i + k, rows[k], kept[k % 2])
                gathered(kept[(k + 1) % 2], rows[(k + 3) % 4])
            return carry

        lax.fori_loop(0, quads_ref[0], body, 0)
        gathered(kept1, rows3)
        for h in range(2):
            for c in range(half // 128):
                at = h * half + 128 * c
                mixed[at : at + 128] = jnp.transpose(acc[128 * h : 128 * h + 128, 128 * c : 128 * c + 128])
        for b in range(bands):
            out_ref[b] = mixed[b * slots : (b + 1) * slots].astype(BF)

    vmem = pl.BlockSpec(memory_space=pltpu.VMEM)
    return pl.pallas_call(
        kernel,
        name="legendre",
        in_specs=[vmem] * 5 + [pl.BlockSpec(memory_space=pltpu.SMEM)],
        out_specs=vmem,
        out_shape=jax.ShapeDtypeStruct((bands, slots, 128), BF),
        scratch_shapes=[
            pltpu.VMEM((total, 128), F32),
            pltpu.VMEM((half, 256), BF),
            pltpu.VMEM((height, half), BF),
            pltpu.VMEM((height, half), BF),
            pltpu.VMEM((height, half), BF),
            pltpu.VMEM((height, half), BF),
            pltpu.VMEM((height, 256), BF),
            pltpu.VMEM((height, 256), BF),
            pltpu.VMEM((256, half), F32),
            pltpu.VMEM((8, half), F32),
            pltpu.VMEM((8, half), F32),
            pltpu.VMEM((8, half), F32),
        ],
    )(*resident(own, *tables[:4]), tables[4])


def synthesise(back, points, lat_ids, orders, nv, nl, width):
    bands, slots, _ = back.shape
    fields = nv * nl
    rows = 2 * (width // 128)
    span = window_rows(width)
    tiles = span // 8
    middle = tiles // 2
    count = orders.shape[1]
    grid = slots // GROUP

    def kernel(points_ref, lat_ref, back_ref, order_ref, out_ref, planes):
        step = pl.program_id(0)

        @pl.when(step == 0)
        def _():
            for tile in range(count // 128):
                value = [back_ref[16 * tile + d].astype(F32) for d in range(16)]
                for k, w in enumerate(block_transpose(value)):
                    planes[k, :, 128 * tile : 128 * tile + 128] = w

        order = order_ref[...]
        position = 128 * (iota((span, 128), 0) // 2) + iota((span, 128), 1)
        shared, blocks = angle_rows(order, tiles)
        sign = jnp.where(iota((8, count), 0) % 2 == 0, 1.0, -1.0)
        double = jnp.where(order == 0.0, 1.0, 2.0)
        for i in range(GROUP):
            base, off = window(i, rows)
            slot = step * GROUP + i
            period = points_ref[lat_ref[slot]]
            cosv, sinv, period_v, _ = slot_angles(shared, blocks, order, off, period)
            table = inner_table(cosv, sinv)
            factor = jnp.where(2.0 * order < period_v, double, 0.0)
            hc, hs = cosv[24:32] * factor, sinv[24:32] * factor
            turns = []
            for t in range(0, tiles, 2):
                pair = []
                for source in (cosv, sinv):
                    lines = []
                    for k in (t, t + 1):
                        u = k - middle if k >= middle else middle - 1 - k
                        line = source[16 + u : 17 + u]
                        if source is sinv and k < middle:
                            line = -line
                        lines.append(jnp.broadcast_to(line, (8, count)))
                    pair.append(jnp.concatenate(lines, axis=0).astype(BF))
                turns.append(pair)
            parts = []
            for f in range(fields):
                both = []
                for ri in range(2):
                    even = planes[2 * f + ri, pl.ds(slot, 1), :]
                    odd = planes[2 * fields + 2 * f + ri, pl.ds(slot, 1), :]
                    both.append(even + sign * odd)
                re, im = both
                wr, wi = hc * re - hs * im, hs * re + hc * im
                wr = jnp.concatenate([wr, wr], axis=0).astype(BF)
                wi = jnp.concatenate([wi, wi], axis=0).astype(BF)
                zr = [c * wr - s * wi for c, s in turns]
                zi = [s * wr + c * wi for c, s in turns]
                parts.append(jnp.concatenate([jnp.concatenate(zr, axis=0), jnp.concatenate(zi, axis=0)], axis=1))
            waves = jnp.concatenate(parts, axis=0)
            values = lax.dot_general(waves, table, (((1,), (1,)), ((), ())), preferred_element_type=F32)
            inside = position < period + 64 * off
            starts = position[:16] >= 64 * off
            for f in range(fields):
                part = jnp.where(inside, values[f * span : (f + 1) * span], 0.0)
                if off:
                    first = jnp.where(starts, part[:16], out_ref[f, base : base + 16, :].astype(F32))
                    out_ref[f, base : base + 16, :] = first.astype(BF)
                    out_ref[f, base + 16 : base + span, :] = part[16:].astype(BF)
                else:
                    out_ref[f, base : base + span, :] = part.astype(BF)

    smem = pl.BlockSpec(memory_space=pltpu.SMEM)
    return pl.pallas_call(
        kernel,
        name="synthesise",
        grid=(grid,),
        in_specs=[
            smem,
            smem,
            pl.BlockSpec((bands, slots, 128), lambda i: (0, 0, 0)),
            pl.BlockSpec((1, count), lambda i: (0, 0)),
        ],
        out_specs=pl.BlockSpec((fields, GROUP * rows, 128), lambda i: (0, i, 0)),
        out_shape=jax.ShapeDtypeStruct((fields, slots * rows, 128), BF),
        scratch_shapes=[pltpu.VMEM((16, slots, count), F32)],
        compiler_params=pltpu.CompilerParams(dimension_semantics=("arbitrary",)),
    )(points, lat_ids, back, orders)


def solution(mesh):
    bands, parts = mesh.shape["band"], mesh.shape["fld"]

    def on_device(grid_field, coupling, points, lat_ids, wn_ids):
        nv, nl, slots, _, width = grid_field.shape
        mine = wn_ids.shape[0]
        spread = jnp.concatenate(
            [jnp.broadcast_to(wn_ids[None], (bands, mine)), jnp.broadcast_to(lat_ids[None], (bands, slots))], axis=1
        )
        known = lax.all_to_all(spread, "band", split_axis=0, concat_axis=0, tiled=True)
        orders = known[:, :mine].astype(F32)
        lats = known[:, mine:].reshape(1, bands * slots).astype(F32)
        weights = math.pi / (2.0 * NH) * jnp.sin(math.pi * (lat_ids.astype(F32) + 0.5) / (2.0 * NH))
        own, sums, orders = analyse(as_rows(grid_field), points, lat_ids, weights, orders, coupling, nv, nl, width)
        earlier = jnp.zeros_like(sums)
        for shift in range(1, parts):
            moved = lax.ppermute(sums, "fld", [(k, k + shift) for k in range(parts - shift)])
            earlier = moved if shift == 1 else earlier + moved
        own, orders = lax.optimization_barrier((mix(own, earlier, bands, nv, nl), orders))
        own = lax.all_to_all(own, "band", split_axis=0, concat_axis=0, tiled=True)
        band = lax.axis_index("band").astype(jnp.int32).reshape(1)
        back = legendre(own, plan(band, orders, lats))
        back = lax.all_to_all(back, "band", split_axis=0, concat_axis=0, tiled=True)
        rows = synthesise(back, points, lat_ids, orders, nv, nl, width)
        return from_rows(rows, nv, nl, slots, width)

    in_specs = (P(None, "fld", "band", None, None), P(None, "fld"), P(), P("band"), P("band"))
    return jax.shard_map(on_device, mesh=mesh, in_specs=in_specs, out_specs=in_specs[0], check_vma=False)
```

```python
import math

import jax
import jax.numpy as jnp
from jax import lax
from jax.experimental import pallas as pl
from jax.experimental.pallas import tpu as pltpu
from jax.experimental.layout import Layout, with_layout_constraint
from jax.sharding import PartitionSpec as P

NT = 1279
NH = 1280
BF = jnp.bfloat16
F32 = jnp.float32
GROUP = 8
STEPS = 32
CHECK = 16
FOLD = 8
RESCALE_LOG = 60.0 * math.log(2.0)


def resident(*arrays):
    return [pltpu.with_memory_space_constraint(a, pltpu.VMEM) for a in arrays]


def iota(shape, dim):
    return lax.broadcasted_iota(jnp.int32, shape, dim)


def turn_cos_sin(turns):
    y = turns * turns
    s = -0.59828975 + y * 0.07765416
    s = 2.55007732 + y * s
    s = -5.16771007 + y * s
    s = turns * (3.14159264 + y * s)
    c = -1.33187126 + y * 0.21967748
    c = 4.05841064 + y * c
    c = -4.9347928 + y * c
    c = 0.99999995 + y * c
    twice = s + s
    return 1.0 - twice * s, twice * c


def block_transpose(planes):
    lane = iota((1, 128), 1) // 8
    planes = list(planes)
    for bit in (8, 4, 2, 1):
        low = (lane & bit) == 0
        for at in range(16):
            if at & bit:
                continue
            a, b = planes[at], planes[at | bit]
            planes[at] = jnp.where(low, a, pltpu.roll(b, 8 * bit, 1))
            planes[at | bit] = jnp.where(low, pltpu.roll(a, 128 - 8 * bit, 1), b)
    return planes


def window(i, rows):
    start = i * rows
    base = start // 16 * 16
    return base, start - base


def window_rows(width):
    return -(-(2 * (width // 128) + 14) // 16) * 16


def as_rows(field):
    nv, nl, slots, _, width = field.shape
    blocks = width // 128
    split = field.reshape(nv, nl, slots, 2, blocks, 128)
    split = with_layout_constraint(split, Layout(major_to_minor=(0, 1, 2, 4, 3, 5)))
    return split.transpose(0, 1, 2, 4, 3, 5).reshape(nv * nl, slots * 2 * blocks, 128)


def from_rows(rows, nv, nl, slots, width):
    split = rows.reshape(nv, nl, slots, width // 128, 2, 128).transpose(0, 1, 2, 4, 3, 5)
    split = with_layout_constraint(split, Layout(major_to_minor=(0, 1, 2, 4, 3, 5)))
    return split.reshape(nv, nl, slots, 2, width)


def angle_rows(order, tiles):
    count = order.shape[1]
    row = iota((8, count), 0)
    steps = jnp.where(row < tiles // 2, 256 * (2 * row + 1), 64)
    shared = jnp.concatenate([row, 8 * row, steps], axis=0).astype(F32) * order
    blocks = (128 * (2 * tiles - 2 + row // 2)).astype(F32)
    return shared, blocks


def slot_angles(shared, blocks, order, off, period):
    product = jnp.concatenate([shared, (blocks - 64.0 * off) * order], axis=0)
    period_v = jnp.full(order.shape, period, jnp.int32).astype(F32)
    inverse = 1.0 / period_v
    turns = (product - jnp.floor(product * inverse + 0.5) * period_v) * inverse
    cosv, sinv = turn_cos_sin(turns)
    return cosv, sinv, period_v, inverse


def inner_table(cosv, sinv):
    fc, fs = cosv[0:8], sinv[0:8]
    ec, es = cosv[8:16], sinv[8:16]
    wc, ws = cosv[23:24], sinv[23:24]
    ec = jnp.concatenate([ec, ec * wc - es * ws], axis=0)
    es = jnp.concatenate([es, es * wc + cosv[8:16] * ws], axis=0)
    parts_c, parts_s = [], []
    for a in range(16):
        c, s = ec[a : a + 1], es[a : a + 1]
        parts_c.append(c * fc - s * fs)
        parts_s.append((-s) * fc - c * fs)
    halves = [jnp.concatenate(p, axis=0).astype(BF) for p in (parts_c, parts_s)]
    return jnp.concatenate(halves, axis=1)


def analyse(points_rows, points, lat_ids, weights, orders, coupling, nv, nl, width):
    fields = nv * nl
    slots = lat_ids.shape[0]
    rows = 2 * (width // 128)
    span = window_rows(width)
    tiles = span // 8
    middle = tiles // 2
    bands = orders.shape[0]
    count = 8 * bands
    grid = slots // GROUP

    def kernel(points_ref, lat_ref, weight_ref, coupling_ref, x_ref, given_ref, own_ref, sum_ref, order_ref, planes):
        step = pl.program_id(0)

        @pl.when(step == 0)
        def _():
            order_ref[...] = deal(given_ref[...], bands)

        order = order_ref[...]
        position = (128 * (iota((span, 128), 0) // 2) + iota((span, 128), 1)).astype(F32)
        shared, blocks = angle_rows(order, tiles)
        for i in range(GROUP):
            base, off = window(i, rows)
            slot = step * GROUP + i
            period = points_ref[lat_ref[slot]]
            cosv, sinv, period_v, inverse = slot_angles(shared, blocks, order, off, period)
            table = inner_table(cosv, sinv)
            limit = jnp.full((1, 128), period, jnp.int32).astype(F32) + 64.0 * off
            keep = jnp.minimum(jnp.maximum(limit - position, 0.0), 1.0)
            if off:
                head = jnp.where(position[:16] >= 64.0 * off, keep[:16], 0.0)
                keep = jnp.concatenate([head, keep[16:]], axis=0)
            keep = keep.astype(BF)
            data = jnp.concatenate([x_ref[f, base : base + span, :] * keep for f in range(fields)], axis=0)
            sums = jnp.dot(data, table, preferred_element_type=F32)
            re = [None] * fields
            im = [None] * fields
            for u in range(middle):
                c, s = cosv[16 + u : 17 + u], sinv[16 + u : 17 + u]
                for f in range(fields):
                    up = f * span + 8 * (middle + u)
                    down = f * span + 8 * (middle - 1 - u)
                    ur, ui = sums[up : up + 8, :count], sums[up : up + 8, count:]
                    dr, di = sums[down : down + 8, :count], sums[down : down + 8, count:]
                    r = c * (ur + dr) + s * (ui - di)
                    q = c * (ui + di) - s * (ur - dr)
                    re[f] = r if u == 0 else re[f] + r
                    im[f] = q if u == 0 else im[f] + q
            factor = jnp.where(2.0 * order < period_v, weight_ref[slot] * inverse, 0.0)
            hc, hs = cosv[24:32] * factor, sinv[24:32] * factor
            for f in range(fields):
                turned = (hc * re[f] + hs * im[f], hc * im[f] - hs * re[f])
                for ri, acc in enumerate(turned):
                    acc = acc + pltpu.roll(acc, 2, 0)
                    acc = acc + pltpu.roll(acc, 4, 0)
                    other = pltpu.roll(acc, 1, 0)
                    planes[2 * f + ri, pl.ds(slot, 1), :] = (acc + other)[0:1]
                    planes[2 * fields + 2 * f + ri, pl.ds(slot, 1), :] = (acc - other)[0:1]

        @pl.when(step == grid - 1)
        def _():
            for p in range(2):
                for v in range(nv):
                    for ri in range(2):
                        running = None
                        for l in range(nl):
                            at = ((p * nv + v) * nl + l) * 2 + ri
                            value = planes[at].astype(BF).astype(F32)
                            own_ref[at] = value if running is None else value + running
                            term = coupling_ref[v, l] * value
                            running = term if running is None else running + term
                        sum_ref[(p * nv + v) * 2 + ri] = running.astype(BF)

    smem = pl.BlockSpec(memory_space=pltpu.SMEM)
    return pl.pallas_call(
        kernel,
        name="analyse",
        grid=(grid,),
        in_specs=[
            smem,
            smem,
            smem,
            smem,
            pl.BlockSpec((fields, GROUP * rows, 128), lambda i: (0, i, 0)),
            pl.BlockSpec((bands, 8), lambda i: (0, 0)),
        ],
        out_specs=[
            pl.BlockSpec(memory_space=pltpu.VMEM),
            pl.BlockSpec((16 // nl, slots, count), lambda i: (0, 0, 0)),
            pl.BlockSpec((1, count), lambda i: (0, 0)),
        ],
        out_shape=[
            pltpu.VMEM((16, slots, count), F32),
            jax.ShapeDtypeStruct((16 // nl, slots, count), BF),
            jax.ShapeDtypeStruct((1, count), F32),
        ],
        scratch_shapes=[pltpu.VMEM((16, slots, count), F32)],
        compiler_params=pltpu.CompilerParams(dimension_semantics=("arbitrary",)),
    )(points, lat_ids, weights, coupling, points_rows, orders)


def deal(given, bands):
    count = bands * 8
    line, lane = iota((bands, count), 0), iota((bands, count), 1)
    spots = jnp.zeros((bands, count), F32)
    for e in range(8):
        spots = jnp.where(lane == 8 * line + e, given[:, e : e + 1], spots)
    row = jnp.sum(spots, axis=0, keepdims=True)
    line, lane = iota((count, count), 0), iota((count, count), 1)
    column = jnp.sum(jnp.where(line == lane, row, 0.0), axis=1, keepdims=True)
    rank = jnp.sum(jnp.where(row < column, 1.0, 0.0), axis=1, keepdims=True).astype(jnp.int32)
    upper = rank >= count // 2
    pair = jnp.where(upper, count - 1 - rank, rank)
    place = pair % bands * 8 + pair // bands * 2 + jnp.where(upper, 1, 0)
    return jnp.sum(jnp.where(place == lane, column, 0.0), axis=0, keepdims=True)


def mix(own, earlier, bands, nv, nl):
    _, slots, count = own.shape

    def kernel(own_ref, earlier_ref, out_ref):
        for tile in range(count // 128):
            lanes = slice(128 * tile, 128 * tile + 128)
            value = []
            for k in range(16):
                source = k // (2 * nl) * 2 + k % 2
                value.append(own_ref[k, :, lanes] + earlier_ref[source, :, lanes].astype(F32))
            for d, w in enumerate(block_transpose(value)):
                out_ref[16 * tile + d] = w.astype(BF)

    return pl.pallas_call(kernel, name="mix", out_shape=jax.ShapeDtypeStruct((bands, slots, 128), BF))(*resident(own, earlier))


def make_rows(block, term_ref, cos_ref, second_ref, state, rows_ref):
    now, before, log_now = state
    half = cos_ref.shape[1]
    info = term_ref[block]
    restart = jnp.broadcast_to(info[:, 97:98], (8, half)) > 0.5
    current = jnp.where(restart, 1.0, now[...])
    previous = jnp.where(restart, 0.0, before[...])
    running = jnp.where(restart, second_ref[...], log_now[...])
    cosine = cos_ref[...]
    scale = None
    held = None
    for j in range(STEPS):
        if j % CHECK == 0:
            large = jnp.maximum(jnp.abs(current), jnp.abs(previous)) > 1.0
            shrink = jnp.where(large, 2.0**-60, 1.0)
            running = running + jnp.where(large, RESCALE_LOG, 0.0)
            current = current * shrink
            previous = previous * shrink
            scale = jnp.exp(running)
        value = current * scale
        if j % 2 == 0:
            held = value
        else:
            rows_ref[8 * (j - 1) : 8 * (j + 1), :] = jnp.concatenate([held, value], axis=0).astype(BF)
        current, previous = cosine * current - info[:, STEPS + j : STEPS + j + 1] * previous, current
        if j % FOLD == FOLD - 1:
            fold = info[:, j : j + 1]
            current = current * fold
            previous = previous * fold
    now[...] = current
    before[...] = previous
    log_now[...] = running


def plan(band, orders, lats):
    total = lats.shape[1]
    half = total // 2
    count = orders.shape[1]
    blocks = 8 * (-(-(4 * (-(-2 * (NT + 1) // (4 * STEPS))) + 2) // 8))

    def kernel(band_ref, order_ref, lat_ref, term_ref, cos_ref, first_ref, second_ref, quads_ref):
        line, lane = iota((8, count), 0), iota((8, count), 1)
        target = 8 * band_ref[0] + 2 * (line % 4)
        first = jnp.sum(jnp.where(lane == target, order_ref[...], 0.0), axis=1, keepdims=True)
        second = jnp.sum(jnp.where(lane == target + 1, order_ref[...], 0.0), axis=1, keepdims=True)
        index = (iota((1, NT + 1), 1) + 1).astype(F32)
        terms = jnp.log(1.0 + 0.5 / index)
        turned_cos, turned_sin = turn_cos_sin((lat_ref[...] + 0.5) * (1.0 / (4.0 * NH)))
        log_sine = jnp.log(turned_sin)
        top = iota((8, half), 0) < 4
        cos_ref[...] = jnp.where(top, turned_cos[:, :half], turned_cos[:, half:])
        side = jnp.where(top, log_sine[:, :half], log_sine[:, half:])
        for order, target_ref in ((first, first_ref), (second, second_ref)):
            norm = jnp.sum(jnp.where(index <= order, terms, 0.0), axis=1, keepdims=True)
            target_ref[...] = (0.5 * math.log(0.5) + 0.5 * norm) + order * side
        first = jnp.broadcast_to(first, (8, 128))
        second = jnp.broadcast_to(second, (8, 128))
        ends = jnp.floor((NT + STEPS - first) * (1.0 / STEPS))
        stops = ends + jnp.floor((NT + STEPS - second) * (1.0 / STEPS))
        quads_ref[0] = jnp.max(jnp.floor((stops + 3.0) * 0.25).astype(jnp.int32))
        lane = iota((8, 128), 1)
        kind = lane // STEPS
        tick = (lane % STEPS).astype(F32)
        chain = 2.0 * (iota((8, 128), 0) % 4).astype(F32)

        def fill(block):
            at = jnp.full((8, 128), block, jnp.int32).astype(F32)
            late = at >= ends
            order = jnp.where(late, second, first)
            row = order + STEPS * jnp.where(late, at - ends, at) + tick
            degree = row + 1.0
            offset = degree - order
            ahead = jnp.sqrt((4.0 * degree * degree - 1.0) / (offset * (degree + order)))
            below = jnp.maximum(4.0 * row * row - 1.0, 1.0)
            behind = (offset - 1.0) * (row + order) / below
            for reach in (1, 2, 4):
                ahead = ahead * jnp.where(lane % FOLD >= reach, pltpu.roll(ahead, reach, 1), 1.0)
            kappa = jnp.where(lane % FOLD == 0, 1.0, pltpu.roll(ahead, 1, 1))
            damp = kappa * kappa / (1.0 + 4.0 * row * (row + 1.0) / (NT * (NT + 1.0)))
            damp = jnp.where(row <= NT, damp, 0.0)
            last = jnp.where(lane == 96, chain + jnp.where(late, 1.0, 0.0), jnp.where(at == ends, 1.0, 0.0))
            rest = jnp.where(kind == 2, damp, last)
            term_ref[block] = jnp.where(kind == 0, ahead, jnp.where(kind == 1, behind, rest))

        def several(i, carry):
            for k in range(8):
                fill(8 * i + k)
            return carry

        lax.fori_loop(0, blocks // 8, several, 0)

    smem = pl.BlockSpec(memory_space=pltpu.SMEM)
    vmem = pl.BlockSpec(memory_space=pltpu.VMEM)
    wide = pltpu.VMEM((8, half), F32)
    return pl.pallas_call(
        kernel,
        name="plan",
        in_specs=[smem, vmem, vmem],
        out_specs=[vmem] * 4 + [smem],
        out_shape=[pltpu.VMEM((blocks, 8, 128), F32), wide, wide, wide, jax.ShapeDtypeStruct((1,), jnp.int32)],
    )(band, orders, lats)


def legendre(own, tables):
    bands, slots, _ = own.shape
    total = bands * slots
    half = total // 2
    height = 8 * STEPS

    def kernel(own_ref, term_ref, cos_ref, first_ref, second_ref, quads_ref, out_ref, mixed, weights, rows0, rows1, rows2, rows3, kept0, kept1, acc, now, before, log_now):
        rows = (rows0, rows1, rows2, rows3)
        kept = (kept0, kept1)
        line, lane = iota((8, 128), 0), iota((8, 128), 1)
        low = line < 4
        for b in range(bands):
            mixed[b * slots : (b + 1) * slots] = own_ref[b].astype(F32)
        weights[...] = jnp.concatenate([mixed[:half], mixed[half:]], axis=1).astype(BF)
        acc[...] = jnp.zeros((256, half), F32)
        rows3[...] = jnp.zeros((height, half), BF)
        kept1[...] = jnp.zeros((height, 256), BF)
        now[...] = jnp.ones((8, half), F32)
        before[...] = jnp.zeros((8, half), F32)
        log_now[...] = first_ref[...]
        state = (now, before, log_now)

        def make(block, target):
            make_rows(block, term_ref, cos_ref, second_ref, state, target)

        def analysed(block, source, target):
            found = jnp.dot(source[...], weights[...], preferred_element_type=F32)
            info = term_ref[block]
            hit = lane % 8 == jnp.broadcast_to(info[:, 96:97], (8, 128)).astype(jnp.int32)
            masks = []
            for parity in range(2):
                match = hit & (lane // 64 == parity)
                masks.append((match & low, match & ~low))
            tops, lows = [], []
            for j in range(STEPS):
                part = found[8 * j : 8 * j + 8]
                part = jnp.where(low, part[:, :128], part[:, 128:])
                part = (part + pltpu.roll(part, 4, 0)) * info[:, 2 * STEPS + j : 2 * STEPS + j + 1]
                tops.append(jnp.where(masks[j % 2][0], part, 0.0))
                lows.append(jnp.where(masks[j % 2][1], part, 0.0))
            target[...] = jnp.concatenate([jnp.concatenate(tops, axis=0), jnp.concatenate(lows, axis=0)], axis=1).astype(BF)

        def gathered(coefficients, source):
            acc[...] += lax.dot_general(
                coefficients[...], source[...], (((0,), (0,)), ((), ())), preferred_element_type=F32
            )

        make(0, rows0)

        def body(i, carry):
            for k in range(4):
                make(4 * i + k + 1, rows[(k + 1) % 4])
                analysed(4 * i + k, rows[k], kept[k % 2])
                gathered(kept[(k + 1) % 2], rows[(k + 3) % 4])
            return carry

        lax.fori_loop(0, quads_ref[0], body, 0)
        gathered(kept1, rows3)
        for h in range(2):
            for c in range(half // 128):
                at = h * half + 128 * c
                mixed[at : at + 128] = jnp.transpose(acc[128 * h : 128 * h + 128, 128 * c : 128 * c + 128])
        for b in range(bands):
            out_ref[b] = mixed[b * slots : (b + 1) * slots].astype(BF)

    vmem = pl.BlockSpec(memory_space=pltpu.VMEM)
    return pl.pallas_call(
        kernel,
        name="legendre",
        in_specs=[vmem] * 5 + [pl.BlockSpec(memory_space=pltpu.SMEM)],
        out_specs=vmem,
        out_shape=jax.ShapeDtypeStruct((bands, slots, 128), BF),
        scratch_shapes=[
            pltpu.VMEM((total, 128), F32),
            pltpu.VMEM((half, 256), BF),
            pltpu.VMEM((height, half), BF),
            pltpu.VMEM((height, half), BF),
            pltpu.VMEM((height, half), BF),
            pltpu.VMEM((height, half), BF),
            pltpu.VMEM((height, 256), BF),
            pltpu.VMEM((height, 256), BF),
            pltpu.VMEM((256, half), F32),
            pltpu.VMEM((8, half), F32),
            pltpu.VMEM((8, half), F32),
            pltpu.VMEM((8, half), F32),
        ],
    )(*resident(own, *tables[:4]), tables[4])


def synthesise(back, points, lat_ids, orders, nv, nl, width):
    bands, slots, _ = back.shape
    fields = nv * nl
    rows = 2 * (width // 128)
    span = window_rows(width)
    tiles = span // 8
    middle = tiles // 2
    count = orders.shape[1]
    grid = slots // GROUP

    def kernel(points_ref, lat_ref, back_ref, order_ref, out_ref, planes):
        step = pl.program_id(0)

        @pl.when(step == 0)
        def _():
            for tile in range(count // 128):
                value = [back_ref[16 * tile + d].astype(F32) for d in range(16)]
                for k, w in enumerate(block_transpose(value)):
                    planes[k, :, 128 * tile : 128 * tile + 128] = w

        order = order_ref[...]
        position = 128 * (iota((span, 128), 0) // 2) + iota((span, 128), 1)
        shared, blocks = angle_rows(order, tiles)
        sign = jnp.where(iota((8, count), 0) % 2 == 0, 1.0, -1.0)
        double = jnp.where(order == 0.0, 1.0, 2.0)
        for i in range(GROUP):
            base, off = window(i, rows)
            slot = step * GROUP + i
            period = points_ref[lat_ref[slot]]
            cosv, sinv, period_v, _ = slot_angles(shared, blocks, order, off, period)
            table = inner_table(cosv, sinv)
            factor = jnp.where(2.0 * order < period_v, double, 0.0)
            hc, hs = cosv[24:32] * factor, sinv[24:32] * factor
            turns = []
            for t in range(0, tiles, 2):
                pair = []
                for source in (cosv, sinv):
                    lines = []
                    for k in (t, t + 1):
                        u = k - middle if k >= middle else middle - 1 - k
                        line = source[16 + u : 17 + u]
                        if source is sinv and k < middle:
                            line = -line
                        lines.append(jnp.broadcast_to(line, (8, count)))
                    pair.append(jnp.concatenate(lines, axis=0).astype(BF))
                turns.append(pair)
            parts = []
            for f in range(fields):
                both = []
                for ri in range(2):
                    even = planes[2 * f + ri, pl.ds(slot, 1), :]
                    odd = planes[2 * fields + 2 * f + ri, pl.ds(slot, 1), :]
                    both.append(even + sign * odd)
                re, im = both
                wr, wi = hc * re - hs * im, hs * re + hc * im
                wr = jnp.concatenate([wr, wr], axis=0).astype(BF)
                wi = jnp.concatenate([wi, wi], axis=0).astype(BF)
                zr = [c * wr - s * wi for c, s in turns]
                zi = [s * wr + c * wi for c, s in turns]
                parts.append(jnp.concatenate([jnp.concatenate(zr, axis=0), jnp.concatenate(zi, axis=0)], axis=1))
            waves = jnp.concatenate(parts, axis=0)
            values = lax.dot_general(waves, table, (((1,), (1,)), ((), ())), preferred_element_type=F32)
            inside = position < period + 64 * off
            starts = position[:16] >= 64 * off
            for f in range(fields):
                part = jnp.where(inside, values[f * span : (f + 1) * span], 0.0)
                if off:
                    first = jnp.where(starts, part[:16], out_ref[f, base : base + 16, :].astype(F32))
                    out_ref[f, base : base + 16, :] = first.astype(BF)
                    out_ref[f, base + 16 : base + span, :] = part[16:].astype(BF)
                else:
                    out_ref[f, base : base + span, :] = part.astype(BF)

    smem = pl.BlockSpec(memory_space=pltpu.SMEM)
    return pl.pallas_call(
        kernel,
        name="synthesise",
        grid=(grid,),
        in_specs=[
            smem,
            smem,
            pl.BlockSpec(memory_space=pltpu.VMEM),
            pl.BlockSpec((1, count), lambda i: (0, 0)),
        ],
        out_specs=pl.BlockSpec((fields, GROUP * rows, 128), lambda i: (0, i, 0)),
        out_shape=jax.ShapeDtypeStruct((fields, slots * rows, 128), BF),
        scratch_shapes=[pltpu.VMEM((16, slots, count), F32)],
        compiler_params=pltpu.CompilerParams(dimension_semantics=("arbitrary",)),
    )(points, lat_ids, *resident(back), orders)


def solution(mesh):
    bands, parts = mesh.shape["band"], mesh.shape["fld"]

    def on_device(grid_field, coupling, points, lat_ids, wn_ids):
        nv, nl, slots, _, width = grid_field.shape
        mine = wn_ids.shape[0]
        spread = jnp.concatenate(
            [jnp.broadcast_to(wn_ids[None], (bands, mine)), jnp.broadcast_to(lat_ids[None], (bands, slots))], axis=1
        )
        known = lax.all_to_all(spread, "band", split_axis=0, concat_axis=0, tiled=True)
        orders = known[:, :mine].astype(F32)
        lats = known[:, mine:].reshape(1, bands * slots).astype(F32)
        weights = math.pi / (2.0 * NH) * jnp.sin(math.pi * (lat_ids.astype(F32) + 0.5) / (2.0 * NH))
        own, sums, orders = analyse(as_rows(grid_field), points, lat_ids, weights, orders, coupling, nv, nl, width)
        earlier = jnp.zeros_like(sums)
        for shift in range(1, parts):
            moved = lax.ppermute(sums, "fld", [(k, k + shift) for k in range(parts - shift)])
            earlier = moved if shift == 1 else earlier + moved
        own, orders = lax.optimization_barrier((mix(own, earlier, bands, nv, nl), orders))
        own = lax.all_to_all(own, "band", split_axis=0, concat_axis=0, tiled=True)
        band = lax.axis_index("band").astype(jnp.int32).reshape(1)
        back = legendre(own, plan(band, orders, lats))
        back = lax.all_to_all(back, "band", split_axis=0, concat_axis=0, tiled=True)
        rows = synthesise(back, points, lat_ids, orders, nv, nl, width)
        return from_rows(rows, nv, nl, slots, width)

    in_specs = (P(None, "fld", "band", None, None), P(None, "fld"), P(), P("band"), P("band"))
    return jax.shard_map(on_device, mesh=mesh, in_specs=in_specs, out_specs=in_specs[0], check_vma=False)
```
